32 devices in a mesh: parts: 2 (over y), row: 4 (over z), col: 2 (over x), rhs: 2 (over core).
Axes of the slice: x: 2, y: 2, z: 4, core: 2. Of those that a mesh axis runs over, the one named last changes fastest.
Arguments:
- blocks: bfloat16 [8, 2, 96, 128, 128], P(('parts', 'row'), 'col'), parts along dimension 0, as said below
- block_rows: int32 [8, 2, 96], P(('parts', 'row'), 'col'), parts along dimension 0, may hold values from 0 to 127, as said below
- block_cols: int32 [8, 2, 96], P(('parts', 'row'), 'col'), parts along dimension 0, may hold values from 0 to 255, as said below
- counts: int32 [8, 2], P(('parts', 'row'), 'col'), parts along dimension 0, may hold values from 1 to 96, as said below
- diagonal: float32 [131072], P(('parts', 'row', 'col')), parts along dimension 0, may hold values from 1.2 to 4
- target: float32 [131072, 256], P(('parts', 'row', 'col'), 'rhs'), parts along dimension 0, may hold values from -6 to 6
Outputs:
- solution: float32 [131072, 256], P(('parts', 'row', 'col'), 'rhs'), parts along dimension 0
- residual: float32 [131072, 256], P(('parts', 'row', 'col'), 'rhs'), parts along dimension 0
The draws below stay inside these ranges and needn't reach their ends.
There are 2 independent parts, one for each index of `parts`. The reference program is written for one: setup_inputs(seed, part) draws one part's arguments, and reference() takes and returns one part's arrays. A program takes and returns all parts, laid end to end along the dimension named above; each array names one. Nothing has to cross between parts.
Inputs may be any that keep to these rules, and one draw needn't show every extreme that they name: Each tile's used slots are its first counts slots; the busiest tile has exactly 96. `block_rows`: used slots of one tile name distinct blocks on or above the diagonal. `block_cols`: see block_rows. `blocks`: unused slots hold values that do not enter the operator; the operator is positive definite.
All inputs are finite; a program needn't handle non-finite values.
Results may differ from the reference program's by a relative error of at most 0.0045.
Values may be sent and summed in bfloat16 or wider, within the bound.
A program may use at most 128 MiB of HBM per device.

```python
import math
import jax
import jax.numpy as jnp
from jax import lax

LAT = 65536
BS = 128
RHS = 256
BLK_DEV = 96
ITERS = 2
RB = 128
CB = 256
QB = 64
N_ROW = 4
N_COL = 2


def pattern(key):
    grid_rows = CB // QB
    grid_cols = RB // QB
    pairs = RB * CB
    inner = jnp.arange(pairs, dtype=jnp.int32)
    local_row = inner // CB
    local_col = inner % CB
    ridx = jnp.arange(grid_rows, dtype=jnp.int32)[:, None, None]
    cidx = jnp.arange(grid_cols, dtype=jnp.int32)[None, :, None]
    upper_i = ridx * RB + local_row[None, None, :]
    upper_j = (local_col[None, None, :] // QB * grid_cols + cidx) * QB + local_col[None, None, :] % QB
    valid = (upper_i <= upper_j).astype(jnp.int32)
    upper = jnp.sum(valid, axis=2)
    cap = jnp.minimum(BLK_DEV, upper).astype(jnp.int32)
    low = jnp.maximum(1, cap // 2).astype(jnp.int32)
    drawn = jax.random.randint(jax.random.fold_in(key, 5), (grid_rows, grid_cols), low, cap + 1, dtype=jnp.int32)
    flat = jnp.arange(grid_rows * grid_cols, dtype=jnp.int32).reshape(grid_rows, grid_cols)
    busiest = jnp.argmax(upper.reshape(-1)).astype(jnp.int32)
    counts = jnp.where(flat == busiest, BLK_DEV, drawn).astype(jnp.int32)
    span = 2 ** 28 // pairs
    noise = jax.random.randint(jax.random.fold_in(key, 7), (grid_rows, grid_cols, pairs), 0, span, dtype=jnp.int32)
    score = valid * 2 ** 28 + noise * pairs + inner[None, None, :]
    _, picked = lax.top_k(score, BLK_DEV)
    picked = picked.astype(jnp.int32)
    return (picked // CB, picked % CB, counts)


def draw_block_rows(key, part):
    return pattern(key)[0]


def draw_block_cols(key, part):
    return pattern(key)[1]


def draw_counts(key, part):
    return pattern(key)[2]


def draw_blocks(key, part):
    grid_rows = CB // QB
    grid_cols = RB // QB
    amp = 0.6 * (RB * CB / (BLK_DEV * LAT)) ** 0.5
    shape = (grid_rows, grid_cols, BLK_DEV, BS, BS)
    values = jax.random.uniform(jax.random.fold_in(key, 11), shape, jnp.float32, -1.0, 1.0)
    return (values * amp).astype(jnp.bfloat16)


def shard_levels(stream_key, dims, shards, least, largest):
    level = 1.0
    for axis_at, parts in shards:
        steps = jax.random.uniform(jax.random.fold_in(jax.random.fold_in(stream_key, 6), axis_at), (parts,), jnp.float32, least / len(shards), largest / len(shards))
        level = level * jnp.repeat(jnp.exp(steps), dims[axis_at] // parts).reshape((-1,) + (1,) * (len(dims) - 1 - axis_at))
    return level


def gaussian(rng, extent, width, limit, pieces=(), kind=jnp.bfloat16):
    loudness = shard_levels(rng, extent, pieces, -0.22, 0.18) if pieces else 1.0
    entries = jax.random.normal(rng, extent, jnp.float32) * width * loudness
    return jnp.minimum(jnp.maximum(entries, -limit), limit).astype(kind)


def setup_inputs(seed: int = 0, part: int = 0) -> dict:
    streams_of = jax.random.split(jax.random.key(seed), 7)
    own_keys = jax.random.split(jax.random.fold_in(streams_of[6], part), 7)
    return {
        "blocks": draw_blocks(jax.random.fold_in(jax.random.fold_in(streams_of[6], part), 71), part),
        "block_rows": draw_block_rows(jax.random.fold_in(jax.random.fold_in(streams_of[6], part), 71), part),
        "block_cols": draw_block_cols(jax.random.fold_in(jax.random.fold_in(streams_of[6], part), 71), part),
        "counts": draw_counts(jax.random.fold_in(jax.random.fold_in(streams_of[6], part), 71), part),
        "diagonal": jnp.clip(jnp.exp(math.log(4.0) - 1.2039728 * jax.random.uniform(own_keys[4], (LAT,), jnp.float32) ** shard_levels(own_keys[4], (LAT,), ((0, 8),), -0.2, 0.2)), 1.2, 4.0),
        "target": gaussian(own_keys[5], (LAT, RHS), 1.0, 6.0, ((0, 8), (1, 2)), jnp.float32),
    }


def tile_terms(blk, rows, cols, count, prow, pcol, nrb, ncb):
    hi = lax.Precision.HIGHEST
    valid = jnp.arange(blk.shape[0]) < count
    prod = jnp.einsum('kab,kbc->kac', blk, pcol[cols], precision=hi)
    rows_hot = ((rows[None, :] == jnp.arange(nrb)[:, None]) & valid[None, :]).astype(jnp.float32)
    direct = jnp.einsum('ik,kac->iac', rows_hot, prod, precision=hi)
    tprod = jnp.einsum('kba,kbc->kac', blk, prow[rows], precision=hi)
    cols_hot = ((cols[None, :] == jnp.arange(ncb)[:, None]) & valid[None, :]).astype(jnp.float32)
    mirrored = jnp.einsum('jk,kac->jac', cols_hot, tprod, precision=hi)
    return direct, mirrored


def rounded(value):
    return lax.optimization_barrier(value.astype(jnp.bfloat16)).astype(jnp.float32)


def operate(blocks, block_rows, block_cols, counts, diagonal, field):
    ncols = field.shape[1]
    grid = rounded(field).reshape(N_ROW, N_COL, QB * BS, ncols)

    def step(total, tile):
        ridx = tile // N_COL
        cidx = tile % N_COL
        prow = lax.dynamic_index_in_dim(grid, ridx, 0, keepdims=False).reshape(RB, BS, ncols)
        pcol = lax.dynamic_index_in_dim(grid, cidx, 1, keepdims=False).reshape(CB, BS, ncols)
        blk = blocks[ridx, cidx].astype(jnp.float32)
        direct, mirrored = tile_terms(blk, block_rows[ridx, cidx], block_cols[ridx, cidx], counts[ridx, cidx], prow, pcol, RB, CB)
        total = total.at[ridx].add(rounded(direct).reshape(N_COL, QB * BS, ncols))
        total = total.at[:, cidx].add(rounded(mirrored).reshape(N_ROW, QB * BS, ncols))
        return total, None

    start = jnp.zeros((N_ROW, N_COL, QB * BS, ncols), jnp.float32)
    total, _ = lax.scan(step, start, jnp.arange(N_ROW * N_COL, dtype=jnp.int32))
    return diagonal[:, None] * field + total.reshape(LAT, ncols)


def reference(blocks, block_rows, block_cols, counts, diagonal, target):
    solution = jnp.zeros_like(target)
    residual = target
    direction = target
    norm_now = jnp.sum(residual * residual, axis=0)
    for step in range(ITERS):
        image = operate(blocks, block_rows, block_cols, counts, diagonal, direction)
        alpha = norm_now / jnp.sum(direction * image, axis=0)
        solution = solution + alpha * direction
        residual = residual - alpha * image
        if step + 1 < ITERS:
            norm_next = jnp.sum(residual * residual, axis=0)
            direction = residual + (norm_next / norm_now) * direction
            norm_now = norm_next
    return solution, residual
```

```python
import functools
import jax
import jax.numpy as jnp
from jax import lax
from jax.experimental import pallas as pl
from jax.experimental.pallas import tpu as pltpu
from jax.sharding import PartitionSpec as P

ITERS = 2
UNROLL = 8
GATHER_BYTES = 32 * 2**20
MESH = pl.DeviceIdType.MESH
ANY = pl.BlockSpec(memory_space=pl.ANY)


def flipped(index, bits, devices):
    total, unit = index, 1
    while unit < devices:
        if bits & unit:
            total = total + unit * (1 - 2 * lax.rem(index // unit, 2))
        unit *= 2
    return total


def spread_kernel(
    nrow, stored, target, names, diag,
    tiles, field, theirs, all_names, all_diag,
    parcel, ring_send, ring_recv, send, recv, own_sem, pair_sem,
):
    devices = 2 * nrow
    row, col, core = lax.axis_index("row"), lax.axis_index("col"), lax.axis_index("rhs")
    me = row * 2 + col
    place = jnp.where(col == 0, row, devices - 1 - row)

    def device_at(place):
        place = lax.rem(place + devices, devices)
        back = place >= nrow
        return jnp.where(back, devices - 1 - place, place), jnp.where(back, 1, 0)

    def peer(offset):
        other = lax.rem(me + offset, devices)
        return {"row": other // 2, "col": lax.rem(other, 2)}

    barrier = pltpu.get_barrier_semaphore()
    for offset in range(1, devices):
        pl.semaphore_signal(barrier, inc=1, device_id=peer(offset), device_id_type=MESH)
    sibling = {"rhs": 1 - core}
    pl.semaphore_signal(barrier, inc=1, device_id=sibling, device_id_type=MESH)
    pl.semaphore_wait(barrier, devices)

    half = tiles.shape[1]
    lanes = ring_send.shape[0]
    piece = half // lanes
    hops = []

    def hop(lane, step):
        way = lane % 2
        r, c = device_at(place + (1 if way == 0 else -1))
        if step == 0:
            source = stored.at[pl.ds(lane * piece, piece), core]
            origin = me
        else:
            orow, ocol = device_at(place + (-step if way == 0 else step))
            origin = orow * 2 + ocol
            source = tiles.at[origin, pl.ds(lane * piece, piece)]
        copy = pltpu.make_async_remote_copy(
            src_ref=source,
            dst_ref=tiles.at[origin, pl.ds(lane * piece, piece)],
            send_sem=ring_send.at[lane, step],
            recv_sem=ring_recv.at[lane, step],
            device_id={"row": r, "col": c},
            device_id_type=MESH,
        )
        copy.start()
        return copy

    now = [hop(lane, 0) for lane in range(lanes)]

    def pack(b, carry):
        low = target[b].astype(jnp.bfloat16).T
        parcel[:, b] = low.reshape(devices, parcel.shape[2], parcel.shape[3])
        return carry

    lax.fori_loop(0, target.shape[0], pack, 0)
    straight = []
    pairs = ((names, all_names, False), (diag, all_diag, False), (parcel, field, True))
    for n, (source, whole, apart) in enumerate(pairs):
        for offset in range(1, devices):
            copy = pltpu.make_async_remote_copy(
                src_ref=source.at[lax.rem(me + offset, devices)] if apart else source,
                dst_ref=whole.at[me],
                send_sem=send.at[n, offset - 1],
                recv_sem=recv.at[n, offset - 1],
                device_id=peer(offset),
                device_id_type=MESH,
            )
            copy.start()
            straight.append(copy)
    local = []
    owns = (
        (stored.at[:, core], tiles.at[me]),
        (names, all_names.at[me]),
        (diag, all_diag.at[me]),
        (parcel.at[me], field.at[me]),
    )
    for n, (source, whole) in enumerate(owns):
        copy = pltpu.make_async_copy(source, whole, own_sem.at[n])
        copy.start()
        local.append(copy)
    for step in range(1, devices):
        if step == devices - 1:
            for copy in straight:
                copy.wait()
            for copy in local:
                copy.wait()
            pair = pltpu.make_async_remote_copy(
                src_ref=field,
                dst_ref=theirs,
                send_sem=pair_sem.at[0],
                recv_sem=pair_sem.at[1],
                device_id=sibling,
                device_id_type=MESH,
            )
            pair.start()
        for lane in range(lanes):
            now[lane].wait_recv()
            if step < devices - 1:
                hops.append(now[lane])
                now[lane] = hop(lane, step)
    hops += now
    for copy in hops:
        copy.wait_send()
    pair.wait()


def spread(stored, target, names, diag):
    nrow = lax.axis_size("row")
    devices = 2 * nrow
    half, cores, width, _ = stored.shape
    parcel = (devices, target.shape[0], target.shape[2] // devices, target.shape[1])
    lanes = 6 if half % 6 == 0 else 2
    return pl.pallas_call(
        functools.partial(spread_kernel, nrow),
        out_shape=(
            jax.ShapeDtypeStruct((devices, half, width, width), stored.dtype),
            jax.ShapeDtypeStruct(parcel, jnp.bfloat16),
            jax.ShapeDtypeStruct(parcel, jnp.bfloat16),
            jax.ShapeDtypeStruct((devices,) + names.shape, names.dtype),
            jax.ShapeDtypeStruct((devices,) + diag.shape, diag.dtype),
        ),
        in_specs=[ANY, pl.BlockSpec(memory_space=pltpu.VMEM), ANY, ANY],
        out_specs=[ANY] * 5,
        scratch_shapes=[
            pltpu.VMEM(parcel, jnp.bfloat16),
            pltpu.SemaphoreType.DMA((lanes, devices - 1)),
            pltpu.SemaphoreType.DMA((lanes, devices - 1)),
            pltpu.SemaphoreType.DMA((3, devices - 1)),
            pltpu.SemaphoreType.DMA((3, devices - 1)),
            pltpu.SemaphoreType.DMA((4,)),
            pltpu.SemaphoreType.DMA((2,)),
        ],
        compiler_params=pltpu.CompilerParams(collective_id=0, has_side_effects=True),
    )(stored, target, names, diag)


def home_kernel(nrow, early, first, parcel, scale, late, field, scales, send, recv, own_sem):
    devices = 2 * nrow
    me = lax.axis_index("row") * 2 + lax.axis_index("col")

    def peer(bits):
        other = flipped(me, bits, devices)
        return {"row": other // 2, "col": lax.rem(other, 2)}

    barrier = pltpu.get_barrier_semaphore()
    for offset in range(1, devices):
        pl.semaphore_signal(barrier, inc=1, device_id=peer(offset), device_id_type=MESH)
    pl.semaphore_wait(barrier, devices - 1)
    copies = []
    rest = pl.ds(early, late.shape[1] - early)
    for n in range(3):
        for offset in range(1, devices):
            to = flipped(me, offset, devices)
            if n == 0:
                source, target = scale, scales.at[me]
            elif n == 2:
                source, target = parcel.at[to], field.at[me]
            elif offset < devices // 2:
                source, target = first.at[to], late.at[me]
            else:
                source, target = first.at[to, rest], late.at[me, rest]
            copy = pltpu.make_async_remote_copy(
                src_ref=source,
                dst_ref=target,
                send_sem=send.at[n, offset - 1],
                recv_sem=recv.at[n, offset - 1],
                device_id=peer(offset),
                device_id_type=MESH,
            )
            copy.start()
            copies.append(copy)
    owns = (
        (scale, scales.at[me]),
        (first.at[me], late.at[me]),
        (parcel.at[me], field.at[me]),
    )
    for n, (source, target) in enumerate(owns):
        copy = pltpu.make_async_copy(source, target, own_sem.at[n])
        copy.start()
        copies.append(copy)
    for copy in copies:
        copy.wait()


def send_home(first, parcel, scale, early):
    nrow = lax.axis_size("row")
    devices = parcel.shape[0]
    return pl.pallas_call(
        functools.partial(home_kernel, nrow, early),
        out_shape=(
            jax.ShapeDtypeStruct(parcel.shape, parcel.dtype),
            jax.ShapeDtypeStruct(parcel.shape, parcel.dtype),
            jax.ShapeDtypeStruct((devices,) + scale.shape, scale.dtype),
        ),
        in_specs=[ANY] * 3,
        out_specs=[ANY] * 3,
        scratch_shapes=[
            pltpu.SemaphoreType.DMA((3, devices - 1)),
            pltpu.SemaphoreType.DMA((3, devices - 1)),
            pltpu.SemaphoreType.DMA((3,)),
        ],
        compiler_params=pltpu.CompilerParams(collective_id=1, has_side_effects=True),
    )(first, parcel, scale)


def finish_kernel(last, me_ref, target_ref, diag_ref, early_ref, late_ref, second_ref, scale_ref,
                  answer_ref, residual_ref, first_ref):
    blocks, width, columns = target_ref.shape
    alpha1, alpha2, beta = scale_ref[0:1], scale_ref[1:2], scale_ref[2:3]
    devices = second_ref.shape[0]
    first_ref[...] = late_ref[...]

    @pl.when(pl.program_id(0) < last)
    def _():
        for far in range(devices // 2):
            first_ref[me_ref[0] ^ (devices // 2 + far)] = early_ref[far]

    diags = diag_ref[...].T
    for b in range(blocks):
        target = target_ref[b]
        diag = diags[:, b : b + 1]
        first = first_ref[:, b].reshape(columns, width).T.astype(jnp.float32)
        second = second_ref[:, b].reshape(columns, width).T.astype(jnp.float32)
        lost = target - target.astype(jnp.bfloat16).astype(jnp.float32)
        lost1 = lost - alpha1 * diag * lost
        answer_ref[b] = alpha1 * target + alpha2 * (first + lost1 + beta * target)
        residual_ref[b] = second + lost1 - alpha2 * diag * (lost1 + beta * lost)


def finish(me, target, diag, early, late, second, scales):
    blocks, width, columns = target.shape
    devices, _, own, _ = second.shape
    step = 8
    last = early.shape[1] // step
    whole = pl.BlockSpec((step, width, columns), lambda g: (g, 0, 0))
    part = pl.BlockSpec((devices, step, own, width), lambda g: (0, g, 0, 0))
    return pl.pallas_call(
        functools.partial(finish_kernel, last),
        out_shape=(jax.ShapeDtypeStruct(target.shape, jnp.float32),) * 2,
        grid=(blocks // step,),
        in_specs=[
            pl.BlockSpec(memory_space=pltpu.SMEM),
            whole,
            pl.BlockSpec((step, width), lambda g: (g, 0)),
            pl.BlockSpec(early.shape[:1] + (step, own, width), lambda g: (0, jnp.minimum(g, last - 1), 0, 0)),
            part,
            part,
            pl.BlockSpec(scales.shape, lambda g: (0, 0)),
        ],
        out_specs=(whole, whole),
        scratch_shapes=[pltpu.VMEM((devices, step, own, width), jnp.bfloat16)],
    )(me, target, diag, early, late, second, scales)


def operate_kernel(slots, irow_ref, icol_ref, count_ref, blocks_ref, mine_ref, theirs_ref,
                   image_ref, away_ref, sum_ref):
    tile = pl.program_id(0)
    own = mine_ref.shape[1]

    @pl.when(tile == 0)
    def _():
        image_ref[...] = jnp.zeros_like(image_ref)
        sum_ref[...] = jnp.zeros_like(sum_ref)

    count = count_ref[tile]

    def group(step, carry):
        base = step * UNROLL
        terms = []
        for u in range(UNROLL):
            k = base + u
            i = irow_ref[tile * slots + k]
            j = icol_ref[tile * slots + k]
            block = blocks_ref[0, k]
            at_i = jnp.concatenate([mine_ref[i], theirs_ref[i]], axis=0)
            at_j = jnp.concatenate([mine_ref[j], theirs_ref[j]], axis=0)
            direct = lax.dot_general(
                at_j, block, (((1,), (1,)), ((), ())), preferred_element_type=jnp.float32
            )
            mirrored = lax.dot_general(
                at_i, block, (((1,), (0,)), ((), ())), preferred_element_type=jnp.float32
            )
            terms.append((k < count, i, j, direct, mirrored))
        for used, i, j, direct, mirrored in terms:
            direct = jnp.where(used, direct, 0.0)
            mirrored = jnp.where(used, mirrored, 0.0)
            image_ref[i] += direct[:own]
            sum_ref[i] += direct[own:]
            image_ref[j] += mirrored[:own]
            sum_ref[j] += mirrored[own:]
        return carry

    lax.fori_loop(0, (count + UNROLL - 1) // UNROLL, group, 0)

    @pl.when(tile == pl.num_programs(0) - 1)
    def _():
        away_ref[...] = sum_ref[...].astype(away_ref.dtype)


def operate(blocks, irow, icol, count, mine, theirs):
    tiles, slots, width, _ = blocks.shape
    whole = pl.BlockSpec(mine.shape, lambda t, *_: (0, 0, 0))
    return pl.pallas_call(
        functools.partial(operate_kernel, slots),
        out_shape=(
            jax.ShapeDtypeStruct(mine.shape, jnp.float32),
            jax.ShapeDtypeStruct(mine.shape, jnp.bfloat16),
        ),
        grid_spec=pltpu.PrefetchScalarGridSpec(
            num_scalar_prefetch=3,
            grid=(tiles,),
            in_specs=[
                pl.BlockSpec((1, slots, width, width), lambda t, *_: (t, 0, 0, 0)),
                whole,
                whole,
            ],
            out_specs=(whole, whole),
            scratch_shapes=[pltpu.VMEM(mine.shape, jnp.float32)],
        ),
        compiler_params=pltpu.CompilerParams(vmem_limit_bytes=40 * 2**20),
        cost_estimate=pl.CostEstimate(
            flops=tiles * slots * width**3 * 4, bytes_accessed=60 * 2**20, transcendentals=0
        ),
    )(irow, icol, count, blocks, mine, theirs)


def by_columns(blocks, block_rows, block_cols, counts, diagonal, target):
    grid = ("row", "col")
    nrow, ncol = lax.axis_size("row"), lax.axis_size("col")
    devices = nrow * ncol
    stored = blocks[0, 0]
    slots, width, _ = stored.shape
    quarter = target.shape[0] // width
    own = target.shape[1] // devices
    row_blocks = ncol * quarter
    half = slots // 2
    row, col, core = lax.axis_index("row"), lax.axis_index("col"), lax.axis_index("rhs")

    irow = row * row_blocks + block_rows[0, 0]
    jcol = block_cols[0, 0]
    icol = (jcol // quarter * ncol + col) * quarter + jcol % quarter

    def every_other(index):
        return jnp.where(core == 0, index[0::2], index[1::2])

    used = (counts[0] - core + 1) // 2
    names = jnp.concatenate([every_other(irow), every_other(icol), used])
    names = jnp.pad(names, (0, -names.shape[0] % 1024)).reshape(-1, 128)
    diag_own = diagonal.reshape(quarter, width)
    target_blocks = target.reshape(quarter, width, target.shape[1])

    tiles, field, field_pair, all_names, all_diag = spread(
        stored.reshape(half, 2, width, width), target_blocks, names, diag_own
    )
    all_names = all_names.reshape(devices, -1)
    irows = all_names[:, :half].reshape(-1)
    icols = all_names[:, half : 2 * half].reshape(-1)
    used = all_names[:, 2 * half]
    diag = all_diag.reshape(-1, 1, width)
    swap = [(0, 1), (1, 0)]

    def image_of(direction, low, theirs, beside=()):
        here, away = operate(tiles, irows, icols, used, low, theirs)
        (here, away), beside = lax.optimization_barrier(((here, away), beside))
        away = lax.ppermute(away, "rhs", swap)
        return diag * direction + here + away.astype(jnp.float32), beside

    def inner(a, b):
        return jnp.sum(a * b, axis=(0, 2), keepdims=True)

    me = row * ncol + col

    def parcels(value):
        return value.astype(jnp.bfloat16).reshape(devices, quarter, own, width)

    def far_home(parcel):
        pieces = []
        for bits in range(devices // 2, devices):
            piece = lax.dynamic_index_in_dim(parcel, me ^ bits, 0, keepdims=False)
            pieces.append(lax.ppermute(piece, grid, [(d, d ^ bits) for d in range(devices)]))
        return pieces

    low = field.reshape(-1, own, width)
    start = low.astype(jnp.float32)
    norm0 = inner(start, start)
    image, _ = image_of(start, low, field_pair.reshape(low.shape))
    alpha1 = norm0 / inner(start, image)
    first = start - alpha1 * image
    norm1 = inner(first, first)
    beta = norm1 / norm0
    direction = first + beta * start
    first_parcel = parcels(first)
    early = quarter // 8 * 5
    pieces = far_home(first_parcel[:, :early])
    low = direction.astype(jnp.bfloat16)
    image, pieces = image_of(direction, low, lax.ppermute(low, "rhs", swap), pieces)
    first_early = jnp.stack(pieces)
    alpha2 = norm1 / inner(direction, image)
    second = first - alpha2 * image
    scale = jnp.stack([alpha1, alpha2, beta]).reshape(3, own)
    scale = jnp.pad(scale, ((0, 5), (0, 128 - own)))
    first_late, second_home, scales = send_home(first_parcel, parcels(second), scale, early)
    scales = scales[:, :3, :own]
    scales = scales.transpose(1, 0, 2).reshape(3, devices * own)
    answer, residual = finish(
        me.reshape(1), target_blocks, diag_own, first_early, first_late, second_home, scales
    )
    return (answer.reshape(target.shape), residual.reshape(target.shape))


def one_hot_slots(indices, valid, extent):
    return ((indices[None, :] == jnp.arange(extent)[:, None]) & valid[None, :]).astype(jnp.float32)


def picked(blocks, index):
    return lax.map(lambda i: lax.dynamic_index_in_dim(blocks, i, 0, keepdims=False), index)


def on_device(blocks, block_rows, block_cols, counts, diagonal, target):
    highest = lax.Precision.HIGHEST
    nrow = lax.axis_size("row")
    ncol = lax.axis_size("col")
    tile_bytes = blocks[0, 0].size * blocks.dtype.itemsize
    if (
        nrow * ncol * tile_bytes <= GATHER_BYTES
        and ncol == 2
        and nrow & (nrow - 1) == 0
        and lax.axis_size("rhs") == 2
        and target.shape[1] == 16 * nrow * ncol
        and blocks.shape[2] % (2 * UNROLL) == 0
        and target.shape[0] // blocks.shape[3] % 64 == 0
    ):
        return by_columns(blocks, block_rows, block_cols, counts, diagonal, target)
    stored = blocks[0, 0]
    slots = stored.shape[0]
    width = stored.shape[1]
    local = target.shape[0]
    ncols = target.shape[1]
    quarter = local // width
    row_blocks = ncol * quarter
    col_blocks = nrow * quarter
    valid = jnp.arange(slots) < counts[0, 0]
    rows_hot = one_hot_slots(block_rows[0, 0], valid, row_blocks)
    cols_hot = one_hot_slots(block_cols[0, 0], valid, col_blocks)

    def squares(vector):
        return lax.psum(jnp.sum(vector * vector, axis=0), ("row", "col"))

    solution = jnp.zeros_like(target)
    residual = target
    direction = target
    norm_now = squares(residual)
    for step in range(ITERS):
        operate_field_low = direction.astype(jnp.bfloat16)
        direct_gathered = lax.all_gather(operate_field_low, "row", axis=0, tiled=True).reshape(
            col_blocks, width, ncols
        )
        prod = jnp.einsum(
            "kab,kbc->kac",
            stored,
            picked(direct_gathered, block_cols[0, 0]),
            preferred_element_type=jnp.float32,
        )
        direct_partial_value = jnp.einsum("ik,kac->iac", rows_hot, prod, precision=highest)
        direct = lax.psum_scatter(
            direct_partial_value.reshape(row_blocks * width, ncols).astype(jnp.bfloat16),
            "col",
            scatter_dimension=0,
            tiled=True,
        ).astype(jnp.float32)
        gathered = lax.all_gather(operate_field_low, "col", axis=0, tiled=True).reshape(
            row_blocks, width, ncols
        )
        tprod = jnp.einsum(
            "kba,kbc->kac",
            stored,
            picked(gathered, block_rows[0, 0]),
            preferred_element_type=jnp.float32,
        )
        partial_value = jnp.einsum("jk,kac->jac", cols_hot, tprod, precision=highest)
        parcel = partial_value.astype(jnp.bfloat16).reshape(nrow, local, ncols)
        mirrored = jnp.sum(
            lax.all_to_all(parcel, "row", split_axis=0, concat_axis=0, tiled=True).astype(
                jnp.float32
            ),
            axis=0,
        )
        image = diagonal[:, None] * direction + direct + mirrored
        curve = lax.psum(jnp.sum(direction * image, axis=0), ("row", "col"))
        alpha = norm_now / curve
        solution = solution + alpha * direction
        residual = residual - alpha * image
        if step + 1 < ITERS:
            norm_next = squares(residual)
            direction = residual + norm_next / norm_now * direction
            norm_now = norm_next
    return (solution, residual)


def solution(mesh):
    return jax.shard_map(
        on_device,
        mesh=mesh,
        in_specs=(
            P(("parts", "row"), "col", None, None, None),
            P(("parts", "row"), "col", None),
            P(("parts", "row"), "col", None),
            P(("parts", "row"), "col"),
            P(("parts", "row", "col")),
            P(("parts", "row", "col"), "rhs"),
        ),
        out_specs=(P(("parts", "row", "col"), "rhs"), P(("parts", "row", "col"), "rhs")),
        check_vma=False,
    )
```

```python
import functools
import jax
import jax.numpy as jnp
from jax import lax
from jax.experimental import pallas as pl
from jax.experimental.pallas import tpu as pltpu
from jax.sharding import PartitionSpec as P

ITERS = 2
UNROLL = 8
PIECES = 6
MESH = pl.DeviceIdType.MESH
ANY = pl.BlockSpec(memory_space=pl.ANY)


ROUTES = (
    (
        (0, 0, 0, 2, 1, 2),
        (0, 0, 0, 0, 2, 1),
        (0, 0, 0, 3, 1, 2),
        (0, 0, 0, 1, 1, 2),
        (0, 0, 0, 4, 0, 2),
        (0, 0, 0, 5, 1, 0),
        (1, 1, 1, 0, 2),
        (0, 0, 1, 4, 1),
        (0, 1, 0, 1, 0),
        (0, 0, 1, 5, 2),
        (1, 1, 1, 2, 2),
        (0, 1, 0, 2, 0),
        (0, 0, 1, 2),
        (0, 1, 0, 5),
        (0, 1, 1, 1),
        (0, 0, 1, 0),
        (0, 1, 1, 2, 1),
        (0, 2, 0, 1, 2),
        (0, 1, 1, 4, 1, 0),
        (0, 1, 1, 3, 0, 2),
        (0, 1, 1, 0, 0, 1),
        (0, 2, 0, 2, 0, 2),
        (0, 1, 0, 4),
        (0, 0, 1, 1, 2),
        (0, 1, 0, 3),
        (0, 2, 0, 3),
        (0, 1, 0, 0, 1),
        (0, 1, 1, 5),
        (0, 2, 1, 2, 2),
        (0, 2, 1, 0, 0),
        (0, 0, 1, 3),
        (0, 2, 1, 3),
        (0, 2, 1, 5, 2),
        (0, 2, 0, 0),
        (0, 3, 0, 0, 0),
        (0, 3, 1, 5, 2),
        (0, 2, 0, 4, 0),
        (0, 3, 1, 0, 2, 1),
        (0, 2, 0, 5),
        (0, 3, 1, 4, 0),
        (0, 2, 1, 1),
        (0, 2, 1, 4),
        (0, 3, 0, 2, 0, 2),
        (0, 3, 0, 1),
        (0, 3, 0, 4, 1, 2),
        (0, 3, 0, 5),
        (0, 3, 1, 3),
        (0, 3, 1, 2),
        (0, 3, 0, 3),
        (0, 3, 1, 1),
    ),
    (
        (1, 1, 0, 5, 2),
        (1, 1, 0, 4, 2),
        (1, 1, 0, 0, 1),
        (1, 1, 0, 3, 2),
        (1, 1, 0, 1, 2),
        (1, 1, 0, 2, 1),
        (0, 0, 0, 2, 0),
        (0, 0, 0, 0, 0),
        (0, 0, 1, 2, 1, 2),
        (0, 1, 0, 5, 1),
        (0, 0, 0, 3, 2, 0),
        (0, 0, 1, 0, 1),
        (0, 1, 0, 3, 0),
        (0, 0, 0, 1, 0),
        (0, 2, 0, 1, 1, 0),
        (0, 0, 1, 3),
        (0, 0, 0, 5, 2, 0),
        (0, 1, 0, 1, 0),
        (0, 1, 1, 3, 1, 2),
        (0, 2, 0, 2, 1, 0),
        (0, 0, 1, 1, 1, 2),
        (0, 0, 1, 4, 2, 0),
        (0, 2, 1, 1),
        (0, 2, 0, 3, 0, 1),
        (0, 0, 1, 5),
        (0, 2, 0, 0),
        (0, 1, 1, 1),
        (0, 1, 1, 5, 1),
        (0, 1, 1, 2, 0, 2),
        (0, 2, 1, 2),
        (0, 2, 1, 0, 1),
        (0, 0, 0, 4),
        (0, 2, 0, 4, 0),
        (0, 1, 1, 4, 0),
        (0, 2, 1, 3, 1),
        (0, 2, 1, 5, 1, 0),
        (0, 1, 1, 0),
        (0, 1, 0, 2, 2),
        (0, 3, 0, 0, 1),
        (0, 2, 1, 4),
        (0, 3, 1, 5, 1, 0),
        (0, 1, 0, 0, 2),
        (0, 1, 0, 4),
        (0, 3, 0, 1),
        (0, 2, 0, 5, 1),
        (0, 3, 1, 4, 1),
        (0, 3, 0, 2, 1, 0),
        (0, 3, 0, 5, 1),
        (0, 3, 1, 3, 0),
        (0, 3, 1, 2),
        (0, 3, 1, 0),
        (0, 3, 1, 1),
        (0, 3, 0, 3, 1),
        (0, 3, 0, 4),
    ),
    (
        (0, 1, 0, 5, 0, 1),
        (0, 1, 0, 3, 1),
        (0, 1, 0, 4, 0),
        (0, 1, 0, 0, 0),
        (0, 1, 0, 1, 1, 2, 0),
        (0, 1, 0, 2, 2, 0),
        (0, 0, 0, 2, 0, 1),
        (0, 1, 1, 5, 1),
        (1, 0, 1, 1, 3),
        (0, 0, 0, 0, 1),
        (0, 1, 1, 4, 2, 1),
        (1, 0, 1, 2, 3),
        (0, 0, 0, 3, 0),
        (1, 0, 1, 3, 3),
        (0, 1, 1, 0, 2, 1),
        (0, 0, 0, 1, 1),
        (1, 0, 1, 0, 3),
        (0, 1, 1, 1, 1),
        (1, 0, 1, 5, 3),
        (0, 0, 0, 4),
        (0, 1, 1, 2),
        (1, 0, 1, 4, 3),
        (1, 1, 1, 5, 3),
        (0, 0, 1, 2),
        (1, 1, 1, 4, 3),
        (1, 1, 1, 3, 3),
        (1, 1, 1, 0, 3),
        (0, 0, 1, 3, 2),
        (1, 1, 1, 1, 3),
        (0, 0, 1, 5),
        (0, 2, 0, 3, 0),
        (1, 1, 1, 2, 3),
        (0, 2, 0, 0),
        (0, 2, 0, 5),
        (0, 2, 0, 1, 0),
        (0, 2, 1, 0),
        (0, 1, 1, 3),
        (0, 2, 0, 4, 2, 0),
        (0, 2, 0, 2),
        (0, 2, 1, 3),
        (0, 0, 1, 0),
        (0, 0, 1, 1),
        (0, 3, 0, 3, 0),
        (0, 2, 1, 2, 1),
        (0, 2, 1, 1, 2),
        (0, 3, 0, 1, 0, 2),
        (0, 2, 1, 5),
        (0, 2, 1, 4),
        (0, 3, 1, 4),
        (0, 3, 1, 5, 0),
        (0, 3, 1, 3, 2),
        (0, 0, 0, 5),
        (0, 3, 1, 0, 0, 1),
        (0, 3, 1, 1, 2),
        (0, 3, 1, 2),
        (0, 3, 0, 5),
        (0, 3, 0, 2),
        (0, 0, 1, 4),
        (0, 3, 0, 0),
        (0, 3, 0, 4),
    ),
    (
        (1, 0, 0, 1, 1),
        (1, 0, 0, 2, 1),
        (1, 0, 0, 3, 1),
        (1, 0, 0, 0, 1),
        (1, 0, 0, 5, 1),
        (1, 0, 0, 4, 1),
        (1, 1, 1, 5, 1),
        (0, 1, 0, 5, 2),
        (1, 1, 1, 4, 1),
        (0, 1, 0, 3, 2),
        (0, 2, 0, 1, 2, 0),
        (1, 1, 1, 3, 1),
        (0, 1, 0, 1, 2),
        (0, 2, 0, 2, 2),
        (0, 2, 1, 1),
        (1, 1, 1, 1, 1),
        (0, 2, 0, 3, 2, 1, 0),
        (0, 0, 0, 2),
        (0, 2, 0, 0, 0, 2, 1),
        (0, 2, 1, 3),
        (0, 1, 1, 5, 2),
        (0, 2, 0, 5, 0, 1),
        (0, 2, 1, 0, 2, 1),
        (0, 0, 0, 0, 0),
        (0, 2, 0, 4, 1, 2, 0),
        (0, 2, 1, 5, 2),
        (0, 1, 1, 4, 0),
        (0, 3, 0, 5, 0),
        (0, 0, 1, 0, 1),
        (0, 3, 0, 4, 0),
        (0, 2, 1, 4),
        (0, 1, 1, 0),
        (0, 3, 0, 3, 0, 1),
        (0, 1, 0, 4),
        (0, 0, 0, 1),
        (0, 3, 0, 0, 2),
        (0, 3, 1, 5, 2),
        (0, 1, 1, 1),
        (0, 3, 0, 1, 1, 0, 2),
        (0, 3, 1, 4, 2, 1),
        (0, 0, 1, 2),
        (0, 3, 0, 2, 2, 0),
        (0, 3, 1, 3, 2),
        (0, 0, 0, 3, 0),
        (0, 3, 1, 1, 2),
        (0, 0, 0, 5, 1, 0),
        (0, 3, 1, 2, 1),
        (0, 1, 1, 3),
        (0, 0, 1, 3),
        (0, 0, 1, 1),
        (0, 0, 1, 5),
        (0, 0, 1, 4, 1, 0),
        (0, 1, 1, 2),
        (0, 2, 1, 2),
        (0, 0, 0, 4),
        (0, 1, 0, 2),
        (0, 1, 0, 0),
        (0, 3, 1, 0),
    ),
)


def flipped(index, bits, devices):
    total, unit = index, 1
    while unit < devices:
        if bits & unit:
            total = total + unit * (1 - 2 * lax.rem(index // unit, 2))
        unit *= 2
    return total


class Place:
    def __init__(self):
        self.part, self.row = lax.axis_index("parts"), lax.axis_index("row")
        self.col, self.core = lax.axis_index("col"), lax.axis_index("rhs")
        self.half = self.row // 2
        self.low = lax.rem(self.row, 2)
        self.shard = self.row * 2 + self.col
        self.group = self.low * 4 + self.part * 2 + self.col
        self.foreign = lax.rem(self.half + self.part, 2)
        self.inner = lax.rem(self.half + self.low, 2)

    def link(self, way):
        if way == 0:
            return {"col": 1 - self.col}
        if way == 1:
            return {"parts": 1 - self.part}
        if way == 2:
            return {"row": self.half * 2 + 1 - self.low}
        return {"row": 3 - self.row}

    def tile_row(self, kind):
        return (3 * self.half, 1 + self.half, 2 - self.half, 3 - 3 * self.half)[kind]

    def solver(self, group):
        return {
            "row": 2 * self.part + group // 4,
            "parts": lax.rem(group // 2, 2),
            "col": lax.rem(group, 2),
        }

    def owner(self, shard):
        return {"row": shard // 2, "parts": self.half, "col": lax.rem(shard, 2)}


def greet_all(place, sibling):
    barrier = pltpu.get_barrier_semaphore()
    me = place.part * 8 + place.shard
    for offset in range(1, 16):
        other = lax.rem(me + offset, 16)
        peer = {"parts": other // 8, "row": lax.rem(other, 8) // 2, "col": lax.rem(other, 2)}
        pl.semaphore_signal(barrier, inc=1, device_id=peer, device_id_type=MESH)
    if sibling:
        pl.semaphore_signal(barrier, inc=1, device_id={"rhs": 1 - place.core}, device_id_type=MESH)
    pl.semaphore_wait(barrier, 15 + sibling)


def spread_kernel(
    stored, target, names, diag,
    tiles, field, theirs, all_names, all_diag, transit,
    parcel, piece_send, piece_recv, pass_recv, send, recv, own_sem, pair_sem,
):
    place = Place()
    shard, core, foreign = place.shard, place.core, place.foreign
    half = tiles.shape[1]
    size = half // PIECES
    greet_all(place, 1)

    def part_of(k):
        return pl.ds(k * size, size)

    def piece_copy(source, target, way, send_sem, recv_sem):
        return pltpu.make_async_remote_copy(
            src_ref=source, dst_ref=target, send_sem=send_sem, recv_sem=recv_sem,
            device_id=place.link(way), device_id_type=MESH,
        )

    def run(kind, entries, count, do_wait):
        for entry in entries:
            own = kind in (0, 2) and entry[0] == 0 and entry[1] == kind // 2 and entry[2] == 0
            own = own or (entry[0] == 1 and entry[2] == 0)
            k = entry[3]
            if entry[0] == 0:
                s = place.tile_row(entry[1]) * 2 + (1 - place.col if entry[2] else place.col)
                source = stored.at[part_of(k), core] if own else tiles.at[s, part_of(k)]
            else:
                row = place.tile_row(1 if entry[1] == 0 else 0)
                s = row * 2 + place.col
                source = stored.at[part_of(k), core] if own else transit.at[entry[1], part_of(k)]
            if own == do_wait:
                if not do_wait:
                    continue
                count += len(entry) - 4
                continue
            if not own:
                if entry[0] == 0:
                    landed, sem = tiles.at[s, part_of(k)], piece_recv.at[s, k]
                else:
                    landed, sem = transit.at[entry[1], part_of(k)], pass_recv.at[entry[1], k]
                piece_copy(landed, landed, 0, piece_send.at[0], sem).wait_recv()
            for way in entry[4:]:
                if entry[0] == 0 or way == 3:
                    target, sem = tiles.at[s, part_of(k)], piece_recv.at[s, k]
                else:
                    target, sem = transit.at[entry[1], part_of(k)], pass_recv.at[entry[1], k]
                piece_copy(source, target, way, piece_send.at[count], sem).start()
                count += 1
        return count

    def each_class(body):
        for kind in range(4):
            @pl.when((foreign == kind % 2) & (place.inner == kind // 2))
            def _(kind=kind):
                body(kind, ROUTES[kind])

    each_class(lambda kind, entries: run(kind, entries, 0, False))

    def pack(b, carry):
        low = target[b].astype(jnp.bfloat16).T
        parcel[:, b] = low.reshape(parcel.shape[0], parcel.shape[2], parcel.shape[3])
        return carry

    lax.fori_loop(0, target.shape[0], pack, 0)
    pairs = ((names, all_names), (diag, all_diag), (parcel, field))
    mine = (lambda n: parcel.at[place.group] if n == 2 else pairs[n][0])

    def straight(n, bits):
        group = flipped(place.group, bits, 8)
        return pltpu.make_async_remote_copy(
            src_ref=parcel.at[group] if n == 2 else pairs[n][0],
            dst_ref=pairs[n][1].at[shard],
            send_sem=send.at[n, bits],
            recv_sem=recv.at[n, shard],
            device_id=place.solver(group),
            device_id_type=MESH,
        )

    def arrival(n, bits):
        landed = pairs[n][1].at[flipped(shard, bits, 8)]
        return pltpu.make_async_remote_copy(
            src_ref=landed, dst_ref=landed, send_sem=send.at[n, 0],
            recv_sem=recv.at[n, flipped(shard, bits, 8)],
            device_id=place.link(0), device_id_type=MESH,
        )

    def local(n):
        if n == 3:
            return pltpu.make_async_copy(stored.at[:, core], tiles.at[shard], own_sem.at[n])
        return pltpu.make_async_copy(mine(n), pairs[n][1].at[shard], own_sem.at[n])

    for n in range(3):
        for bits in range(1, 8):
            straight(n, bits).start()

    @pl.when(foreign == 1)
    def _():
        for n in range(3):
            straight(n, 0).start()

    @pl.when(foreign == 0)
    def _():
        for n in range(4):
            local(n).start()

    each_class(lambda kind, entries: run(kind, entries, 0, True))

    for n in range(3):
        for bits in range(1, 8):
            arrival(n, bits).wait_recv()

    @pl.when(foreign == 1)
    def _():
        for n in range(3):
            arrival(n, 0).wait_recv()

    @pl.when(foreign == 0)
    def _():
        for n in range(4):
            local(n).wait()

    pair = pltpu.make_async_remote_copy(
        src_ref=field, dst_ref=theirs, send_sem=pair_sem.at[0], recv_sem=pair_sem.at[1],
        device_id={"rhs": 1 - core}, device_id_type=MESH,
    )
    pair.start()
    for n in range(3):
        for bits in range(1, 8):
            straight(n, bits).wait_send()

    @pl.when(foreign == 1)
    def _():
        for n in range(3):
            straight(n, 0).wait_send()

    def sent(kind, entries):
        total = sum(len(entry) - 4 for entry in entries)
        block = stored.at[part_of(0), core]
        for n in range(total):
            piece_copy(block, tiles.at[shard, part_of(0)], 0, piece_send.at[n], piece_recv.at[shard, 0]).wait_send()

    each_class(sent)
    pair.wait()


def spread(stored, target, names, diag):
    half, cores, width, _ = stored.shape
    parcel = (8, target.shape[0], target.shape[2] // 8, target.shape[1])
    sends = max(sum(len(entry) - 4 for entry in entries) for entries in ROUTES)
    return pl.pallas_call(
        spread_kernel,
        out_shape=(
            jax.ShapeDtypeStruct((8, half, width, width), stored.dtype),
            jax.ShapeDtypeStruct(parcel, jnp.bfloat16),
            jax.ShapeDtypeStruct(parcel, jnp.bfloat16),
            jax.ShapeDtypeStruct((8,) + names.shape, names.dtype),
            jax.ShapeDtypeStruct((8,) + diag.shape, diag.dtype),
            jax.ShapeDtypeStruct((2, half, width, width), stored.dtype),
        ),
        in_specs=[ANY, pl.BlockSpec(memory_space=pltpu.VMEM), ANY, ANY],
        out_specs=[ANY] * 6,
        scratch_shapes=[
            pltpu.VMEM(parcel, jnp.bfloat16),
            pltpu.SemaphoreType.DMA((sends,)),
            pltpu.SemaphoreType.DMA((8, PIECES)),
            pltpu.SemaphoreType.DMA((2, PIECES)),
            pltpu.SemaphoreType.DMA((3, 8)),
            pltpu.SemaphoreType.DMA((3, 8)),
            pltpu.SemaphoreType.DMA((4,)),
            pltpu.SemaphoreType.DMA((2,)),
        ],
        compiler_params=pltpu.CompilerParams(collective_id=0, has_side_effects=True),
    )(stored, target, names, diag)[:5]


def home_kernel(first, second, scale, first_home, second_home, scales, send, recv, own_sem):
    place = Place()
    foreign = place.foreign
    greet_all(place, 0)
    pairs = ((scale, scales), (first, first_home), (second, second_home))

    def copy(n, bits):
        to = flipped(place.shard, bits, 8)
        return pltpu.make_async_remote_copy(
            src_ref=pairs[n][0].at[to] if n else scale,
            dst_ref=pairs[n][1].at[place.group],
            send_sem=send.at[n, bits],
            recv_sem=recv.at[n, place.group],
            device_id=place.owner(to),
            device_id_type=MESH,
        )

    def arrival(n, bits):
        landed = pairs[n][1].at[flipped(place.group, bits, 8)]
        return pltpu.make_async_remote_copy(
            src_ref=landed, dst_ref=landed, send_sem=send.at[n, 0],
            recv_sem=recv.at[n, flipped(place.group, bits, 8)],
            device_id=place.link(0), device_id_type=MESH,
        )

    def local(n):
        return pltpu.make_async_copy(
            pairs[n][0].at[place.shard] if n else scale, pairs[n][1].at[place.group], own_sem.at[n]
        )

    for n in range(3):
        for bits in range(1, 8):
            copy(n, bits).start()

        @pl.when(foreign == 1)
        def _(n=n):
            copy(n, 0).start()

        @pl.when(foreign == 0)
        def _(n=n):
            local(n).start()

    for n in range(3):
        for bits in range(1, 8):
            copy(n, bits).wait_send()
            arrival(n, bits).wait_recv()

        @pl.when(foreign == 1)
        def _(n=n):
            copy(n, 0).wait_send()
            arrival(n, 0).wait_recv()

        @pl.when(foreign == 0)
        def _(n=n):
            local(n).wait()


def send_home(first, second, scale):
    return pl.pallas_call(
        home_kernel,
        out_shape=(
            jax.ShapeDtypeStruct(first.shape, first.dtype),
            jax.ShapeDtypeStruct(second.shape, second.dtype),
            jax.ShapeDtypeStruct((8,) + scale.shape, scale.dtype),
        ),
        in_specs=[ANY] * 3,
        out_specs=[ANY] * 3,
        scratch_shapes=[
            pltpu.SemaphoreType.DMA((3, 8)),
            pltpu.SemaphoreType.DMA((3, 8)),
            pltpu.SemaphoreType.DMA((3,)),
        ],
        compiler_params=pltpu.CompilerParams(collective_id=1, has_side_effects=True),
    )(first, second, scale)


def finish_kernel(target_ref, diag_ref, first_ref, second_ref, scale_ref, answer_ref, residual_ref):
    blocks, width, columns = target_ref.shape
    alpha1, alpha2, beta = scale_ref[0:1], scale_ref[1:2], scale_ref[2:3]
    diags = diag_ref[...].T
    for b in range(blocks):
        target = target_ref[b]
        diag = diags[:, b : b + 1]
        first = first_ref[:, b].reshape(columns, width).T.astype(jnp.float32)
        second = second_ref[:, b].reshape(columns, width).T.astype(jnp.float32)
        lost = target - target.astype(jnp.bfloat16).astype(jnp.float32)
        lost1 = lost - alpha1 * diag * lost
        answer_ref[b] = alpha1 * target + alpha2 * (first + lost1 + beta * target)
        residual_ref[b] = second + lost1 - alpha2 * diag * (lost1 + beta * lost)


def finish(target, diag, first, second, scales):
    blocks, width, columns = target.shape
    devices, _, own, _ = second.shape
    step = 8
    whole = pl.BlockSpec((step, width, columns), lambda g: (g, 0, 0))
    part = pl.BlockSpec((devices, step, own, width), lambda g: (0, g, 0, 0))
    return pl.pallas_call(
        finish_kernel,
        out_shape=(jax.ShapeDtypeStruct(target.shape, jnp.float32),) * 2,
        grid=(blocks // step,),
        in_specs=[
            whole,
            pl.BlockSpec((step, width), lambda g: (g, 0)),
            part,
            part,
            pl.BlockSpec(scales.shape, lambda g: (0, 0)),
        ],
        out_specs=(whole, whole),
    )(target, diag, first, second, scales)


def operate_kernel(slots, irow_ref, icol_ref, count_ref, blocks_ref, mine_ref, theirs_ref,
                   image_ref, away_ref, sum_ref):
    tile = pl.program_id(0)
    own = mine_ref.shape[1]

    @pl.when(tile == 0)
    def _():
        image_ref[...] = jnp.zeros_like(image_ref)
        sum_ref[...] = jnp.zeros_like(sum_ref)

    count = count_ref[tile]

    def group(step, carry):
        base = step * UNROLL
        terms = []
        for u in range(UNROLL):
            k = base + u
            i = irow_ref[tile * slots + k]
            j = icol_ref[tile * slots + k]
            block = blocks_ref[0, k]
            at_i = jnp.concatenate([mine_ref[i], theirs_ref[i]], axis=0)
            at_j = jnp.concatenate([mine_ref[j], theirs_ref[j]], axis=0)
            direct = lax.dot_general(
                at_j, block, (((1,), (1,)), ((), ())), preferred_element_type=jnp.float32
            )
            mirrored = lax.dot_general(
                at_i, block, (((1,), (0,)), ((), ())), preferred_element_type=jnp.float32
            )
            terms.append((k < count, i, j, direct, mirrored))
        for used, i, j, direct, mirrored in terms:
            direct = jnp.where(used, direct, 0.0)
            mirrored = jnp.where(used, mirrored, 0.0)
            image_ref[i] += direct[:own]
            sum_ref[i] += direct[own:]
            image_ref[j] += mirrored[:own]
            sum_ref[j] += mirrored[own:]
        return carry

    lax.fori_loop(0, (count + UNROLL - 1) // UNROLL, group, 0)

    @pl.when(tile == pl.num_programs(0) - 1)
    def _():
        away_ref[...] = sum_ref[...].astype(away_ref.dtype)


def operate(blocks, irow, icol, count, mine, theirs):
    tiles, slots, width, _ = blocks.shape
    whole = pl.BlockSpec(mine.shape, lambda t, *_: (0, 0, 0))
    return pl.pallas_call(
        functools.partial(operate_kernel, slots),
        out_shape=(
            jax.ShapeDtypeStruct(mine.shape, jnp.float32),
            jax.ShapeDtypeStruct(mine.shape, jnp.bfloat16),
        ),
        grid_spec=pltpu.PrefetchScalarGridSpec(
            num_scalar_prefetch=3,
            grid=(tiles,),
            in_specs=[
                pl.BlockSpec((1, slots, width, width), lambda t, *_: (t, 0, 0, 0)),
                whole,
                whole,
            ],
            out_specs=(whole, whole),
            scratch_shapes=[pltpu.VMEM(mine.shape, jnp.float32)],
        ),
        compiler_params=pltpu.CompilerParams(vmem_limit_bytes=40 * 2**20),
        cost_estimate=pl.CostEstimate(
            flops=tiles * slots * width**3 * 4, bytes_accessed=60 * 2**20, transcendentals=0
        ),
    )(irow, icol, count, blocks, mine, theirs)


def by_columns(blocks, block_rows, block_cols, counts, diagonal, target):
    nrow, ncol = lax.axis_size("row"), lax.axis_size("col")
    devices = nrow * ncol
    stored = blocks[0, 0]
    slots, width, _ = stored.shape
    quarter = target.shape[0] // width
    own = target.shape[1] // devices
    row_blocks = ncol * quarter
    half = slots // 2
    row, col, core = lax.axis_index("row"), lax.axis_index("col"), lax.axis_index("rhs")

    irow = row * row_blocks + block_rows[0, 0]
    jcol = block_cols[0, 0]
    icol = (jcol // quarter * ncol + col) * quarter + jcol % quarter

    def every_other(index):
        return jnp.where(core == 0, index[0::2], index[1::2])

    used = (counts[0] - core + 1) // 2
    names = jnp.concatenate([every_other(irow), every_other(icol), used])
    names = jnp.pad(names, (0, -names.shape[0] % 1024)).reshape(-1, 128)
    diag_own = diagonal.reshape(quarter, width)
    target_blocks = target.reshape(quarter, width, target.shape[1])

    tiles, field, field_pair, all_names, all_diag = spread(
        stored.reshape(half, 2, width, width), target_blocks, names, diag_own
    )
    all_names = all_names.reshape(devices, -1)
    irows = all_names[:, :half].reshape(-1)
    icols = all_names[:, half : 2 * half].reshape(-1)
    used = all_names[:, 2 * half]
    diag = all_diag.reshape(-1, 1, width)
    swap = [(0, 1), (1, 0)]

    def image_of(direction, low, theirs):
        here, away = operate(tiles, irows, icols, used, low, theirs)
        away = lax.ppermute(away, "rhs", swap)
        return diag * direction + here + away.astype(jnp.float32)

    def inner(a, b):
        return jnp.sum(a * b, axis=(0, 2), keepdims=True)

    def parcels(value):
        return value.astype(jnp.bfloat16).reshape(devices, quarter, own, width)

    low = field.reshape(-1, own, width)
    start = low.astype(jnp.float32)
    norm0 = inner(start, start)
    image = image_of(start, low, field_pair.reshape(low.shape))
    alpha1 = norm0 / inner(start, image)
    first = start - alpha1 * image
    norm1 = inner(first, first)
    beta = norm1 / norm0
    direction = first + beta * start
    first_parcel = parcels(first)
    low = direction.astype(jnp.bfloat16)
    image = image_of(direction, low, lax.ppermute(low, "rhs", swap))
    alpha2 = norm1 / inner(direction, image)
    second = first - alpha2 * image
    scale = jnp.stack([alpha1, alpha2, beta]).reshape(3, own)
    scale = jnp.pad(scale, ((0, 5), (0, 128 - own)))
    first_home, second_home, scales = send_home(first_parcel, parcels(second), scale)
    scales = scales[:, :3, :own]
    scales = scales.transpose(1, 0, 2).reshape(3, devices * own)
    answer, residual = finish(target_blocks, diag_own, first_home, second_home, scales)
    return (answer.reshape(target.shape), residual.reshape(target.shape))


def one_hot_slots(indices, valid, extent):
    return ((indices[None, :] == jnp.arange(extent)[:, None]) & valid[None, :]).astype(jnp.float32)


def picked(blocks, index):
    return lax.map(lambda i: lax.dynamic_index_in_dim(blocks, i, 0, keepdims=False), index)


def on_device(blocks, block_rows, block_cols, counts, diagonal, target):
    highest = lax.Precision.HIGHEST
    nrow = lax.axis_size("row")
    ncol = lax.axis_size("col")
    if (
        (lax.axis_size("parts"), nrow, ncol, lax.axis_size("rhs")) == (2, 4, 2, 2)
        and target.shape[1] == 128
        and blocks.shape[2] % (16 * PIECES) == 0
        and target.shape[0] // blocks.shape[3] % 64 == 0
    ):
        return by_columns(blocks, block_rows, block_cols, counts, diagonal, target)
    stored = blocks[0, 0]
    slots = stored.shape[0]
    width = stored.shape[1]
    local = target.shape[0]
    ncols = target.shape[1]
    quarter = local // width
    row_blocks = ncol * quarter
    col_blocks = nrow * quarter
    valid = jnp.arange(slots) < counts[0, 0]
    rows_hot = one_hot_slots(block_rows[0, 0], valid, row_blocks)
    cols_hot = one_hot_slots(block_cols[0, 0], valid, col_blocks)

    def squares(vector):
        return lax.psum(jnp.sum(vector * vector, axis=0), ("row", "col"))

    solution = jnp.zeros_like(target)
    residual = target
    direction = target
    norm_now = squares(residual)
    for step in range(ITERS):
        operate_field_low = direction.astype(jnp.bfloat16)
        direct_gathered = lax.all_gather(operate_field_low, "row", axis=0, tiled=True).reshape(
            col_blocks, width, ncols
        )
        prod = jnp.einsum(
            "kab,kbc->kac",
            stored,
            picked(direct_gathered, block_cols[0, 0]),
            preferred_element_type=jnp.float32,
        )
        direct_partial_value = jnp.einsum("ik,kac->iac", rows_hot, prod, precision=highest)
        direct = lax.psum_scatter(
            direct_partial_value.reshape(row_blocks * width, ncols).astype(jnp.bfloat16),
            "col",
            scatter_dimension=0,
            tiled=True,
        ).astype(jnp.float32)
        gathered = lax.all_gather(operate_field_low, "col", axis=0, tiled=True).reshape(
            row_blocks, width, ncols
        )
        tprod = jnp.einsum(
            "kba,kbc->kac",
            stored,
            picked(gathered, block_rows[0, 0]),
            preferred_element_type=jnp.float32,
        )
        partial_value = jnp.einsum("jk,kac->jac", cols_hot, tprod, precision=highest)
        parcel = partial_value.astype(jnp.bfloat16).reshape(nrow, local, ncols)
        mirrored = jnp.sum(
            lax.all_to_all(parcel, "row", split_axis=0, concat_axis=0, tiled=True).astype(
                jnp.float32
            ),
            axis=0,
        )
        image = diagonal[:, None] * direction + direct + mirrored
        curve = lax.psum(jnp.sum(direction * image, axis=0), ("row", "col"))
        alpha = norm_now / curve
        solution = solution + alpha * direction
        residual = residual - alpha * image
        if step + 1 < ITERS:
            norm_next = squares(residual)
            direction = residual + norm_next / norm_now * direction
            norm_now = norm_next
    return (solution, residual)


def solution(mesh):
    return jax.shard_map(
        on_device,
        mesh=mesh,
        in_specs=(
            P(("parts", "row"), "col", None, None, None),
            P(("parts", "row"), "col", None),
            P(("parts", "row"), "col", None),
            P(("parts", "row"), "col"),
            P(("parts", "row", "col")),
            P(("parts", "row", "col"), "rhs"),
        ),
        out_specs=(P(("parts", "row", "col"), "rhs"), P(("parts", "row", "col"), "rhs")),
        check_vma=False,
    )
```

```python
import functools
import jax
import jax.numpy as jnp
from jax import lax
from jax.experimental import pallas as pl
from jax.experimental.pallas import tpu as pltpu
from jax.sharding import PartitionSpec as P

ITERS = 2
UNROLL = 8
PIECES = 6
MESH = pl.DeviceIdType.MESH
ANY = pl.BlockSpec(memory_space=pl.ANY)


HOLD = 19
ROUTES = (
    (
        (0,0,0,0,0,1), (0,0,0,3,1), (2,0,3,0,0,0,-1,0,1), (2,0,2,0,0,0,-1,-1,2), (0,0,0,5,2), (0,0,0,1,0,2),
        (2,0,0,1,0,0,-1,-1,0), (2,0,1,0,0,0,-1,-1,1), (2,0,2,1,0,0,-1,0,2), (2,0,1,1,0,0,-1,0,0), (0,0,0,2,0),
        (2,0,3,1,0,0,-1,1,1), (0,0,0,4,0,1), (0,0,1,0,2), (1,1,1,4,2), (1,1,1,3,2), (0,0,1,1,1),
        (2,2,0,1,0,0,2,-1,0), (1,1,1,1,2), (2,0,0,1,1,0,-1,-1,-1), (0,1,0,0), (1,1,1,0,2), (2,0,1,1,1,0,0,-1,1),
        (0,1,0,4,1), (1,1,1,2,2), (0,0,1,2,1), (2,2,0,0,0,0,-1,-1,-1), (1,1,1,5,2), (0,0,1,4,2), (0,1,1,0,1),
        (0,1,0,1,0), (2,2,0,1,1,0,-1,-1,-1), (2,3,0,0,0,0,-1,-1,-1), (0,0,1,3), (0,1,1,2,0,1), (0,1,1,1), (0,2,0,5),
        (0,1,1,5,0), (0,1,0,2,1), (0,2,0,2,0), (2,3,0,1,0,0,3,-1,0), (0,1,0,5,1), (0,2,0,0,2,0), (0,1,1,4),
        (0,2,1,2,2), (0,2,0,1,0), (0,1,1,3), (2,3,0,1,1,0,-1,-1,-1), (0,2,0,3,0,2), (2,3,1,1,1,0,4,-1,1), (0,2,1,0),
        (2,1,1,0,0,0,1,-1,1), (0,2,1,1,1), (0,2,1,5), (0,2,1,3,2), (0,2,1,4,0), (2,1,0,0,0,0,-1,-1,-1),
        (0,3,0,1,2,0), (0,2,0,4), (2,1,0,1,1,0,-1,-1,-1), (0,3,1,4,0,2), (0,3,1,1,1), (0,3,1,3,0), (0,3,0,2,2),
        (0,3,0,4), (0,3,0,0,1), (0,0,1,5), (0,3,0,3,1), (0,3,0,5,0), (0,3,1,2), (0,3,1,0), (0,3,1,5), (0,1,0,3),
    ),
    (
        (1,1,0,4,1), (1,1,0,3,1), (2,1,3,1,0,1,-1,11,2), (2,1,1,0,0,1,-1,3,2), (2,1,3,0,0,1,-1,10,2),
        (2,1,1,1,0,1,-1,4,2), (2,1,2,0,0,1,-1,7,2), (1,1,0,1,1), (2,1,0,1,0,1,-1,1,2), (1,1,0,0,1),
        (2,1,0,0,0,1,-1,0,2), (1,1,0,2,1), (1,1,0,5,1), (2,1,2,1,0,1,-1,8,2), (0,0,0,0,0), (0,0,0,3,0), (0,0,1,0),
        (0,1,0,1,1,0), (2,0,3,0,0,0,0,-1,2), (0,0,1,3,2,1), (0,2,0,5,1,0), (2,0,1,0,0,0,-1,-1,-1), (0,1,1,1),
        (0,2,0,2,1,0), (2,0,3,1,0,0,1,2,0), (0,2,1,5), (0,2,0,0,1,0), (0,0,0,4), (0,2,1,2), (2,2,1,1,0,0,3,-1,0),
        (0,0,1,1,0), (2,0,3,1,1,0,2,-1,2), (0,2,0,1,1), (2,0,1,1,1,0,-1,-1,-1), (0,2,1,0), (0,2,0,3,1,0),
        (0,1,0,4,0), (2,2,1,1,1,0,-1,-1,-1), (2,2,1,0,0,0,-1,-1,-1), (0,0,1,2,0,2), (0,0,0,1,2), (0,2,0,4,0),
        (0,1,1,0,0), (0,2,1,3,2), (2,3,1,0,0,0,-1,-1,-1), (0,1,1,2,2), (0,1,1,4,2), (0,3,0,4,0), (0,1,0,2),
        (0,0,0,2,2), (0,0,0,5,0), (0,1,0,5,0,2), (0,2,1,4,1), (0,3,0,1,1), (2,3,1,1,1,0,-1,-1,-1), (0,1,0,0),
        (2,1,1,1,1,0,-1,-1,-1), (2,1,1,0,0,0,-1,-1,-1), (0,3,1,4,1), (0,3,0,2,1,0), (0,2,1,1), (0,0,1,5,1,2),
        (0,1,1,3,0), (0,1,1,5), (0,3,0,5,0), (0,3,1,1), (0,3,1,2,1,2), (0,3,1,0), (0,1,0,3,1), (0,3,0,0), (0,0,1,4),
        (0,3,1,5), (0,3,0,3), (0,3,1,3),
    ),
    (
        (0,1,0,1,1,0), (2,2,3,0,0,0,-1,-1,1), (2,2,0,1,0,0,-1,2,2), (0,1,0,0,0,2,1), (0,1,0,2,0,1),
        (2,2,1,1,0,0,-1,13,1), (2,2,3,1,0,0,-1,14,1), (0,1,0,5,0), (2,2,1,0,0,0,-1,12,1), (2,2,2,1,0,0,-1,-1,0),
        (0,1,0,4,2,0), (2,2,0,0,0,0,-1,-1,2), (0,1,0,3,0), (1,0,1,5,3), (0,1,1,1), (1,0,1,2,3),
        (2,0,2,0,0,0,-1,-1,-1), (2,3,1,0,0,0,10,15,1), (0,1,1,0,2,1), (1,0,1,0,3), (0,0,0,5,1,0),
        (2,3,0,0,0,0,8,-1,2), (0,1,1,2,2), (1,0,1,1,3), (0,0,0,1,0), (2,3,2,0,0,0,-1,-1,-1), (0,1,1,5,2,1),
        (1,0,1,3,3), (2,3,3,0,0,0,12,-1,1), (2,0,2,1,0,0,0,-1,0), (2,2,2,1,1,0,-1,-1,-1), (1,0,1,4,3),
        (2,3,0,1,0,0,9,3,2), (0,1,1,4,2), (0,0,1,0,1), (2,1,3,1,0,1,6,7,0), (0,1,1,3,1,2), (1,1,1,4,3),
        (2,3,1,1,1,0,11,4,2), (0,2,0,5,0), (1,1,1,3,3), (2,1,1,0,0,0,3,1,2), (0,0,1,5), (0,2,0,4), (1,1,1,1,3),
        (2,3,2,1,1,0,-1,-1,-1), (0,0,1,1,1), (2,1,1,1,1,1,4,6,3), (1,1,1,0,3), (2,1,3,0,0,0,5,-1,1),
        (2,0,2,1,1,0,-1,-1,-1), (0,3,0,4), (2,3,3,1,1,0,13,-1,1), (1,1,1,2,3), (2,1,3,1,1,1,7,-1,3), (0,2,1,1,0),
        (1,1,1,5,3), (2,1,2,0,0,0,-1,-1,-1), (0,2,1,5,2), (0,3,0,3,0), (0,0,1,4,1,0), (2,1,0,0,0,0,1,-1,2),
        (0,2,0,1), (0,0,1,3,0), (0,2,0,0,0), (2,1,0,1,1,0,2,-1,2), (0,3,1,3,2,1), (0,2,1,4), (0,2,1,2,0), (0,0,0,4),
        (2,1,2,1,1,0,-1,-1,-1), (0,3,0,0,2,0), (0,2,0,3), (0,0,0,3), (0,0,1,2), (0,2,1,3), (0,2,1,0,1), (0,3,0,5,2),
        (0,3,0,1,0), (0,2,0,2), (0,0,0,0), (0,3,1,4), (0,3,1,0,2), (0,0,0,2), (0,3,0,2,0), (0,3,1,1,1), (0,3,1,5),
        (0,3,1,2),
    ),
    (
        (1,0,0,5,1), (1,0,0,2,1), (2,3,1,1,0,1,-1,16,0), (2,3,1,0,0,1,-1,10,3), (1,0,0,0,1), (2,3,0,0,0,1,-1,8,3),
        (1,0,0,1,1), (2,3,2,0,0,1,-1,-1,3), (2,3,2,1,0,1,-1,17,0), (1,0,0,3,1), (1,0,0,4,1), (2,3,3,0,0,1,-1,12,3),
        (2,3,0,1,0,1,-1,9,3), (2,3,3,1,0,1,-1,18,0), (0,1,0,1,2,0), (2,1,3,1,0,1,11,6,1), (2,3,1,1,1,1,16,11,3),
        (2,2,3,0,0,0,-1,-1,-1), (0,2,0,5,1,2,0), (2,1,1,0,0,1,3,3,3), (0,1,0,0), (2,3,2,1,1,1,17,-1,3),
        (0,2,0,2,2,0), (2,1,3,0,0,1,10,5,3), (0,1,0,2), (2,3,3,1,1,1,18,13,3), (0,2,0,0,2), (2,1,1,1,0,1,4,5,0),
        (2,2,1,1,0,0,13,3,2), (0,1,1,1), (0,2,0,1,2,0), (2,1,2,0,0,1,7,-1,3), (2,2,3,1,0,0,14,-1,0), (0,2,1,5),
        (0,2,0,3,2), (2,1,0,1,0,1,1,2,0), (2,2,1,0,0,0,12,-1,2), (0,2,1,2), (0,2,0,4,2,0,1), (2,1,0,0,0,1,0,1,3),
        (2,3,1,0,0,0,15,-1,2), (2,1,1,1,1,1,5,4,1), (0,3,0,4,2,1,0), (2,1,2,1,0,1,8,9,0), (0,1,1,0), (0,2,1,1,1),
        (0,3,0,3,1), (2,0,3,0,0,0,-1,-1,-1), (0,0,0,5,2), (2,2,3,1,1,0,-1,-1,-1), (0,3,0,1,2), (0,0,1,3,1,0),
        (0,1,1,5), (2,1,0,1,1,1,2,2,3), (2,1,1,1,1,0,6,-1,2), (2,3,3,0,0,0,-1,-1,-1), (2,0,3,1,1,0,-1,-1,-1),
        (0,2,1,4,1), (0,3,0,0,1,0), (0,0,1,0,0), (0,3,1,4), (0,0,1,2,1), (0,3,0,2,2), (0,1,1,3,2,0),
        (2,1,2,1,1,1,9,-1,3), (0,0,0,1), (2,1,3,1,1,0,-1,-1,-1), (0,0,1,1), (0,0,0,3), (0,2,1,3), (0,3,0,5,1,2,0),
        (2,1,3,0,0,0,-1,-1,-1), (0,1,1,2), (0,3,1,0,2), (2,3,3,1,1,0,-1,-1,-1), (0,1,1,4,0), (0,0,0,0,1),
        (0,0,1,4,2,0), (0,0,0,2,1), (0,1,0,3), (0,1,0,5), (0,3,1,3,2), (0,3,1,5,1), (0,1,0,4), (0,0,1,5), (0,2,1,0),
        (0,0,0,4), (0,3,1,2), (0,3,1,1),
    ),
)


def flipped(index, bits, devices):
    total, unit = index, 1
    while unit < devices:
        if bits & unit:
            total = total + unit * (1 - 2 * lax.rem(index // unit, 2))
        unit *= 2
    return total


class Place:
    def __init__(self):
        self.part, self.row = lax.axis_index("parts"), lax.axis_index("row")
        self.col, self.core = lax.axis_index("col"), lax.axis_index("rhs")
        self.half = self.row // 2
        self.low = lax.rem(self.row, 2)
        self.shard = self.row * 2 + self.col
        self.group = self.low * 4 + self.part * 2 + self.col
        self.foreign = lax.rem(self.half + self.part, 2)
        self.inner = lax.rem(self.half + self.low, 2)

    def link(self, way):
        if way == 0:
            return {"col": 1 - self.col}
        if way == 1:
            return {"parts": 1 - self.part}
        if way == 2:
            return {"row": self.half * 2 + 1 - self.low}
        return {"row": 3 - self.row}

    def tile_row(self, kind):
        return (3 * self.half, 1 + self.half, 2 - self.half, 3 - 3 * self.half)[kind]

    def solver(self, group):
        return {
            "row": 2 * self.part + group // 4,
            "parts": lax.rem(group // 2, 2),
            "col": lax.rem(group, 2),
        }

    def owner(self, shard):
        return {"row": shard // 2, "parts": self.half, "col": lax.rem(shard, 2)}


def greet_all(place, sibling):
    barrier = pltpu.get_barrier_semaphore()
    me = place.part * 8 + place.shard
    for offset in range(1, 16):
        other = lax.rem(me + offset, 16)
        peer = {"parts": other // 8, "row": lax.rem(other, 8) // 2, "col": lax.rem(other, 2)}
        pl.semaphore_signal(barrier, inc=1, device_id=peer, device_id_type=MESH)
    if sibling:
        pl.semaphore_signal(barrier, inc=1, device_id={"rhs": 1 - place.core}, device_id_type=MESH)
    pl.semaphore_wait(barrier, 15 + sibling)


def spread_kernel(
    stored, target, names, diag,
    tiles, field, theirs, all_names, all_diag, transit, hold,
    parcel, piece_send, piece_recv, pass_recv, hold_recv, send, recv, own_sem, pair_sem,
):
    place = Place()
    shard, core, foreign = place.shard, place.core, place.foreign
    half = tiles.shape[1]
    size = half // PIECES
    greet_all(place, 1)

    def part_of(k):
        return pl.ds(k * size, size)

    def piece_copy(source, target, way, send_sem, recv_sem):
        return pltpu.make_async_remote_copy(
            src_ref=source, dst_ref=target, send_sem=send_sem, recv_sem=recv_sem,
            device_id=place.link(way), device_id_type=MESH,
        )

    def source_shard(entry):
        solved = place.half if entry[5] == 0 else 1 - place.half
        row = (3 * solved, 3 - 3 * solved, 1 + solved, 2 - solved)[entry[1]]
        return row * 2 + (1 - place.col if entry[4] else place.col)

    def dest_group(entry):
        low = lax.rem(entry[2] // 2 + place.part, 2)
        part = 1 - place.part if entry[2] % 2 else place.part
        return low * 4 + part * 2 + (1 - place.col if entry[3] else place.col)

    def step(kind, entry, count):
        if entry[0] == 2:
            slot_in, slot_out, way = entry[6:]
            if entry[4] == 0 and slot_in < 0 and way >= 0:
                source = parcel.at[dest_group(entry)]
            elif way < 0:
                s = source_shard(entry)
                piece_copy(field.at[s], field.at[s], 0, piece_send.at[0], recv.at[2, s]).wait_recv()
                return count
            else:
                source = hold.at[slot_in]
                piece_copy(source, source, 0, piece_send.at[0], hold_recv.at[slot_in]).wait_recv()
            if slot_out < 0:
                s = source_shard(entry)
                target, sem = field.at[s], recv.at[2, s]
            else:
                target, sem = hold.at[slot_out], hold_recv.at[slot_out]
            piece_copy(source, target, way, piece_send.at[count], sem).start()
            return count + 1
        k = entry[3]
        if entry[0] == 0:
            s = place.tile_row(entry[1]) * 2 + (1 - place.col if entry[2] else place.col)
            own = kind in (0, 2) and entry[1] == kind // 2 and entry[2] == 0
            source, sem = tiles.at[s, part_of(k)], piece_recv.at[s, k]
        else:
            s = place.tile_row(1 - entry[1]) * 2 + place.col
            own = entry[2] == 0
            source, sem = transit.at[entry[1], part_of(k)], pass_recv.at[entry[1], k]
        if own:
            source = stored.at[part_of(k), core]
        else:
            piece_copy(source, source, 0, piece_send.at[0], sem).wait_recv()
        for way in entry[4:]:
            if entry[0] == 0 or way == 3:
                target, sem = tiles.at[s, part_of(k)], piece_recv.at[s, k]
            else:
                target, sem = transit.at[entry[1], part_of(k)], pass_recv.at[entry[1], k]
            piece_copy(source, target, way, piece_send.at[count], sem).start()
            count += 1
        return count

    def sends(entry):
        return int(entry[8] >= 0) if entry[0] == 2 else len(entry) - 4

    def each_class(body):
        for kind in range(4):
            @pl.when((foreign == kind % 2) & (place.inner == kind // 2))
            def _(kind=kind):
                entries = ROUTES[kind]
                first = [entry[0] for entry in entries].index(2)
                body(kind, entries, first)

    def before_pack(kind, entries, first):
        count = 0
        for entry in entries[:first]:
            count = step(kind, entry, count)

    def after_pack(kind, entries, first):
        count = sum(sends(entry) for entry in entries[:first])
        for entry in entries[first:]:
            count = step(kind, entry, count)

    each_class(before_pack)

    def pack(b, carry):
        low = target[b].astype(jnp.bfloat16).T
        parcel[:, b] = low.reshape(parcel.shape[0], parcel.shape[2], parcel.shape[3])
        return carry

    lax.fori_loop(0, target.shape[0], pack, 0)
    pairs = ((names, all_names), (diag, all_diag), (parcel, field))
    mine = (lambda n: parcel.at[place.group] if n == 2 else pairs[n][0])

    def straight(n, bits):
        group = flipped(place.group, bits, 8)
        return pltpu.make_async_remote_copy(
            src_ref=parcel.at[group] if n == 2 else pairs[n][0],
            dst_ref=pairs[n][1].at[shard],
            send_sem=send.at[n, bits],
            recv_sem=recv.at[n, shard],
            device_id=place.solver(group),
            device_id_type=MESH,
        )

    def arrival(n, bits):
        landed = pairs[n][1].at[flipped(shard, bits, 8)]
        return pltpu.make_async_remote_copy(
            src_ref=landed, dst_ref=landed, send_sem=send.at[n, 0],
            recv_sem=recv.at[n, flipped(shard, bits, 8)],
            device_id=place.link(0), device_id_type=MESH,
        )

    def local(n):
        if n == 3:
            return pltpu.make_async_copy(stored.at[:, core], tiles.at[shard], own_sem.at[n])
        return pltpu.make_async_copy(mine(n), pairs[n][1].at[shard], own_sem.at[n])

    for n in range(2):
        for bits in range(1, 8):
            straight(n, bits).start()

    @pl.when(foreign == 1)
    def _():
        for n in range(2):
            straight(n, 0).start()

    @pl.when(foreign == 0)
    def _():
        for n in range(4):
            local(n).start()

    each_class(after_pack)

    for n in range(2):
        for bits in range(1, 8):
            arrival(n, bits).wait_recv()

    @pl.when(foreign == 1)
    def _():
        for n in range(2):
            arrival(n, 0).wait_recv()

    @pl.when(foreign == 0)
    def _():
        for n in range(4):
            local(n).wait()

    pair = pltpu.make_async_remote_copy(
        src_ref=field, dst_ref=theirs, send_sem=pair_sem.at[0], recv_sem=pair_sem.at[1],
        device_id={"rhs": 1 - core}, device_id_type=MESH,
    )
    pair.start()
    for n in range(2):
        for bits in range(1, 8):
            straight(n, bits).wait_send()

    @pl.when(foreign == 1)
    def _():
        for n in range(2):
            straight(n, 0).wait_send()

    def sent(kind, entries, first):
        count = 0
        for entry in entries:
            for _ in range(sends(entry)):
                block = parcel.at[0] if entry[0] == 2 else stored.at[part_of(0), core]
                piece_copy(block, block, 0, piece_send.at[count], piece_recv.at[shard, 0]).wait_send()
                count += 1

    each_class(sent)
    pair.wait()


def spread(stored, target, names, diag):
    half, cores, width, _ = stored.shape
    parcel = (8, target.shape[0], target.shape[2] // 8, target.shape[1])
    sends = max(
        sum(int(e[8] >= 0) if e[0] == 2 else len(e) - 4 for e in entries) for entries in ROUTES
    )
    return pl.pallas_call(
        spread_kernel,
        out_shape=(
            jax.ShapeDtypeStruct((8, half, width, width), stored.dtype),
            jax.ShapeDtypeStruct(parcel, jnp.bfloat16),
            jax.ShapeDtypeStruct(parcel, jnp.bfloat16),
            jax.ShapeDtypeStruct((8,) + names.shape, names.dtype),
            jax.ShapeDtypeStruct((8,) + diag.shape, diag.dtype),
            jax.ShapeDtypeStruct((2, half, width, width), stored.dtype),
            jax.ShapeDtypeStruct((HOLD,) + parcel[1:], jnp.bfloat16),
        ),
        in_specs=[ANY, pl.BlockSpec(memory_space=pltpu.VMEM), ANY, ANY],
        out_specs=[ANY] * 7,
        scratch_shapes=[
            pltpu.VMEM(parcel, jnp.bfloat16),
            pltpu.SemaphoreType.DMA((sends,)),
            pltpu.SemaphoreType.DMA((8, PIECES)),
            pltpu.SemaphoreType.DMA((2, PIECES)),
            pltpu.SemaphoreType.DMA((HOLD,)),
            pltpu.SemaphoreType.DMA((3, 8)),
            pltpu.SemaphoreType.DMA((3, 8)),
            pltpu.SemaphoreType.DMA((4,)),
            pltpu.SemaphoreType.DMA((2,)),
        ],
        compiler_params=pltpu.CompilerParams(collective_id=0, has_side_effects=True),
    )(stored, target, names, diag)[:5]


def home_kernel(first, second, scale, first_home, second_home, scales, send, recv, own_sem):
    place = Place()
    foreign = place.foreign
    greet_all(place, 0)
    pairs = ((scale, scales), (first, first_home), (second, second_home))

    def copy(n, bits):
        to = flipped(place.shard, bits, 8)
        return pltpu.make_async_remote_copy(
            src_ref=pairs[n][0].at[to] if n else scale,
            dst_ref=pairs[n][1].at[place.group],
            send_sem=send.at[n, bits],
            recv_sem=recv.at[n, place.group],
            device_id=place.owner(to),
            device_id_type=MESH,
        )

    def arrival(n, bits):
        landed = pairs[n][1].at[flipped(place.group, bits, 8)]
        return pltpu.make_async_remote_copy(
            src_ref=landed, dst_ref=landed, send_sem=send.at[n, 0],
            recv_sem=recv.at[n, flipped(place.group, bits, 8)],
            device_id=place.link(0), device_id_type=MESH,
        )

    def local(n):
        return pltpu.make_async_copy(
            pairs[n][0].at[place.shard] if n else scale, pairs[n][1].at[place.group], own_sem.at[n]
        )

    for n in range(3):
        for bits in range(1, 8):
            copy(n, bits).start()

        @pl.when(foreign == 1)
        def _(n=n):
            copy(n, 0).start()

        @pl.when(foreign == 0)
        def _(n=n):
            local(n).start()

    for n in range(3):
        for bits in range(1, 8):
            copy(n, bits).wait_send()
            arrival(n, bits).wait_recv()

        @pl.when(foreign == 1)
        def _(n=n):
            copy(n, 0).wait_send()
            arrival(n, 0).wait_recv()

        @pl.when(foreign == 0)
        def _(n=n):
            local(n).wait()


def send_home(first, second, scale):
    return pl.pallas_call(
        home_kernel,
        out_shape=(
            jax.ShapeDtypeStruct(first.shape, first.dtype),
            jax.ShapeDtypeStruct(second.shape, second.dtype),
            jax.ShapeDtypeStruct((8,) + scale.shape, scale.dtype),
        ),
        in_specs=[ANY] * 3,
        out_specs=[ANY] * 3,
        scratch_shapes=[
            pltpu.SemaphoreType.DMA((3, 8)),
            pltpu.SemaphoreType.DMA((3, 8)),
            pltpu.SemaphoreType.DMA((3,)),
        ],
        compiler_params=pltpu.CompilerParams(collective_id=1, has_side_effects=True),
    )(first, second, scale)


def finish_kernel(target_ref, diag_ref, first_ref, second_ref, scale_ref, answer_ref, residual_ref):
    blocks, width, columns = target_ref.shape
    alpha1, alpha2, beta = scale_ref[0:1], scale_ref[1:2], scale_ref[2:3]
    diags = diag_ref[...].T
    for b in range(blocks):
        target = target_ref[b]
        diag = diags[:, b : b + 1]
        first = first_ref[:, b].reshape(columns, width).T.astype(jnp.float32)
        second = second_ref[:, b].reshape(columns, width).T.astype(jnp.float32)
        lost = target - target.astype(jnp.bfloat16).astype(jnp.float32)
        lost1 = lost - alpha1 * diag * lost
        answer_ref[b] = alpha1 * target + alpha2 * (first + lost1 + beta * target)
        residual_ref[b] = second + lost1 - alpha2 * diag * (lost1 + beta * lost)


def finish(target, diag, first, second, scales):
    blocks, width, columns = target.shape
    devices, _, own, _ = second.shape
    step = 8
    whole = pl.BlockSpec((step, width, columns), lambda g: (g, 0, 0))
    part = pl.BlockSpec((devices, step, own, width), lambda g: (0, g, 0, 0))
    return pl.pallas_call(
        finish_kernel,
        out_shape=(jax.ShapeDtypeStruct(target.shape, jnp.float32),) * 2,
        grid=(blocks // step,),
        in_specs=[
            whole,
            pl.BlockSpec((step, width), lambda g: (g, 0)),
            part,
            part,
            pl.BlockSpec(scales.shape, lambda g: (0, 0)),
        ],
        out_specs=(whole, whole),
    )(target, diag, first, second, scales)


def operate_kernel(slots, irow_ref, icol_ref, count_ref, blocks_ref, mine_ref, theirs_ref,
                   image_ref, away_ref, sum_ref):
    tile = pl.program_id(0)
    own = mine_ref.shape[1]

    @pl.when(tile == 0)
    def _():
        image_ref[...] = jnp.zeros_like(image_ref)
        sum_ref[...] = jnp.zeros_like(sum_ref)

    count = count_ref[tile]

    def group(step, carry):
        base = step * UNROLL
        terms = []
        for u in range(UNROLL):
            k = base + u
            i = irow_ref[tile * slots + k]
            j = icol_ref[tile * slots + k]
            block = blocks_ref[0, k]
            at_i = jnp.concatenate([mine_ref[i], theirs_ref[i]], axis=0)
            at_j = jnp.concatenate([mine_ref[j], theirs_ref[j]], axis=0)
            direct = lax.dot_general(
                at_j, block, (((1,), (1,)), ((), ())), preferred_element_type=jnp.float32
            )
            mirrored = lax.dot_general(
                at_i, block, (((1,), (0,)), ((), ())), preferred_element_type=jnp.float32
            )
            terms.append((k < count, i, j, direct, mirrored))
        for used, i, j, direct, mirrored in terms:
            direct = jnp.where(used, direct, 0.0)
            mirrored = jnp.where(used, mirrored, 0.0)
            image_ref[i] += direct[:own]
            sum_ref[i] += direct[own:]
            image_ref[j] += mirrored[:own]
            sum_ref[j] += mirrored[own:]
        return carry

    lax.fori_loop(0, (count + UNROLL - 1) // UNROLL, group, 0)

    @pl.when(tile == pl.num_programs(0) - 1)
    def _():
        away_ref[...] = sum_ref[...].astype(away_ref.dtype)


def operate(blocks, irow, icol, count, mine, theirs):
    tiles, slots, width, _ = blocks.shape
    whole = pl.BlockSpec(mine.shape, lambda t, *_: (0, 0, 0))
    return pl.pallas_call(
        functools.partial(operate_kernel, slots),
        out_shape=(
            jax.ShapeDtypeStruct(mine.shape, jnp.float32),
            jax.ShapeDtypeStruct(mine.shape, jnp.bfloat16),
        ),
        grid_spec=pltpu.PrefetchScalarGridSpec(
            num_scalar_prefetch=3,
            grid=(tiles,),
            in_specs=[
                pl.BlockSpec((1, slots, width, width), lambda t, *_: (t, 0, 0, 0)),
                whole,
                whole,
            ],
            out_specs=(whole, whole),
            scratch_shapes=[pltpu.VMEM(mine.shape, jnp.float32)],
        ),
        compiler_params=pltpu.CompilerParams(vmem_limit_bytes=40 * 2**20),
        cost_estimate=pl.CostEstimate(
            flops=tiles * slots * width**3 * 4, bytes_accessed=60 * 2**20, transcendentals=0
        ),
    )(irow, icol, count, blocks, mine, theirs)


def by_columns(blocks, block_rows, block_cols, counts, diagonal, target):
    nrow, ncol = lax.axis_size("row"), lax.axis_size("col")
    devices = nrow * ncol
    stored = blocks[0, 0]
    slots, width, _ = stored.shape
    quarter = target.shape[0] // width
    own = target.shape[1] // devices
    row_blocks = ncol * quarter
    half = slots // 2
    row, col, core = lax.axis_index("row"), lax.axis_index("col"), lax.axis_index("rhs")

    irow = row * row_blocks + block_rows[0, 0]
    jcol = block_cols[0, 0]
    icol = (jcol // quarter * ncol + col) * quarter + jcol % quarter

    def every_other(index):
        return jnp.where(core == 0, index[0::2], index[1::2])

    used = (counts[0] - core + 1) // 2
    names = jnp.concatenate([every_other(irow), every_other(icol), used])
    names = jnp.pad(names, (0, -names.shape[0] % 1024)).reshape(-1, 128)
    diag_own = diagonal.reshape(quarter, width)
    target_blocks = target.reshape(quarter, width, target.shape[1])

    tiles, field, field_pair, all_names, all_diag = spread(
        stored.reshape(half, 2, width, width), target_blocks, names, diag_own
    )
    all_names = all_names.reshape(devices, -1)
    irows = all_names[:, :half].reshape(-1)
    icols = all_names[:, half : 2 * half].reshape(-1)
    used = all_names[:, 2 * half]
    diag = all_diag.reshape(-1, 1, width)
    swap = [(0, 1), (1, 0)]

    def image_of(direction, low, theirs):
        here, away = operate(tiles, irows, icols, used, low, theirs)
        away = lax.ppermute(away, "rhs", swap)
        return diag * direction + here + away.astype(jnp.float32)

    def inner(a, b):
        return jnp.sum(a * b, axis=(0, 2), keepdims=True)

    def parcels(value):
        return value.astype(jnp.bfloat16).reshape(devices, quarter, own, width)

    low = field.reshape(-1, own, width)
    start = low.astype(jnp.float32)
    norm0 = inner(start, start)
    image = image_of(start, low, field_pair.reshape(low.shape))
    alpha1 = norm0 / inner(start, image)
    first = start - alpha1 * image
    norm1 = inner(first, first)
    beta = norm1 / norm0
    direction = first + beta * start
    first_parcel = parcels(first)
    low = direction.astype(jnp.bfloat16)
    image = image_of(direction, low, lax.ppermute(low, "rhs", swap))
    alpha2 = norm1 / inner(direction, image)
    second = first - alpha2 * image
    scale = jnp.stack([alpha1, alpha2, beta]).reshape(3, own)
    scale = jnp.pad(scale, ((0, 5), (0, 128 - own)))
    first_home, second_home, scales = send_home(first_parcel, parcels(second), scale)
    scales = scales[:, :3, :own]
    scales = scales.transpose(1, 0, 2).reshape(3, devices * own)
    answer, residual = finish(target_blocks, diag_own, first_home, second_home, scales)
    return (answer.reshape(target.shape), residual.reshape(target.shape))


def one_hot_slots(indices, valid, extent):
    return ((indices[None, :] == jnp.arange(extent)[:, None]) & valid[None, :]).astype(jnp.float32)


def picked(blocks, index):
    return lax.map(lambda i: lax.dynamic_index_in_dim(blocks, i, 0, keepdims=False), index)


def on_device(blocks, block_rows, block_cols, counts, diagonal, target):
    highest = lax.Precision.HIGHEST
    nrow = lax.axis_size("row")
    ncol = lax.axis_size("col")
    if (
        (lax.axis_size("parts"), nrow, ncol, lax.axis_size("rhs")) == (2, 4, 2, 2)
        and target.shape[1] == 128
        and blocks.shape[2] % (16 * PIECES) == 0
        and target.shape[0] // blocks.shape[3] % 64 == 0
    ):
        return by_columns(blocks, block_rows, block_cols, counts, diagonal, target)
    stored = blocks[0, 0]
    slots = stored.shape[0]
    width = stored.shape[1]
    local = target.shape[0]
    ncols = target.shape[1]
    quarter = local // width
    row_blocks = ncol * quarter
    col_blocks = nrow * quarter
    valid = jnp.arange(slots) < counts[0, 0]
    rows_hot = one_hot_slots(block_rows[0, 0], valid, row_blocks)
    cols_hot = one_hot_slots(block_cols[0, 0], valid, col_blocks)

    def squares(vector):
        return lax.psum(jnp.sum(vector * vector, axis=0), ("row", "col"))

    solution = jnp.zeros_like(target)
    residual = target
    direction = target
    norm_now = squares(residual)
    for step in range(ITERS):
        operate_field_low = direction.astype(jnp.bfloat16)
        direct_gathered = lax.all_gather(operate_field_low, "row", axis=0, tiled=True).reshape(
            col_blocks, width, ncols
        )
        prod = jnp.einsum(
            "kab,kbc->kac",
            stored,
            picked(direct_gathered, block_cols[0, 0]),
            preferred_element_type=jnp.float32,
        )
        direct_partial_value = jnp.einsum("ik,kac->iac", rows_hot, prod, precision=highest)
        direct = lax.psum_scatter(
            direct_partial_value.reshape(row_blocks * width, ncols).astype(jnp.bfloat16),
            "col",
            scatter_dimension=0,
            tiled=True,
        ).astype(jnp.float32)
        gathered = lax.all_gather(operate_field_low, "col", axis=0, tiled=True).reshape(
            row_blocks, width, ncols
        )
        tprod = jnp.einsum(
            "kba,kbc->kac",
            stored,
            picked(gathered, block_rows[0, 0]),
            preferred_element_type=jnp.float32,
        )
        partial_value = jnp.einsum("jk,kac->jac", cols_hot, tprod, precision=highest)
        parcel = partial_value.astype(jnp.bfloat16).reshape(nrow, local, ncols)
        mirrored = jnp.sum(
            lax.all_to_all(parcel, "row", split_axis=0, concat_axis=0, tiled=True).astype(
                jnp.float32
            ),
            axis=0,
        )
        image = diagonal[:, None] * direction + direct + mirrored
        curve = lax.psum(jnp.sum(direction * image, axis=0), ("row", "col"))
        alpha = norm_now / curve
        solution = solution + alpha * direction
        residual = residual - alpha * image
        if step + 1 < ITERS:
            norm_next = squares(residual)
            direction = residual + norm_next / norm_now * direction
            norm_now = norm_next
    return (solution, residual)


def solution(mesh):
    return jax.shard_map(
        on_device,
        mesh=mesh,
        in_specs=(
            P(("parts", "row"), "col", None, None, None),
            P(("parts", "row"), "col", None),
            P(("parts", "row"), "col", None),
            P(("parts", "row"), "col"),
            P(("parts", "row", "col")),
            P(("parts", "row", "col"), "rhs"),
        ),
        out_specs=(P(("parts", "row", "col"), "rhs"), P(("parts", "row", "col"), "rhs")),
        check_vma=False,
    )
```

```python
import functools
import jax
import jax.numpy as jnp
from jax import lax
from jax.experimental import pallas as pl
from jax.experimental.pallas import tpu as pltpu
from jax.sharding import PartitionSpec as P

ITERS = 2
LANES = 128
PIECES = 6
MESH = pl.DeviceIdType.MESH
ANY = pl.BlockSpec(memory_space=pl.ANY)


HOLD = 17
ROUTES = (
    (
        (0,0,0,1,1,2), (2,0,1,1,0,0,-1,0,1), (2,0,3,0,0,0,-1,0,2), (2,0,3,1,0,0,-1,1,1), (0,0,0,0,0,2),
        (0,0,0,4,2,1,0), (2,0,2,1,0,0,-1,0,0), (0,0,0,2,0,1), (0,0,0,5,1), (2,0,1,0,0,0,-1,-1,1),
        (2,0,0,1,0,0,-1,-1,0), (0,0,0,3,1,2), (2,0,2,0,0,0,-1,-1,2), (0,1,0,0), (1,1,1,3,2), (0,1,0,3,1,0),
        (1,1,1,0,2), (0,0,1,0,1), (1,1,1,1,2), (0,0,1,4), (0,1,0,2,0), (2,0,2,1,1,0,0,-1,2), (2,1,1,1,0,1,3,4,2),
        (0,1,0,5,1,0), (0,0,1,2,2,1), (1,1,1,2,2), (2,2,0,0,0,0,-1,-1,-1), (2,0,0,1,1,0,-1,-1,-1), (1,1,1,4,2),
        (0,1,1,0), (0,1,1,3), (2,3,1,0,0,0,5,-1,1), (0,0,1,1,2), (0,1,1,2,2,1), (2,3,0,1,0,0,4,-1,0), (0,2,0,5,2),
        (0,1,1,5), (0,1,1,1,1,0), (0,2,0,3,0), (2,3,0,0,0,0,-1,-1,-1), (2,3,0,1,1,0,-1,-1,-1), (0,1,0,4,0),
        (2,2,0,1,1,0,-1,-1,-1), (0,1,0,1), (0,0,1,5), (2,1,1,0,0,0,2,-1,1), (0,2,1,3), (0,2,1,0,0), (0,2,0,1,0,1),
        (0,1,1,4), (0,2,0,2), (0,0,1,3), (0,2,0,0), (2,1,0,1,0,0,1,-1,0), (0,3,0,3,0,2), (0,2,1,1,1), (0,2,1,4,0),
        (0,3,0,0,0), (2,1,0,1,1,0,-1,-1,-1), (2,1,0,0,0,0,-1,-1,-1), (0,3,0,1,0), (0,3,1,3,1,2), (0,3,0,5,1),
        (0,2,1,2,2), (0,2,0,4), (0,3,1,5), (0,3,1,0,1,2), (0,3,0,2,0), (0,2,1,5), (0,3,1,1), (0,3,0,4), (0,3,1,4),
        (0,3,1,2),
    ),
    (
        (1,1,0,3,1), (2,1,3,1,0,1,-1,8,2), (2,1,1,0,0,1,-1,3,2), (1,1,0,0,1), (1,1,0,5,2), (1,1,0,1,1),
        (2,1,3,0,0,1,-1,7,2), (2,1,2,0,0,1,-1,5,2), (2,1,0,1,0,1,-1,2,2), (2,1,1,1,0,1,-1,3,1), (2,1,2,1,0,1,-1,2,0),
        (2,1,0,0,0,1,-1,1,2), (1,1,0,2,1), (1,1,0,4,1), (0,0,0,1,0,2), (2,0,1,1,0,0,0,-1,0), (2,1,2,1,1,1,2,6,2),
        (0,1,0,0,0), (2,0,3,1,0,0,1,0,2), (0,0,1,1,1,2), (2,2,1,0,0,0,-1,-1,-1), (0,0,0,4,0), (2,0,1,1,1,0,-1,-1,-1),
        (0,2,0,5,1,0), (0,0,0,2,2), (0,1,1,0), (2,2,1,1,0,0,3,-1,0), (0,0,0,5,2,0), (0,0,1,4), (0,2,0,0,0),
        (2,0,1,0,0,0,-1,-1,-1), (0,2,1,5), (0,2,0,3,1), (0,0,0,3,0), (2,2,1,1,1,0,-1,-1,-1), (0,1,0,4,1,0),
        (0,1,0,3,0), (0,0,1,5,1), (0,2,0,4), (0,0,1,0,0), (0,2,1,0,1), (0,2,0,2,0,1), (0,1,0,5,2,0), (0,0,1,3,2,1),
        (0,3,0,3,1), (0,0,1,2), (0,1,1,4,2), (0,2,1,3), (2,3,1,0,0,0,-1,-1,-1), (0,1,1,3,2), (0,3,0,0,1),
        (0,1,1,2,0), (0,0,0,0), (0,3,0,1,1,0), (0,1,1,1,0), (0,2,1,2,1,2), (2,3,1,1,1,0,-1,-1,-1), (0,1,1,5),
        (2,1,1,0,0,0,-1,-1,-1), (2,1,1,1,1,0,-1,-1,-1), (0,2,0,1), (0,1,0,2), (0,3,0,2,1,0), (0,3,1,1), (0,2,1,1,2),
        (0,2,1,4), (0,1,0,1,2), (0,3,1,3), (0,3,1,4,1,0), (0,3,1,2), (0,3,0,5), (0,3,1,5), (0,3,1,0), (0,3,0,4),
    ),
    (
        (0,1,0,0,1,0,2), (2,2,1,0,0,0,-1,10,1), (0,1,0,3,2), (2,2,2,1,0,0,-1,-1,0), (2,2,1,1,0,0,-1,11,1),
        (0,1,0,2,2), (2,2,3,0,0,0,-1,-1,1), (0,1,0,5,2,0), (2,2,3,1,0,0,-1,12,1), (0,1,0,1,0), (2,2,0,1,0,0,-1,8,0),
        (0,1,0,4,1,0), (2,2,0,0,0,0,-1,-1,2), (1,0,1,5,3), (0,1,1,0,2), (0,0,0,1), (2,0,3,0,0,0,0,-1,1), (1,0,1,0,3),
        (2,2,2,1,1,0,-1,-1,-1), (2,3,1,0,0,0,11,5,2), (1,0,1,1,3), (0,0,0,0,1,0), (2,3,0,1,0,0,10,4,2), (0,1,1,5),
        (0,0,0,4,0,1), (1,0,1,3,3), (2,3,2,0,0,0,-1,-1,-1), (0,1,1,1,2,1), (1,0,1,4,3), (2,3,0,0,0,0,9,-1,2),
        (2,2,0,1,1,0,8,-1,2), (0,0,0,3,0), (2,3,3,0,0,0,13,-1,1), (2,0,2,0,0,0,-1,-1,-1), (0,1,1,4), (1,0,1,2,3),
        (1,1,1,3,3), (2,3,1,1,1,0,12,14,1), (0,0,1,0), (0,2,0,0,0), (1,1,1,0,3), (2,1,1,0,0,0,3,2,2), (1,1,1,5,3),
        (0,0,1,4,1), (1,1,1,1,3), (2,3,2,1,1,0,-1,-1,-1), (0,2,0,1,2,0), (0,0,1,3), (2,0,2,1,1,0,-1,-1,-1),
        (2,3,3,1,1,0,14,-1,1), (2,1,3,0,0,1,6,-1,3), (0,2,1,0,1), (2,1,1,1,0,1,4,5,0), (2,1,2,0,0,0,-1,-1,-1),
        (0,2,0,4,0), (0,2,1,1), (0,0,1,2,0), (2,1,3,1,1,0,7,-1,1), (0,2,0,2), (2,1,1,1,1,1,5,4,3), (1,1,1,2,3),
        (2,1,0,1,0,0,2,1,2), (0,2,1,3,0), (0,2,1,4,2,1), (1,1,1,4,3), (2,1,0,0,0,0,1,-1,2), (0,3,0,0), (0,0,0,2),
        (0,0,1,1), (2,1,2,1,1,0,-1,-1,-1), (0,3,0,5,0,2), (0,2,0,3), (0,1,1,2,1), (0,0,0,5,0), (0,3,1,5,1,2),
        (0,2,0,5,0), (0,3,1,1,0), (0,0,1,5,1), (0,3,0,2,0), (0,3,0,3), (0,2,1,5,2), (0,3,0,4,2), (0,3,1,3),
        (0,3,0,1), (0,1,1,3), (0,2,1,2), (0,3,1,2), (0,3,1,4), (0,3,1,0),
    ),
    (
        (1,0,0,5,1), (1,0,0,0,1), (1,0,0,1,1), (2,3,1,0,0,1,-1,11,3), (1,0,0,3,1), (2,3,1,1,0,1,-1,13,0),
        (2,3,0,1,0,1,-1,10,3), (1,0,0,4,1), (2,3,2,0,0,1,-1,-1,3), (2,3,2,1,0,1,-1,15,0), (2,3,3,1,0,1,-1,16,0),
        (2,3,0,0,0,1,-1,9,3), (2,3,3,0,0,1,-1,13,3), (1,0,0,2,1), (0,1,0,0,2,0), (2,2,1,0,0,0,10,-1,2),
        (2,1,3,1,0,1,8,9,0), (2,3,1,1,1,1,13,12,3), (0,2,0,5,2,0), (2,1,1,0,0,1,3,3,3), (2,2,1,1,0,0,11,3,2),
        (2,3,2,1,1,1,15,-1,3), (0,2,0,0,2,1), (1,1,1,5,1), (2,3,3,1,1,1,16,14,3), (2,2,3,0,0,0,-1,-1,-1),
        (0,2,0,1,1), (2,1,3,0,0,1,7,6,1), (2,2,3,1,0,0,12,-1,0), (0,1,1,0), (0,2,0,3,2,0), (2,1,2,0,0,1,5,-1,3),
        (0,1,0,4,2), (2,1,3,1,1,1,9,7,3), (0,2,0,4,1,2), (2,1,0,1,0,1,2,2,3), (2,0,3,0,0,0,-1,-1,-1), (0,2,1,5),
        (0,2,0,2,2,1), (2,1,0,0,0,1,1,1,3), (0,0,0,0,0), (2,2,3,1,1,0,-1,-1,-1), (0,3,0,3,2,0), (0,0,0,1), (0,0,0,4),
        (0,2,1,3,1,2), (0,3,0,0,2,1,0), (2,1,2,1,1,1,6,-1,3), (0,1,1,1), (0,0,1,0), (0,3,0,5,1),
        (2,0,3,1,0,0,0,-1,0), (2,3,3,0,0,0,-1,-1,-1), (0,3,1,3), (0,3,0,1,2,0), (0,0,1,1), (2,3,1,1,1,0,14,-1,2),
        (0,3,1,0), (2,1,3,0,0,0,-1,-1,-1), (0,0,0,2,0), (0,0,1,4), (2,0,3,1,1,0,-1,-1,-1), (2,1,1,1,1,0,4,-1,2),
        (0,0,0,5,1), (2,3,3,1,1,0,-1,-1,-1), (0,3,1,1,1), (0,3,0,2,2,1,0), (0,2,1,0), (0,1,0,5,0), (0,0,1,2),
        (0,3,0,4,0,1), (0,0,1,3,0), (2,1,3,1,1,0,-1,-1,-1), (0,3,1,2), (0,1,1,4), (0,2,1,4,2), (0,1,1,5),
        (0,1,1,3,1,0), (0,3,1,4,2,1), (0,1,1,2,0), (0,2,1,2), (0,0,0,3), (0,3,1,5,2), (0,0,1,5), (0,1,0,3),
        (0,2,1,1), (0,1,0,2), (0,1,0,1),
    ),
)


def flipped(index, bits, devices):
    total, unit = index, 1
    while unit < devices:
        if bits & unit:
            total = total + unit * (1 - 2 * lax.rem(index // unit, 2))
        unit *= 2
    return total


class Place:
    def __init__(self):
        self.part, self.row = lax.axis_index("parts"), lax.axis_index("row")
        self.col, self.core = lax.axis_index("col"), lax.axis_index("rhs")
        self.half = self.row // 2
        self.low = lax.rem(self.row, 2)
        self.shard = self.row * 2 + self.col
        self.group = self.low * 4 + self.part * 2 + self.col
        self.foreign = lax.rem(self.half + self.part, 2)
        self.inner = lax.rem(self.half + self.low, 2)

    def link(self, way):
        if way == 0:
            return {"col": 1 - self.col}
        if way == 1:
            return {"parts": 1 - self.part}
        if way == 2:
            return {"row": self.half * 2 + 1 - self.low}
        return {"row": 3 - self.row}

    def tile_row(self, kind):
        return (3 * self.half, 1 + self.half, 2 - self.half, 3 - 3 * self.half)[kind]

    def solver(self, group):
        return {
            "row": 2 * self.part + group // 4,
            "parts": lax.rem(group // 2, 2),
            "col": lax.rem(group, 2),
        }

    def owner(self, shard):
        return {"row": shard // 2, "parts": self.half, "col": lax.rem(shard, 2)}


def greet_all(place, sibling):
    barrier = pltpu.get_barrier_semaphore()
    me = place.part * 8 + place.shard
    for offset in range(1, 16):
        other = lax.rem(me + offset, 16)
        peer = {"parts": other // 8, "row": lax.rem(other, 8) // 2, "col": lax.rem(other, 2)}
        pl.semaphore_signal(barrier, inc=1, device_id=peer, device_id_type=MESH)
    if sibling:
        pl.semaphore_signal(barrier, inc=1, device_id={"rhs": 1 - place.core}, device_id_type=MESH)
    pl.semaphore_wait(barrier, 15 + sibling)


def solve_kernel(
    stored, target, names, diag,
    first_home, second_home, scales, transit, hold,
    tiles, parcel, field, start, terms, image, first, away_out, away_in, hot, names_v, names_s, diag_v, scale, norm,
    piece_send, piece_recv, pass_recv, hold_recv, send, recv, own_sem, pair_sem, home_send, home_recv, home_own,
):
    place = Place()
    shard, core, foreign = place.shard, place.core, place.foreign
    half = tiles.shape[1]
    size = half // PIECES
    blocks, both, width = field.shape
    own = both // 2
    quarter = blocks // 8
    step_blocks = 16
    steps = blocks // step_blocks
    rows = hot.shape[1]
    greet_all(place, 1)

    def part_of(k):
        return pl.ds(k * size, size)

    def mine(s):
        return field.at[pl.ds(s * quarter, quarter), pl.ds(0, own)]

    def piece_copy(source, target, way, send_sem, recv_sem):
        return pltpu.make_async_remote_copy(
            src_ref=source, dst_ref=target, send_sem=send_sem, recv_sem=recv_sem,
            device_id=place.link(way), device_id_type=MESH,
        )

    def source_shard(entry):
        solved = place.half if entry[5] == 0 else 1 - place.half
        row = (3 * solved, 3 - 3 * solved, 1 + solved, 2 - solved)[entry[1]]
        return row * 2 + (1 - place.col if entry[4] else place.col)

    def dest_group(entry):
        low = lax.rem(entry[2] // 2 + place.part, 2)
        part = 1 - place.part if entry[2] % 2 else place.part
        return low * 4 + part * 2 + (1 - place.col if entry[3] else place.col)

    def step(kind, entry, count):
        if entry[0] == 2:
            slot_in, slot_out, way = entry[6:]
            if entry[4] == 0 and slot_in < 0 and way >= 0:
                source = parcel.at[dest_group(entry)]
            elif way < 0:
                s = source_shard(entry)
                piece_copy(mine(s), mine(s), 0, piece_send.at[0], recv.at[2, s]).wait_recv()
                return count
            else:
                source = hold.at[slot_in]
                piece_copy(source, source, 0, piece_send.at[0], hold_recv.at[slot_in]).wait_recv()
            if slot_out < 0:
                s = source_shard(entry)
                target, sem = mine(s), recv.at[2, s]
            else:
                target, sem = hold.at[slot_out], hold_recv.at[slot_out]
            piece_copy(source, target, way, piece_send.at[count], sem).start()
            return count + 1
        k = entry[3]
        if entry[0] == 0:
            s = place.tile_row(entry[1]) * 2 + (1 - place.col if entry[2] else place.col)
            here = kind in (0, 2) and entry[1] == kind // 2 and entry[2] == 0
            source, sem = tiles.at[s, part_of(k)], piece_recv.at[s, k]
        else:
            s = place.tile_row(1 - entry[1]) * 2 + place.col
            here = entry[2] == 0
            source, sem = transit.at[entry[1], part_of(k)], pass_recv.at[entry[1], k]
        if here:
            source = stored.at[part_of(k), core]
        else:
            piece_copy(source, source, 0, piece_send.at[0], sem).wait_recv()
        for way in entry[4:]:
            if entry[0] == 0 or way == 3:
                target, sem = tiles.at[s, part_of(k)], piece_recv.at[s, k]
            else:
                target, sem = transit.at[entry[1], part_of(k)], pass_recv.at[entry[1], k]
            piece_copy(source, target, way, piece_send.at[count], sem).start()
            count += 1
        return count

    def sends(entry):
        return int(entry[8] >= 0) if entry[0] == 2 else len(entry) - 4

    def each_class(body):
        for kind in range(4):
            @pl.when((foreign == kind % 2) & (place.inner == kind // 2))
            def _(kind=kind):
                entries = ROUTES[kind]
                begin = [entry[0] for entry in entries].index(2)
                body(kind, entries, begin)

    def before_pack(kind, entries, begin):
        count = 0
        for entry in entries[:begin]:
            count = step(kind, entry, count)

    def sent(kind, entries, begin):
        count = 0
        for entry in entries:
            for _ in range(sends(entry)):
                block = parcel.at[0] if entry[0] == 2 else stored.at[part_of(0), core]
                piece_copy(block, block, 0, piece_send.at[count], piece_recv.at[shard, 0]).wait_send()
                count += 1

    fetch = pltpu.make_async_copy(target, first, own_sem.at[4])
    fetch.start()
    each_class(before_pack)
    fetch.wait()

    def pack(b, carry):
        low = first[pl.ds(b * width, width)].astype(jnp.bfloat16).T
        parcel[:, b] = low.reshape(8, own, width)
        return carry

    lax.fori_loop(0, quarter, pack, 0)
    pairs = ((names, names_v), (diag, diag_v))

    def straight(n, bits):
        group = flipped(place.group, bits, 8)
        return pltpu.make_async_remote_copy(
            src_ref=pairs[n][0],
            dst_ref=pairs[n][1].at[shard],
            send_sem=send.at[n, bits],
            recv_sem=recv.at[n, shard],
            device_id=place.solver(group),
            device_id_type=MESH,
        )

    def arrival(n, bits):
        landed = pairs[n][1].at[flipped(shard, bits, 8)]
        return pltpu.make_async_remote_copy(
            src_ref=landed, dst_ref=landed, send_sem=send.at[n, 0],
            recv_sem=recv.at[n, flipped(shard, bits, 8)],
            device_id=place.link(0), device_id_type=MESH,
        )

    def local(n):
        source, landed = (
            (names, names_v.at[shard]),
            (diag, diag_v.at[shard]),
            (parcel.at[place.group], mine(shard)),
            (stored.at[:, core], tiles.at[shard]),
        )[n]
        return pltpu.make_async_copy(source, landed, own_sem.at[n])

    for n in range(2):
        for bits in range(1, 8):
            straight(n, bits).start()

    @pl.when(foreign == 1)
    def _():
        for n in range(2):
            straight(n, 0).start()

    @pl.when(foreign == 0)
    def _():
        for n in range(4):
            local(n).start()

    def blank(b, carry):
        terms[pl.ds(b * rows, rows)] = jnp.zeros((rows, width), jnp.float32)
        return carry

    lax.fori_loop(0, both, blank, 0)

    for n in range(2):
        for bits in range(1, 8):
            arrival(n, bits).wait_recv()
            straight(n, bits).wait_send()

    @pl.when(foreign == 1)
    def _():
        for n in range(2):
            arrival(n, 0).wait_recv()
            straight(n, 0).wait_send()

    @pl.when(foreign == 0)
    def _():
        for n in range(4):
            local(n).wait()

    read = pltpu.make_async_copy(names_v, names_s, own_sem.at[4])
    read.start()

    for s in range(8):
        names_row = names_v[s, 0:1, :]
        at = lax.broadcasted_iota(jnp.int32, (blocks, LANES), 0)
        hot[:, s * LANES : (s + 1) * LANES] = jnp.where(at == names_row, 1.0, 0.0).astype(jnp.bfloat16)

    read.wait()
    def swap(n, source, landed):
        return pltpu.make_async_remote_copy(
            src_ref=source, dst_ref=landed, send_sem=pair_sem.at[n, 0], recv_sem=pair_sem.at[n, 1],
            device_id={"rhs": 1 - core}, device_id_type=MESH,
        )

    ours, theirs = field.at[:, pl.ds(0, own)], field.at[:, pl.ds(own, own)]
    pair = swap(0, ours, theirs)
    zero = jnp.zeros((own, width), jnp.float32)

    def chunk(ref, n):
        return ref[pl.ds(n * step_blocks, step_blocks)]

    def keep(n, total):
        low = field[pl.ds(n * step_blocks, step_blocks), 0:own]
        start[pl.ds(n * step_blocks, step_blocks)] = low
        value = low.astype(jnp.float32)
        return total + jnp.sum(value * value, axis=0)

    def keep_start():
        norm[...] = lax.fori_loop(0, steps, keep, zero)

    def product(s, k):
        results = []
        for u in range(size):
            slot = k * size + u
            i, j = names_s[s, 0, slot], names_s[s, 0, LANES // 2 + slot]
            block = tiles[s, slot]
            direct = lax.dot_general(
                field[j], block, (((1,), (1,)), ((), ())), preferred_element_type=jnp.float32
            )
            mirrored = lax.dot_general(
                field[i], block, (((1,), (0,)), ((), ())), preferred_element_type=jnp.float32
            )
            results.append((slot, slot < names_s[s, 1, 0], direct, mirrored))
        for slot, used, direct, mirrored in results:
            at = s * LANES + slot
            terms[pl.ds(at, both, stride=rows)] = jnp.where(used, direct, 0.0)
            terms[pl.ds(at + LANES // 2, both, stride=rows)] = jnp.where(used, mirrored, 0.0)

    def products(n, carry):
        product(n // PIECES, lax.rem(n, PIECES))
        return carry

    def product_pair(row, k):
        def one(col, carry):
            product(place.tile_row(row) * 2 + col, k)
            return carry

        lax.fori_loop(0, 2, one, 0)

    def after_pack(kind, entries, begin):
        count = sum(sends(entry) for entry in entries[:begin])
        ready = max(n for n, entry in enumerate(entries) if entry[0] == 2 and entry[8] < 0)
        landed, due = set(), []
        for n, entry in enumerate(entries):
            if n >= begin:
                count = step(kind, entry, count)
            if entry[0] == 0:
                landed.add(entry[1:4])
                if (entry[1], 1 - entry[2], entry[3]) in landed:
                    due.append((entry[1], entry[3]))
            if n == ready:
                pair.start()
            if n == min(ready + 1, len(entries) - 1):
                keep_start()
            if n == min(ready + 2, len(entries) - 1):
                pair.wait()
            if n >= ready + 2:
                for _ in range(-(-len(due) // (len(entries) - n))):
                    product_pair(*due.pop(0))
        for one in due:
            product_pair(*one)

    each_class(after_pack)
    each_class(sent)

    def gather_sums(n, carry):
        c = 2 * n
        pair = [terms[pl.ds((c + m) * rows, rows)].astype(jnp.bfloat16) for m in range(2)]
        total = jnp.dot(
            hot[...], jnp.concatenate(pair, axis=1), preferred_element_type=jnp.float32
        )
        for m in range(2):
            image[pl.ds(c + m, blocks, stride=both)] = total[:, m * width : (m + 1) * width]
        return carry

    def image_chunk(n):
        return image[pl.ds(n * step_blocks * both, step_blocks * both)].reshape(step_blocks, both, width)

    def first_chunk(n):
        return first[pl.ds(n * step_blocks * own, step_blocks * own)].reshape(step_blocks, own, width)

    def start_chunk(n):
        return chunk(start, n).astype(jnp.float32)

    def diag_chunk(n):
        per = quarter // step_blocks
        return diag_v[n // per, pl.ds(lax.rem(n, per) * step_blocks, step_blocks)][:, None, :]

    def operate(exchange, direction_chunk):
        lax.fori_loop(own // 2, own, gather_sums, 0)

        def away(n, carry):
            away_out[pl.ds(n * step_blocks, step_blocks)] = image_chunk(n)[:, own:].astype(jnp.bfloat16)
            return carry

        lax.fori_loop(0, steps, away, 0)
        over = swap(exchange, away_out, away_in)
        over.start()
        lax.fori_loop(0, own // 2, gather_sums, 0)
        over.wait()

        def join(n, total):
            direction = direction_chunk(n)
            value = image_chunk(n)[:, :own] + chunk(away_in, n).astype(jnp.float32)
            value = value + diag_chunk(n) * direction
            image[pl.ds(n * step_blocks * own, step_blocks * own)] = value.reshape(step_blocks * own, width)
            return total + jnp.sum(value * direction, axis=0)

        return jnp.sum(lax.fori_loop(0, steps, join, zero), axis=1, keepdims=True)

    def joined_chunk(n):
        return image[pl.ds(n * step_blocks * own, step_blocks * own)].reshape(step_blocks, own, width)

    home = ((scale, scales), (parcel, first_home), (away_out, second_home))

    def leaving(n, to):
        if n == 0:
            return scale
        return parcel.at[to] if n == 1 else away_out.at[pl.ds(to * quarter, quarter)]

    def home_copy(n, bits):
        to = flipped(shard, bits, 8)
        return pltpu.make_async_remote_copy(
            src_ref=leaving(n, to),
            dst_ref=home[n][1].at[place.group],
            send_sem=home_send.at[n, bits],
            recv_sem=home_recv.at[n, place.group],
            device_id=place.owner(to),
            device_id_type=MESH,
        )

    def home_arrival(n, bits):
        landed = home[n][1].at[flipped(place.group, bits, 8)]
        return pltpu.make_async_remote_copy(
            src_ref=landed, dst_ref=landed, send_sem=home_send.at[n, 0],
            recv_sem=home_recv.at[n, flipped(place.group, bits, 8)],
            device_id=place.link(0), device_id_type=MESH,
        )

    def home_local(n):
        return pltpu.make_async_copy(leaving(n, shard), home[n][1].at[place.group], home_own.at[n])

    def go_home(n):
        for bits in range(7, 0, -1):
            home_copy(n, bits).start()

        @pl.when(foreign == 1)
        def _():
            home_copy(n, 0).start()

        @pl.when(foreign == 0)
        def _():
            home_local(n).start()

    def arrive_home(n):
        for bits in range(1, 8):
            home_copy(n, bits).wait_send()
            home_arrival(n, bits).wait_recv()

        @pl.when(foreign == 1)
        def _():
            home_copy(n, 0).wait_send()
            home_arrival(n, 0).wait_recv()

        @pl.when(foreign == 0)
        def _():
            home_local(n).wait()

    per = quarter // step_blocks
    norm0 = jnp.sum(norm[...], axis=1, keepdims=True)
    alpha1 = norm0 / operate(1, start_chunk)

    def next_first(n, total):
        value = start_chunk(n) - alpha1[None] * joined_chunk(n)
        first[pl.ds(n * step_blocks * own, step_blocks * own)] = value.reshape(step_blocks * own, width)
        parcel[n // per, pl.ds(lax.rem(n, per) * step_blocks, step_blocks)] = value.astype(jnp.bfloat16)
        return total + jnp.sum(value * value, axis=0)

    norm1 = jnp.sum(lax.fori_loop(0, steps, next_first, zero), axis=1, keepdims=True)
    go_home(1)
    beta = norm1 / norm0

    def direction_chunk(n):
        return first_chunk(n) + beta[None] * start_chunk(n)

    def next_low(n, carry):
        field[pl.ds(n * step_blocks, step_blocks), 0:own] = direction_chunk(n).astype(jnp.bfloat16)
        return carry

    lax.fori_loop(0, steps, next_low, 0)
    pair = swap(2, ours, theirs)
    pair.start()
    pair.wait()
    lax.fori_loop(0, 8 * PIECES, products, 0)
    alpha2 = norm1 / operate(3, direction_chunk)

    def last(n, carry):
        value = first_chunk(n) - alpha2[None] * joined_chunk(n)
        away_out[pl.ds(n * step_blocks, step_blocks)] = value.astype(jnp.bfloat16)
        return carry

    lax.fori_loop(0, steps, last, 0)
    go_home(2)
    for n, value in enumerate((alpha1, alpha2, beta)):
        scale[n] = jnp.broadcast_to(value, (own, width))
    go_home(0)
    for n in (1, 2, 0):
        arrive_home(n)


def solve(stored, target, names, diag):
    half, cores, width, _ = stored.shape
    quarter, columns = target.shape[0] // width, target.shape[1]
    own = columns // 8
    parcel = (8, quarter, own, width)
    blocks, both, rows = 8 * quarter, 2 * own, 8 * LANES
    sends = max(
        sum(int(e[8] >= 0) if e[0] == 2 else len(e) - 4 for e in entries) for entries in ROUTES
    )
    dma = pltpu.SemaphoreType.DMA
    return pl.pallas_call(
        solve_kernel,
        out_shape=(
            jax.ShapeDtypeStruct(parcel, jnp.bfloat16),
            jax.ShapeDtypeStruct(parcel, jnp.bfloat16),
            jax.ShapeDtypeStruct((8, 3, own, width), jnp.float32),
            jax.ShapeDtypeStruct((2, half, width, width), stored.dtype),
            jax.ShapeDtypeStruct((HOLD,) + parcel[1:], jnp.bfloat16),
        ),
        in_specs=[ANY] * 4,
        out_specs=[ANY] * 5,
        scratch_shapes=[
            pltpu.VMEM((8, half, width, width), stored.dtype),
            pltpu.VMEM(parcel, jnp.bfloat16),
            pltpu.VMEM((blocks, both, width), jnp.bfloat16),
            pltpu.VMEM((blocks, own, width), jnp.bfloat16),
            pltpu.VMEM((both * rows, width), jnp.float32),
            pltpu.VMEM((blocks * both, width), jnp.float32),
            pltpu.VMEM((blocks * own, width), jnp.float32),
            pltpu.VMEM((blocks, own, width), jnp.bfloat16),
            pltpu.VMEM((blocks, own, width), jnp.bfloat16),
            pltpu.VMEM((blocks, rows), jnp.bfloat16),
            pltpu.VMEM((8,) + names.shape, names.dtype),
            pltpu.SMEM((8,) + names.shape, names.dtype),
            pltpu.VMEM((8,) + diag.shape, diag.dtype),
            pltpu.VMEM((3, own, width), jnp.float32),
            pltpu.VMEM((own, width), jnp.float32),
            dma((sends,)),
            dma((8, PIECES)),
            dma((2, PIECES)),
            dma((HOLD,)),
            dma((2, 8)),
            dma((3, 8)),
            dma((5,)),
            dma((4, 2)),
            dma((3, 8)),
            dma((3, 8)),
            dma((3,)),
        ],
        compiler_params=pltpu.CompilerParams(
            collective_id=0, has_side_effects=True, vmem_limit_bytes=60 * 2**20
        ),
    )(stored, target, names, diag)[:3]


def finish_kernel(target_ref, diag_ref, first_ref, second_ref, scale_ref, answer_ref, residual_ref):
    blocks, width, columns = target_ref.shape
    alpha1, alpha2, beta = scale_ref[0:1], scale_ref[1:2], scale_ref[2:3]
    diags = diag_ref[...].T
    for b in range(blocks):
        target = target_ref[b]
        diag = diags[:, b : b + 1]
        first = first_ref[:, b].reshape(columns, width).T.astype(jnp.float32)
        second = second_ref[:, b].reshape(columns, width).T.astype(jnp.float32)
        lost = target - target.astype(jnp.bfloat16).astype(jnp.float32)
        lost1 = lost - alpha1 * diag * lost
        answer_ref[b] = alpha1 * target + alpha2 * (first + lost1 + beta * target)
        residual_ref[b] = second + lost1 - alpha2 * diag * (lost1 + beta * lost)


def finish(target, diag, first, second, scales):
    blocks, width, columns = target.shape
    devices, _, own, _ = second.shape
    step = 8
    whole = pl.BlockSpec((step, width, columns), lambda g: (g, 0, 0))
    part = pl.BlockSpec((devices, step, own, width), lambda g: (0, g, 0, 0))
    return pl.pallas_call(
        finish_kernel,
        out_shape=(jax.ShapeDtypeStruct(target.shape, jnp.float32),) * 2,
        grid=(blocks // step,),
        in_specs=[
            whole,
            pl.BlockSpec((step, width), lambda g: (g, 0)),
            part,
            part,
            pl.BlockSpec(scales.shape, lambda g: (0, 0)),
        ],
        out_specs=(whole, whole),
    )(target, diag, first, second, scales)


def by_columns(blocks, block_rows, block_cols, counts, diagonal, target):
    nrow, ncol = lax.axis_size("row"), lax.axis_size("col")
    devices = nrow * ncol
    stored = blocks[0, 0]
    slots, width, _ = stored.shape
    quarter = target.shape[0] // width
    own = target.shape[1] // devices
    row_blocks = ncol * quarter
    half = slots // 2
    row, col, core = lax.axis_index("row"), lax.axis_index("col"), lax.axis_index("rhs")

    irow = row * row_blocks + block_rows[0, 0]
    jcol = block_cols[0, 0]
    icol = (jcol // quarter * ncol + col) * quarter + jcol % quarter

    def every_other(index):
        return jnp.where(core == 0, index[0::2], index[1::2])

    used = (counts[0] - core + 1) // 2
    gap = jnp.full((LANES // 2 - half,), -1, jnp.int32)
    slots = jnp.concatenate([every_other(irow), gap, every_other(icol), gap])
    names = jnp.stack([slots, jnp.broadcast_to(used, (LANES,))])
    names = jnp.pad(names, ((0, 6), (0, 0)))
    diag_own = diagonal.reshape(quarter, width)
    target_blocks = target.reshape(quarter, width, target.shape[1])
    first_home, second_home, scales = solve(
        stored.reshape(half, 2, width, width), target, names, diag_own
    )
    scales = scales[..., 0].transpose(1, 0, 2).reshape(3, devices * own)
    answer, residual = finish(target_blocks, diag_own, first_home, second_home, scales)
    return (answer.reshape(target.shape), residual.reshape(target.shape))


def one_hot_slots(indices, valid, extent):
    return ((indices[None, :] == jnp.arange(extent)[:, None]) & valid[None, :]).astype(jnp.float32)


def picked(blocks, index):
    return lax.map(lambda i: lax.dynamic_index_in_dim(blocks, i, 0, keepdims=False), index)


def on_device(blocks, block_rows, block_cols, counts, diagonal, target):
    highest = lax.Precision.HIGHEST
    nrow = lax.axis_size("row")
    ncol = lax.axis_size("col")
    if (
        (lax.axis_size("parts"), nrow, ncol, lax.axis_size("rhs")) == (2, 4, 2, 2)
        and target.shape[1] == 128
        and blocks.shape[2] % (16 * PIECES) == 0
        and target.shape[0] // blocks.shape[3] % 64 == 0
    ):
        return by_columns(blocks, block_rows, block_cols, counts, diagonal, target)
    stored = blocks[0, 0]
    slots = stored.shape[0]
    width = stored.shape[1]
    local = target.shape[0]
    ncols = target.shape[1]
    quarter = local // width
    row_blocks = ncol * quarter
    col_blocks = nrow * quarter
    valid = jnp.arange(slots) < counts[0, 0]
    rows_hot = one_hot_slots(block_rows[0, 0], valid, row_blocks)
    cols_hot = one_hot_slots(block_cols[0, 0], valid, col_blocks)

    def squares(vector):
        return lax.psum(jnp.sum(vector * vector, axis=0), ("row", "col"))

    solution = jnp.zeros_like(target)
    residual = target
    direction = target
    norm_now = squares(residual)
    for step in range(ITERS):
        operate_field_low = direction.astype(jnp.bfloat16)
        direct_gathered = lax.all_gather(operate_field_low, "row", axis=0, tiled=True).reshape(
            col_blocks, width, ncols
        )
        prod = jnp.einsum(
            "kab,kbc->kac",
            stored,
            picked(direct_gathered, block_cols[0, 0]),
            preferred_element_type=jnp.float32,
        )
        direct_partial_value = jnp.einsum("ik,kac->iac", rows_hot, prod, precision=highest)
        direct = lax.psum_scatter(
            direct_partial_value.reshape(row_blocks * width, ncols).astype(jnp.bfloat16),
            "col",
            scatter_dimension=0,
            tiled=True,
        ).astype(jnp.float32)
        gathered = lax.all_gather(operate_field_low, "col", axis=0, tiled=True).reshape(
            row_blocks, width, ncols
        )
        tprod = jnp.einsum(
            "kba,kbc->kac",
            stored,
            picked(gathered, block_rows[0, 0]),
            preferred_element_type=jnp.float32,
        )
        partial_value = jnp.einsum("jk,kac->jac", cols_hot, tprod, precision=highest)
        parcel = partial_value.astype(jnp.bfloat16).reshape(nrow, local, ncols)
        mirrored = jnp.sum(
            lax.all_to_all(parcel, "row", split_axis=0, concat_axis=0, tiled=True).astype(
                jnp.float32
            ),
            axis=0,
        )
        image = diagonal[:, None] * direction + direct + mirrored
        curve = lax.psum(jnp.sum(direction * image, axis=0), ("row", "col"))
        alpha = norm_now / curve
        solution = solution + alpha * direction
        residual = residual - alpha * image
        if step + 1 < ITERS:
            norm_next = squares(residual)
            direction = residual + norm_next / norm_now * direction
            norm_now = norm_next
    return (solution, residual)


def solution(mesh):
    return jax.shard_map(
        on_device,
        mesh=mesh,
        in_specs=(
            P(("parts", "row"), "col", None, None, None),
            P(("parts", "row"), "col", None),
            P(("parts", "row"), "col", None),
            P(("parts", "row"), "col"),
            P(("parts", "row", "col")),
            P(("parts", "row", "col"), "rhs"),
        ),
        out_specs=(P(("parts", "row", "col"), "rhs"), P(("parts", "row", "col"), "rhs")),
        check_vma=False,
    )
```

```python
import functools
import jax
import jax.numpy as jnp
from jax import lax
from jax.experimental import pallas as pl
from jax.experimental.pallas import tpu as pltpu
from jax.sharding import PartitionSpec as P

ITERS = 2
LANES = 128
PIECES = 6
MESH = pl.DeviceIdType.MESH
ANY = pl.BlockSpec(memory_space=pl.ANY)


HOLD = 17
ROUTES = (
    (
        (0,0,0,1,1,2), (2,0,1,1,0,0,-1,0,1), (2,0,3,0,0,0,-1,0,2), (2,0,3,1,0,0,-1,1,1), (0,0,0,0,0,2),
        (0,0,0,4,2,1,0), (2,0,2,1,0,0,-1,0,0), (0,0,0,2,0,1), (0,0,0,5,1), (2,0,1,0,0,0,-1,-1,1),
        (2,0,0,1,0,0,-1,-1,0), (0,0,0,3,1,2), (2,0,2,0,0,0,-1,-1,2), (0,1,0,0), (1,1,1,3,2), (0,1,0,3,1,0),
        (1,1,1,0,2), (0,0,1,0,1), (1,1,1,1,2), (0,0,1,4), (0,1,0,2,0), (2,0,2,1,1,0,0,-1,2), (2,1,1,1,0,1,3,4,2),
        (0,1,0,5,1,0), (0,0,1,2,2,1), (1,1,1,2,2), (2,2,0,0,0,0,-1,-1,-1), (2,0,0,1,1,0,-1,-1,-1), (1,1,1,4,2),
        (0,1,1,0), (0,1,1,3), (2,3,1,0,0,0,5,-1,1), (0,0,1,1,2), (0,1,1,2,2,1), (2,3,0,1,0,0,4,-1,0), (0,2,0,5,2),
        (0,1,1,5), (0,1,1,1,1,0), (0,2,0,3,0), (2,3,0,0,0,0,-1,-1,-1), (2,3,0,1,1,0,-1,-1,-1), (0,1,0,4,0),
        (2,2,0,1,1,0,-1,-1,-1), (0,1,0,1), (0,0,1,5), (2,1,1,0,0,0,2,-1,1), (0,2,1,3), (0,2,1,0,0), (0,2,0,1,0,1),
        (0,1,1,4), (0,2,0,2), (0,0,1,3), (0,2,0,0), (2,1,0,1,0,0,1,-1,0), (0,3,0,3,0,2), (0,2,1,1,1), (0,2,1,4,0),
        (0,3,0,0,0), (2,1,0,1,1,0,-1,-1,-1), (2,1,0,0,0,0,-1,-1,-1), (0,3,0,1,0), (0,3,1,3,1,2), (0,3,0,5,1),
        (0,2,1,2,2), (0,2,0,4), (0,3,1,5), (0,3,1,0,1,2), (0,3,0,2,0), (0,2,1,5), (0,3,1,1), (0,3,0,4), (0,3,1,4),
        (0,3,1,2),
    ),
    (
        (1,1,0,3,1), (2,1,3,1,0,1,-1,8,2), (2,1,1,0,0,1,-1,3,2), (1,1,0,0,1), (1,1,0,5,2), (1,1,0,1,1),
        (2,1,3,0,0,1,-1,7,2), (2,1,2,0,0,1,-1,5,2), (2,1,0,1,0,1,-1,2,2), (2,1,1,1,0,1,-1,3,1), (2,1,2,1,0,1,-1,2,0),
        (2,1,0,0,0,1,-1,1,2), (1,1,0,2,1), (1,1,0,4,1), (0,0,0,1,0,2), (2,0,1,1,0,0,0,-1,0), (2,1,2,1,1,1,2,6,2),
        (0,1,0,0,0), (2,0,3,1,0,0,1,0,2), (0,0,1,1,1,2), (2,2,1,0,0,0,-1,-1,-1), (0,0,0,4,0), (2,0,1,1,1,0,-1,-1,-1),
        (0,2,0,5,1,0), (0,0,0,2,2), (0,1,1,0), (2,2,1,1,0,0,3,-1,0), (0,0,0,5,2,0), (0,0,1,4), (0,2,0,0,0),
        (2,0,1,0,0,0,-1,-1,-1), (0,2,1,5), (0,2,0,3,1), (0,0,0,3,0), (2,2,1,1,1,0,-1,-1,-1), (0,1,0,4,1,0),
        (0,1,0,3,0), (0,0,1,5,1), (0,2,0,4), (0,0,1,0,0), (0,2,1,0,1), (0,2,0,2,0,1), (0,1,0,5,2,0), (0,0,1,3,2,1),
        (0,3,0,3,1), (0,0,1,2), (0,1,1,4,2), (0,2,1,3), (2,3,1,0,0,0,-1,-1,-1), (0,1,1,3,2), (0,3,0,0,1),
        (0,1,1,2,0), (0,0,0,0), (0,3,0,1,1,0), (0,1,1,1,0), (0,2,1,2,1,2), (2,3,1,1,1,0,-1,-1,-1), (0,1,1,5),
        (2,1,1,0,0,0,-1,-1,-1), (2,1,1,1,1,0,-1,-1,-1), (0,2,0,1), (0,1,0,2), (0,3,0,2,1,0), (0,3,1,1), (0,2,1,1,2),
        (0,2,1,4), (0,1,0,1,2), (0,3,1,3), (0,3,1,4,1,0), (0,3,1,2), (0,3,0,5), (0,3,1,5), (0,3,1,0), (0,3,0,4),
    ),
    (
        (0,1,0,0,1,0,2), (2,2,1,0,0,0,-1,10,1), (0,1,0,3,2), (2,2,2,1,0,0,-1,-1,0), (2,2,1,1,0,0,-1,11,1),
        (0,1,0,2,2), (2,2,3,0,0,0,-1,-1,1), (0,1,0,5,2,0), (2,2,3,1,0,0,-1,12,1), (0,1,0,1,0), (2,2,0,1,0,0,-1,8,0),
        (0,1,0,4,1,0), (2,2,0,0,0,0,-1,-1,2), (1,0,1,5,3), (0,1,1,0,2), (0,0,0,1), (2,0,3,0,0,0,0,-1,1), (1,0,1,0,3),
        (2,2,2,1,1,0,-1,-1,-1), (2,3,1,0,0,0,11,5,2), (1,0,1,1,3), (0,0,0,0,1,0), (2,3,0,1,0,0,10,4,2), (0,1,1,5),
        (0,0,0,4,0,1), (1,0,1,3,3), (2,3,2,0,0,0,-1,-1,-1), (0,1,1,1,2,1), (1,0,1,4,3), (2,3,0,0,0,0,9,-1,2),
        (2,2,0,1,1,0,8,-1,2), (0,0,0,3,0), (2,3,3,0,0,0,13,-1,1), (2,0,2,0,0,0,-1,-1,-1), (0,1,1,4), (1,0,1,2,3),
        (1,1,1,3,3), (2,3,1,1,1,0,12,14,1), (0,0,1,0), (0,2,0,0,0), (1,1,1,0,3), (2,1,1,0,0,0,3,2,2), (1,1,1,5,3),
        (0,0,1,4,1), (1,1,1,1,3), (2,3,2,1,1,0,-1,-1,-1), (0,2,0,1,2,0), (0,0,1,3), (2,0,2,1,1,0,-1,-1,-1),
        (2,3,3,1,1,0,14,-1,1), (2,1,3,0,0,1,6,-1,3), (0,2,1,0,1), (2,1,1,1,0,1,4,5,0), (2,1,2,0,0,0,-1,-1,-1),
        (0,2,0,4,0), (0,2,1,1), (0,0,1,2,0), (2,1,3,1,1,0,7,-1,1), (0,2,0,2), (2,1,1,1,1,1,5,4,3), (1,1,1,2,3),
        (2,1,0,1,0,0,2,1,2), (0,2,1,3,0), (0,2,1,4,2,1), (1,1,1,4,3), (2,1,0,0,0,0,1,-1,2), (0,3,0,0), (0,0,0,2),
        (0,0,1,1), (2,1,2,1,1,0,-1,-1,-1), (0,3,0,5,0,2), (0,2,0,3), (0,1,1,2,1), (0,0,0,5,0), (0,3,1,5,1,2),
        (0,2,0,5,0), (0,3,1,1,0), (0,0,1,5,1), (0,3,0,2,0), (0,3,0,3), (0,2,1,5,2), (0,3,0,4,2), (0,3,1,3),
        (0,3,0,1), (0,1,1,3), (0,2,1,2), (0,3,1,2), (0,3,1,4), (0,3,1,0),
    ),
    (
        (1,0,0,5,1), (1,0,0,0,1), (1,0,0,1,1), (2,3,1,0,0,1,-1,11,3), (1,0,0,3,1), (2,3,1,1,0,1,-1,13,0),
        (2,3,0,1,0,1,-1,10,3), (1,0,0,4,1), (2,3,2,0,0,1,-1,-1,3), (2,3,2,1,0,1,-1,15,0), (2,3,3,1,0,1,-1,16,0),
        (2,3,0,0,0,1,-1,9,3), (2,3,3,0,0,1,-1,13,3), (1,0,0,2,1), (0,1,0,0,2,0), (2,2,1,0,0,0,10,-1,2),
        (2,1,3,1,0,1,8,9,0), (2,3,1,1,1,1,13,12,3), (0,2,0,5,2,0), (2,1,1,0,0,1,3,3,3), (2,2,1,1,0,0,11,3,2),
        (2,3,2,1,1,1,15,-1,3), (0,2,0,0,2,1), (1,1,1,5,1), (2,3,3,1,1,1,16,14,3), (2,2,3,0,0,0,-1,-1,-1),
        (0,2,0,1,1), (2,1,3,0,0,1,7,6,1), (2,2,3,1,0,0,12,-1,0), (0,1,1,0), (0,2,0,3,2,0), (2,1,2,0,0,1,5,-1,3),
        (0,1,0,4,2), (2,1,3,1,1,1,9,7,3), (0,2,0,4,1,2), (2,1,0,1,0,1,2,2,3), (2,0,3,0,0,0,-1,-1,-1), (0,2,1,5),
        (0,2,0,2,2,1), (2,1,0,0,0,1,1,1,3), (0,0,0,0,0), (2,2,3,1,1,0,-1,-1,-1), (0,3,0,3,2,0), (0,0,0,1), (0,0,0,4),
        (0,2,1,3,1,2), (0,3,0,0,2,1,0), (2,1,2,1,1,1,6,-1,3), (0,1,1,1), (0,0,1,0), (0,3,0,5,1),
        (2,0,3,1,0,0,0,-1,0), (2,3,3,0,0,0,-1,-1,-1), (0,3,1,3), (0,3,0,1,2,0), (0,0,1,1), (2,3,1,1,1,0,14,-1,2),
        (0,3,1,0), (2,1,3,0,0,0,-1,-1,-1), (0,0,0,2,0), (0,0,1,4), (2,0,3,1,1,0,-1,-1,-1), (2,1,1,1,1,0,4,-1,2),
        (0,0,0,5,1), (2,3,3,1,1,0,-1,-1,-1), (0,3,1,1,1), (0,3,0,2,2,1,0), (0,2,1,0), (0,1,0,5,0), (0,0,1,2),
        (0,3,0,4,0,1), (0,0,1,3,0), (2,1,3,1,1,0,-1,-1,-1), (0,3,1,2), (0,1,1,4), (0,2,1,4,2), (0,1,1,5),
        (0,1,1,3,1,0), (0,3,1,4,2,1), (0,1,1,2,0), (0,2,1,2), (0,0,0,3), (0,3,1,5,2), (0,0,1,5), (0,1,0,3),
        (0,2,1,1), (0,1,0,2), (0,1,0,1),
    ),
)


def flipped(index, bits, devices):
    total, unit = index, 1
    while unit < devices:
        if bits & unit:
            total = total + unit * (1 - 2 * lax.rem(index // unit, 2))
        unit *= 2
    return total


class Place:
    def __init__(self):
        self.part, self.row = lax.axis_index("parts"), lax.axis_index("row")
        self.col, self.core = lax.axis_index("col"), lax.axis_index("rhs")
        self.half = self.row // 2
        self.low = lax.rem(self.row, 2)
        self.shard = self.row * 2 + self.col
        self.group = self.low * 4 + self.part * 2 + self.col
        self.foreign = lax.rem(self.half + self.part, 2)
        self.inner = lax.rem(self.half + self.low, 2)

    def link(self, way):
        if way == 0:
            return {"col": 1 - self.col}
        if way == 1:
            return {"parts": 1 - self.part}
        if way == 2:
            return {"row": self.half * 2 + 1 - self.low}
        return {"row": 3 - self.row}

    def tile_row(self, kind):
        return (3 * self.half, 1 + self.half, 2 - self.half, 3 - 3 * self.half)[kind]

    def solver(self, group):
        return {
            "row": 2 * self.part + group // 4,
            "parts": lax.rem(group // 2, 2),
            "col": lax.rem(group, 2),
        }

    def owner(self, shard):
        return {"row": shard // 2, "parts": self.half, "col": lax.rem(shard, 2)}


def greet_all(place, sibling):
    barrier = pltpu.get_barrier_semaphore()
    me = place.part * 8 + place.shard
    for offset in range(1, 16):
        other = lax.rem(me + offset, 16)
        peer = {"parts": other // 8, "row": lax.rem(other, 8) // 2, "col": lax.rem(other, 2)}
        pl.semaphore_signal(barrier, inc=1, device_id=peer, device_id_type=MESH)
    if sibling:
        pl.semaphore_signal(barrier, inc=1, device_id={"rhs": 1 - place.core}, device_id_type=MESH)
    pl.semaphore_wait(barrier, 15 + sibling)


def solve_kernel(
    stored, target, names, diag,
    first_home, second_home, scales, transit, hold,
    tiles, parcel, field, start, terms, image, first, away_out, away_in, hot, names_v, names_s, diag_v, scale, norm,
    piece_send, piece_recv, pass_recv, hold_recv, send, recv, own_sem, pair_sem, home_send, home_recv, home_own,
):
    place = Place()
    shard, core, foreign = place.shard, place.core, place.foreign
    half = tiles.shape[1]
    size = half // PIECES
    blocks, both, width = field.shape
    own = both // 2
    quarter = blocks // 8
    step_blocks = 16
    steps = blocks // step_blocks
    rows = hot.shape[1]
    fetch = pltpu.make_async_copy(target, first, own_sem.at[4])
    fetch.start()
    greet_all(place, 1)

    def part_of(k):
        return pl.ds(k * size, size)

    def mine(s):
        return field.at[pl.ds(s * quarter, quarter), pl.ds(0, own)]

    def piece_copy(source, target, way, send_sem, recv_sem):
        return pltpu.make_async_remote_copy(
            src_ref=source, dst_ref=target, send_sem=send_sem, recv_sem=recv_sem,
            device_id=place.link(way), device_id_type=MESH,
        )

    def source_shard(entry):
        solved = place.half if entry[5] == 0 else 1 - place.half
        row = (3 * solved, 3 - 3 * solved, 1 + solved, 2 - solved)[entry[1]]
        return row * 2 + (1 - place.col if entry[4] else place.col)

    def dest_group(entry):
        low = lax.rem(entry[2] // 2 + place.part, 2)
        part = 1 - place.part if entry[2] % 2 else place.part
        return low * 4 + part * 2 + (1 - place.col if entry[3] else place.col)

    def step(kind, entry, count):
        if entry[0] == 2:
            slot_in, slot_out, way = entry[6:]
            if entry[4] == 0 and slot_in < 0 and way >= 0:
                source = parcel.at[dest_group(entry)]
            elif way < 0:
                s = source_shard(entry)
                piece_copy(mine(s), mine(s), 0, piece_send.at[0], recv.at[2, s]).wait_recv()
                return count
            else:
                source = hold.at[slot_in]
                piece_copy(source, source, 0, piece_send.at[0], hold_recv.at[slot_in]).wait_recv()
            if slot_out < 0:
                s = source_shard(entry)
                target, sem = mine(s), recv.at[2, s]
            else:
                target, sem = hold.at[slot_out], hold_recv.at[slot_out]
            piece_copy(source, target, way, piece_send.at[count], sem).start()
            return count + 1
        k = entry[3]
        if entry[0] == 0:
            s = place.tile_row(entry[1]) * 2 + (1 - place.col if entry[2] else place.col)
            here = kind in (0, 2) and entry[1] == kind // 2 and entry[2] == 0
            source, sem = tiles.at[s, part_of(k)], piece_recv.at[s, k]
        else:
            s = place.tile_row(1 - entry[1]) * 2 + place.col
            here = entry[2] == 0
            source, sem = transit.at[entry[1], part_of(k)], pass_recv.at[entry[1], k]
        if here:
            source = stored.at[part_of(k), core]
        else:
            piece_copy(source, source, 0, piece_send.at[0], sem).wait_recv()
        for way in entry[4:]:
            if entry[0] == 0 or way == 3:
                target, sem = tiles.at[s, part_of(k)], piece_recv.at[s, k]
            else:
                target, sem = transit.at[entry[1], part_of(k)], pass_recv.at[entry[1], k]
            piece_copy(source, target, way, piece_send.at[count], sem).start()
            count += 1
        return count

    def sends(entry):
        return int(entry[8] >= 0) if entry[0] == 2 else len(entry) - 4

    def each_class(body):
        for kind in range(4):
            @pl.when((foreign == kind % 2) & (place.inner == kind // 2))
            def _(kind=kind):
                entries = ROUTES[kind]
                begin = [entry[0] for entry in entries].index(2)
                body(kind, entries, begin)

    def before_pack(kind, entries, begin):
        count = 0
        for entry in entries[:begin]:
            count = step(kind, entry, count)

    def sent(kind, entries, begin):
        count = 0
        for entry in entries:
            for _ in range(sends(entry)):
                block = parcel.at[0] if entry[0] == 2 else stored.at[part_of(0), core]
                piece_copy(block, block, 0, piece_send.at[count], piece_recv.at[shard, 0]).wait_send()
                count += 1

    each_class(before_pack)
    fetch.wait()

    def pack(n, carry):
        for u in range(4):
            b = n * 4 + u
            low = first[pl.ds(b * width, width)].astype(jnp.bfloat16).T
            parcel[:, b] = low.reshape(8, own, width)
        return carry

    lax.fori_loop(0, quarter // 4, pack, 0)
    pairs = ((names, names_v), (diag, diag_v))

    def straight(n, bits):
        group = flipped(place.group, bits, 8)
        return pltpu.make_async_remote_copy(
            src_ref=pairs[n][0],
            dst_ref=pairs[n][1].at[shard],
            send_sem=send.at[n, bits],
            recv_sem=recv.at[n, shard],
            device_id=place.solver(group),
            device_id_type=MESH,
        )

    def arrival(n, bits):
        landed = pairs[n][1].at[flipped(shard, bits, 8)]
        return pltpu.make_async_remote_copy(
            src_ref=landed, dst_ref=landed, send_sem=send.at[n, 0],
            recv_sem=recv.at[n, flipped(shard, bits, 8)],
            device_id=place.link(0), device_id_type=MESH,
        )

    def local(n):
        source, landed = (
            (names, names_v.at[shard]),
            (diag, diag_v.at[shard]),
            (parcel.at[place.group], mine(shard)),
            (stored.at[:, core], tiles.at[shard]),
        )[n]
        return pltpu.make_async_copy(source, landed, own_sem.at[n])

    for n in range(2):
        for bits in range(1, 8):
            straight(n, bits).start()

    @pl.when(foreign == 1)
    def _():
        for n in range(2):
            straight(n, 0).start()

    @pl.when(foreign == 0)
    def _():
        for n in range(4):
            local(n).start()

    def blank(b, carry):
        terms[pl.ds(b * rows, rows)] = jnp.zeros((rows, width), jnp.float32)
        return carry

    lax.fori_loop(0, both, blank, 0)

    for n in range(2):
        for bits in range(1, 8):
            arrival(n, bits).wait_recv()
            straight(n, bits).wait_send()

    @pl.when(foreign == 1)
    def _():
        for n in range(2):
            arrival(n, 0).wait_recv()
            straight(n, 0).wait_send()

    @pl.when(foreign == 0)
    def _():
        for n in range(4):
            local(n).wait()

    read = pltpu.make_async_copy(names_v, names_s, own_sem.at[4])
    read.start()

    for s in range(8):
        names_row = names_v[s, 0:1, :]
        at = lax.broadcasted_iota(jnp.int32, (blocks, LANES), 0)
        hot[:, s * LANES : (s + 1) * LANES] = jnp.where(at == names_row, 1.0, 0.0).astype(jnp.bfloat16)

    read.wait()
    def swap(n, source, landed):
        return pltpu.make_async_remote_copy(
            src_ref=source, dst_ref=landed, send_sem=pair_sem.at[n, 0], recv_sem=pair_sem.at[n, 1],
            device_id={"rhs": 1 - core}, device_id_type=MESH,
        )

    ours, theirs = field.at[:, pl.ds(0, own)], field.at[:, pl.ds(own, own)]
    pair = swap(0, ours, theirs)
    zero = jnp.zeros((own, width), jnp.float32)

    def chunk(ref, n):
        return ref[pl.ds(n * step_blocks, step_blocks)]

    def keep(n, total):
        low = field[pl.ds(n * step_blocks, step_blocks), 0:own]
        start[pl.ds(n * step_blocks, step_blocks)] = low
        value = low.astype(jnp.float32)
        return total + jnp.sum(value * value, axis=0)

    def keep_start():
        norm[...] = lax.fori_loop(0, steps, keep, zero)

    def product(s, k):
        results = []
        for u in range(size):
            slot = k * size + u
            i, j = names_s[s, 0, slot], names_s[s, 0, LANES // 2 + slot]
            block = tiles[s, slot]
            direct = lax.dot_general(
                field[j], block, (((1,), (1,)), ((), ())), preferred_element_type=jnp.float32
            )
            mirrored = lax.dot_general(
                field[i], block, (((1,), (0,)), ((), ())), preferred_element_type=jnp.float32
            )
            results.append((slot, slot < names_s[s, 1, 0], direct, mirrored))
        for slot, used, direct, mirrored in results:
            at = s * LANES + slot
            terms[pl.ds(at, both, stride=rows)] = jnp.where(used, direct, 0.0)
            terms[pl.ds(at + LANES // 2, both, stride=rows)] = jnp.where(used, mirrored, 0.0)

    def products(n, carry):
        product(n // PIECES, lax.rem(n, PIECES))
        return carry

    def product_pair(row, k):
        def one(col, carry):
            product(place.tile_row(row) * 2 + col, k)
            return carry

        lax.fori_loop(0, 2, one, 0)

    def after_pack(kind, entries, begin):
        count = sum(sends(entry) for entry in entries[:begin])
        ready = max(n for n, entry in enumerate(entries) if entry[0] == 2 and entry[8] < 0)
        landed, due = set(), []
        for n, entry in enumerate(entries):
            if n >= begin:
                count = step(kind, entry, count)
            if entry[0] == 0:
                landed.add(entry[1:4])
                if (entry[1], 1 - entry[2], entry[3]) in landed:
                    due.append((entry[1], entry[3]))
            if n == ready:
                pair.start()
            if n == min(ready + 1, len(entries) - 1):
                keep_start()
            if n == min(ready + 2, len(entries) - 1):
                pair.wait()
            if n >= ready + 2:
                for _ in range(-(-len(due) // (len(entries) - n))):
                    product_pair(*due.pop(0))
        for one in due:
            product_pair(*one)

    each_class(after_pack)
    each_class(sent)

    def gather_sums(n, carry):
        c = 2 * n
        pair = [terms[pl.ds((c + m) * rows, rows)].astype(jnp.bfloat16) for m in range(2)]
        total = jnp.dot(
            hot[...], jnp.concatenate(pair, axis=1), preferred_element_type=jnp.float32
        )
        for m in range(2):
            image[pl.ds(c + m, blocks, stride=both)] = total[:, m * width : (m + 1) * width]
        return carry

    def image_chunk(n):
        return image[pl.ds(n * step_blocks * both, step_blocks * both)].reshape(step_blocks, both, width)

    def first_chunk(n):
        return first[pl.ds(n * step_blocks * own, step_blocks * own)].reshape(step_blocks, own, width)

    def start_chunk(n):
        return chunk(start, n).astype(jnp.float32)

    def diag_chunk(n):
        per = quarter // step_blocks
        return diag_v[n // per, pl.ds(lax.rem(n, per) * step_blocks, step_blocks)][:, None, :]

    def operate(exchange, direction_chunk):
        lax.fori_loop(own // 2, own, gather_sums, 0)

        def away(n, carry):
            away_out[pl.ds(n * step_blocks, step_blocks)] = image_chunk(n)[:, own:].astype(jnp.bfloat16)
            return carry

        lax.fori_loop(0, steps, away, 0)
        over = swap(exchange, away_out, away_in)
        over.start()
        lax.fori_loop(0, own // 2, gather_sums, 0)
        over.wait()

        def join(n, total):
            direction = direction_chunk(n)
            value = image_chunk(n)[:, :own] + chunk(away_in, n).astype(jnp.float32)
            value = value + diag_chunk(n) * direction
            image[pl.ds(n * step_blocks * own, step_blocks * own)] = value.reshape(step_blocks * own, width)
            return total + jnp.sum(value * direction, axis=0)

        return jnp.sum(lax.fori_loop(0, steps, join, zero), axis=1, keepdims=True)

    def joined_chunk(n):
        return image[pl.ds(n * step_blocks * own, step_blocks * own)].reshape(step_blocks, own, width)

    home = ((scale, scales), (parcel, first_home), (away_out, second_home))

    def leaving(n, to):
        if n == 0:
            return scale
        return parcel.at[to] if n == 1 else away_out.at[pl.ds(to * quarter, quarter)]

    def home_copy(n, bits):
        to = flipped(shard, bits, 8)
        return pltpu.make_async_remote_copy(
            src_ref=leaving(n, to),
            dst_ref=home[n][1].at[place.group],
            send_sem=home_send.at[n, bits],
            recv_sem=home_recv.at[n, place.group],
            device_id=place.owner(to),
            device_id_type=MESH,
        )

    def home_arrival(n, bits):
        landed = home[n][1].at[flipped(place.group, bits, 8)]
        return pltpu.make_async_remote_copy(
            src_ref=landed, dst_ref=landed, send_sem=home_send.at[n, 0],
            recv_sem=home_recv.at[n, flipped(place.group, bits, 8)],
            device_id=place.link(0), device_id_type=MESH,
        )

    def home_local(n):
        return pltpu.make_async_copy(leaving(n, shard), home[n][1].at[place.group], home_own.at[n])

    def go_home(n):
        for bits in range(7, 0, -1):
            home_copy(n, bits).start()

        @pl.when(foreign == 1)
        def _():
            home_copy(n, 0).start()

        @pl.when(foreign == 0)
        def _():
            home_local(n).start()

    def arrive_home(n):
        for bits in range(1, 8):
            home_copy(n, bits).wait_send()
            home_arrival(n, bits).wait_recv()

        @pl.when(foreign == 1)
        def _():
            home_copy(n, 0).wait_send()
            home_arrival(n, 0).wait_recv()

        @pl.when(foreign == 0)
        def _():
            home_local(n).wait()

    per = quarter // step_blocks
    norm0 = jnp.sum(norm[...], axis=1, keepdims=True)
    alpha1 = norm0 / operate(1, start_chunk)

    def next_first(n, total):
        value = start_chunk(n) - alpha1[None] * joined_chunk(n)
        first[pl.ds(n * step_blocks * own, step_blocks * own)] = value.reshape(step_blocks * own, width)
        parcel[n // per, pl.ds(lax.rem(n, per) * step_blocks, step_blocks)] = value.astype(jnp.bfloat16)
        return total + jnp.sum(value * value, axis=0)

    norm1 = jnp.sum(lax.fori_loop(0, steps, next_first, zero), axis=1, keepdims=True)
    go_home(1)
    beta = norm1 / norm0

    def direction_chunk(n):
        return first_chunk(n) + beta[None] * start_chunk(n)

    def next_low(n, carry):
        field[pl.ds(n * step_blocks, step_blocks), 0:own] = direction_chunk(n).astype(jnp.bfloat16)
        return carry

    lax.fori_loop(0, steps, next_low, 0)
    pair = swap(2, ours, theirs)
    pair.start()
    pair.wait()
    lax.fori_loop(0, 8 * PIECES, products, 0)
    alpha2 = norm1 / operate(3, direction_chunk)

    def last(n, carry):
        value = first_chunk(n) - alpha2[None] * joined_chunk(n)
        away_out[pl.ds(n * step_blocks, step_blocks)] = value.astype(jnp.bfloat16)
        return carry

    lax.fori_loop(0, steps, last, 0)
    go_home(2)
    for n, value in enumerate((alpha1, alpha2, beta)):
        scale[n] = jnp.broadcast_to(value, (own, width))
    go_home(0)
    for n in (1, 2, 0):
        arrive_home(n)


def solve(stored, target, names, diag):
    half, cores, width, _ = stored.shape
    quarter, columns = target.shape[0] // width, target.shape[1]
    own = columns // 8
    parcel = (8, quarter, own, width)
    blocks, both, rows = 8 * quarter, 2 * own, 8 * LANES
    sends = max(
        sum(int(e[8] >= 0) if e[0] == 2 else len(e) - 4 for e in entries) for entries in ROUTES
    )
    dma = pltpu.SemaphoreType.DMA
    return pl.pallas_call(
        solve_kernel,
        out_shape=(
            jax.ShapeDtypeStruct(parcel, jnp.bfloat16),
            jax.ShapeDtypeStruct(parcel, jnp.bfloat16),
            jax.ShapeDtypeStruct((8, 3, own, width), jnp.float32),
            jax.ShapeDtypeStruct((2, half, width, width), stored.dtype),
            jax.ShapeDtypeStruct((HOLD,) + parcel[1:], jnp.bfloat16),
        ),
        in_specs=[ANY] * 4,
        out_specs=[ANY] * 5,
        scratch_shapes=[
            pltpu.VMEM((8, half, width, width), stored.dtype),
            pltpu.VMEM(parcel, jnp.bfloat16),
            pltpu.VMEM((blocks, both, width), jnp.bfloat16),
            pltpu.VMEM((blocks, own, width), jnp.bfloat16),
            pltpu.VMEM((both * rows, width), jnp.float32),
            pltpu.VMEM((blocks * both, width), jnp.float32),
            pltpu.VMEM((blocks * own, width), jnp.float32),
            pltpu.VMEM((blocks, own, width), jnp.bfloat16),
            pltpu.VMEM((blocks, own, width), jnp.bfloat16),
            pltpu.VMEM((blocks, rows), jnp.bfloat16),
            pltpu.VMEM((8,) + names.shape, names.dtype),
            pltpu.SMEM((8,) + names.shape, names.dtype),
            pltpu.VMEM((8,) + diag.shape, diag.dtype),
            pltpu.VMEM((3, own, width), jnp.float32),
            pltpu.VMEM((own, width), jnp.float32),
            dma((sends,)),
            dma((8, PIECES)),
            dma((2, PIECES)),
            dma((HOLD,)),
            dma((2, 8)),
            dma((3, 8)),
            dma((5,)),
            dma((4, 2)),
            dma((3, 8)),
            dma((3, 8)),
            dma((3,)),
        ],
        compiler_params=pltpu.CompilerParams(
            collective_id=0, has_side_effects=True, vmem_limit_bytes=60 * 2**20
        ),
    )(stored, target, names, diag)[:3]


def finish_kernel(target_ref, diag_ref, first_ref, second_ref, scale_ref, answer_ref, residual_ref, scale_rows):
    blocks, width, columns = target_ref.shape

    @pl.when(pl.program_id(0) == 0)
    def _():
        for n in range(3):
            scale_rows[n] = scale_ref[:, n].reshape(columns, width).T[0:8]

    alpha1, alpha2, beta = scale_rows[0, 0:1], scale_rows[1, 0:1], scale_rows[2, 0:1]
    diags = diag_ref[...].T
    same = lax.broadcasted_iota(jnp.int32, (width, columns), 0) == lax.broadcasted_iota(
        jnp.int32, (width, columns), 1
    )
    unit = jnp.where(same, 1.0, 0.0).astype(jnp.bfloat16)

    def turned(value):
        return lax.dot_general(
            unit, value.reshape(columns, width), (((1,), (1,)), ((), ())), preferred_element_type=jnp.float32
        )

    for b in range(blocks):
        target = target_ref[b]
        diag = diags[:, b : b + 1]
        first, second = turned(first_ref[:, b]), turned(second_ref[:, b])
        lost = target - target.astype(jnp.bfloat16).astype(jnp.float32)
        lost1 = lost - alpha1 * diag * lost
        answer_ref[b] = alpha1 * target + alpha2 * (first + lost1 + beta * target)
        residual_ref[b] = second + lost1 - alpha2 * diag * (lost1 + beta * lost)


def finish(target, diag, first, second, scales):
    blocks, width, columns = target.shape
    devices, _, own, _ = second.shape
    step = 16
    whole = pl.BlockSpec((step, width, columns), lambda g: (g, 0, 0))
    part = pl.BlockSpec((devices, step, own, width), lambda g: (0, g, 0, 0))
    return pl.pallas_call(
        finish_kernel,
        out_shape=(jax.ShapeDtypeStruct(target.shape, jnp.float32),) * 2,
        grid=(blocks // step,),
        in_specs=[
            whole,
            pl.BlockSpec((step, width), lambda g: (g, 0)),
            part,
            part,
            pl.BlockSpec(scales.shape, lambda g: (0, 0, 0, 0)),
        ],
        out_specs=(whole, whole),
        scratch_shapes=[pltpu.VMEM((3, 8, columns), jnp.float32)],
        compiler_params=pltpu.CompilerParams(vmem_limit_bytes=40 * 2**20),
    )(target, diag, first, second, scales)


def by_columns(blocks, block_rows, block_cols, counts, diagonal, target):
    nrow, ncol = lax.axis_size("row"), lax.axis_size("col")
    devices = nrow * ncol
    stored = blocks[0, 0]
    slots, width, _ = stored.shape
    quarter = target.shape[0] // width
    row_blocks = ncol * quarter
    half = slots // 2
    row, col, core = lax.axis_index("row"), lax.axis_index("col"), lax.axis_index("rhs")

    irow = row * row_blocks + block_rows[0, 0]
    jcol = block_cols[0, 0]
    icol = (jcol // quarter * ncol + col) * quarter + jcol % quarter

    def every_other(index):
        return jnp.where(core == 0, index[0::2], index[1::2])

    used = (counts[0] - core + 1) // 2
    gap = jnp.full((LANES // 2 - half,), -1, jnp.int32)
    slots = jnp.concatenate([every_other(irow), gap, every_other(icol), gap])
    names = jnp.stack([slots, jnp.broadcast_to(used, (LANES,))])
    names = jnp.pad(names, ((0, 6), (0, 0)))
    diag_own = diagonal.reshape(quarter, width)
    target_blocks = target.reshape(quarter, width, target.shape[1])
    first_home, second_home, scales = solve(
        stored.reshape(half, 2, width, width), target, names, diag_own
    )
    answer, residual = finish(target_blocks, diag_own, first_home, second_home, scales)
    return (answer.reshape(target.shape), residual.reshape(target.shape))


def one_hot_slots(indices, valid, extent):
    return ((indices[None, :] == jnp.arange(extent)[:, None]) & valid[None, :]).astype(jnp.float32)


def picked(blocks, index):
    return lax.map(lambda i: lax.dynamic_index_in_dim(blocks, i, 0, keepdims=False), index)


def on_device(blocks, block_rows, block_cols, counts, diagonal, target):
    highest = lax.Precision.HIGHEST
    nrow = lax.axis_size("row")
    ncol = lax.axis_size("col")
    if (
        (lax.axis_size("parts"), nrow, ncol, lax.axis_size("rhs")) == (2, 4, 2, 2)
        and target.shape[1] == 128
        and blocks.shape[2] % (16 * PIECES) == 0
        and target.shape[0] // blocks.shape[3] % 64 == 0
    ):
        return by_columns(blocks, block_rows, block_cols, counts, diagonal, target)
    stored = blocks[0, 0]
    slots = stored.shape[0]
    width = stored.shape[1]
    local = target.shape[0]
    ncols = target.shape[1]
    quarter = local // width
    row_blocks = ncol * quarter
    col_blocks = nrow * quarter
    valid = jnp.arange(slots) < counts[0, 0]
    rows_hot = one_hot_slots(block_rows[0, 0], valid, row_blocks)
    cols_hot = one_hot_slots(block_cols[0, 0], valid, col_blocks)

    def squares(vector):
        return lax.psum(jnp.sum(vector * vector, axis=0), ("row", "col"))

    solution = jnp.zeros_like(target)
    residual = target
    direction = target
    norm_now = squares(residual)
    for step in range(ITERS):
        operate_field_low = direction.astype(jnp.bfloat16)
        direct_gathered = lax.all_gather(operate_field_low, "row", axis=0, tiled=True).reshape(
            col_blocks, width, ncols
        )
        prod = jnp.einsum(
            "kab,kbc->kac",
            stored,
            picked(direct_gathered, block_cols[0, 0]),
            preferred_element_type=jnp.float32,
        )
        direct_partial_value = jnp.einsum("ik,kac->iac", rows_hot, prod, precision=highest)
        direct = lax.psum_scatter(
            direct_partial_value.reshape(row_blocks * width, ncols).astype(jnp.bfloat16),
            "col",
            scatter_dimension=0,
            tiled=True,
        ).astype(jnp.float32)
        gathered = lax.all_gather(operate_field_low, "col", axis=0, tiled=True).reshape(
            row_blocks, width, ncols
        )
        tprod = jnp.einsum(
            "kba,kbc->kac",
            stored,
            picked(gathered, block_rows[0, 0]),
            preferred_element_type=jnp.float32,
        )
        partial_value = jnp.einsum("jk,kac->jac", cols_hot, tprod, precision=highest)
        parcel = partial_value.astype(jnp.bfloat16).reshape(nrow, local, ncols)
        mirrored = jnp.sum(
            lax.all_to_all(parcel, "row", split_axis=0, concat_axis=0, tiled=True).astype(
                jnp.float32
            ),
            axis=0,
        )
        image = diagonal[:, None] * direction + direct + mirrored
        curve = lax.psum(jnp.sum(direction * image, axis=0), ("row", "col"))
        alpha = norm_now / curve
        solution = solution + alpha * direction
        residual = residual - alpha * image
        if step + 1 < ITERS:
            norm_next = squares(residual)
            direction = residual + norm_next / norm_now * direction
            norm_now = norm_next
    return (solution, residual)


def solution(mesh):
    return jax.shard_map(
        on_device,
        mesh=mesh,
        in_specs=(
            P(("parts", "row"), "col", None, None, None),
            P(("parts", "row"), "col", None),
            P(("parts", "row"), "col", None),
            P(("parts", "row"), "col"),
            P(("parts", "row", "col")),
            P(("parts", "row", "col"), "rhs"),
        ),
        out_specs=(P(("parts", "row", "col"), "rhs"), P(("parts", "row", "col"), "rhs")),
        check_vma=False,
    )
```

```python
import functools
import jax
import jax.numpy as jnp
from jax import lax
from jax.experimental import pallas as pl
from jax.experimental.pallas import tpu as pltpu
from jax.sharding import PartitionSpec as P

ITERS = 2
LANES = 128
PIECES = 6
MESH = pl.DeviceIdType.MESH
ANY = pl.BlockSpec(memory_space=pl.ANY)


HOLD = 17
ROUTES = (
    (
        (0,0,0,1,1,2), (2,0,1,1,0,0,-1,0,1), (2,0,3,0,0,0,-1,0,2), (2,0,3,1,0,0,-1,1,1), (0,0,0,0,0,2),
        (0,0,0,4,2,1,0), (2,0,2,1,0,0,-1,0,0), (0,0,0,2,0,1), (0,0,0,5,1), (2,0,1,0,0,0,-1,-1,1),
        (2,0,0,1,0,0,-1,-1,0), (0,0,0,3,1,2), (2,0,2,0,0,0,-1,-1,2), (0,1,0,0), (1,1,1,3,2), (0,1,0,3,1,0),
        (1,1,1,0,2), (0,0,1,0,1), (1,1,1,1,2), (0,0,1,4), (0,1,0,2,0), (2,0,2,1,1,0,0,-1,2), (2,1,1,1,0,1,3,4,2),
        (0,1,0,5,1,0), (0,0,1,2,2,1), (1,1,1,2,2), (2,2,0,0,0,0,-1,-1,-1), (2,0,0,1,1,0,-1,-1,-1), (1,1,1,4,2),
        (0,1,1,0), (0,1,1,3), (2,3,1,0,0,0,5,-1,1), (0,0,1,1,2), (0,1,1,2,2,1), (2,3,0,1,0,0,4,-1,0), (0,2,0,5,2),
        (0,1,1,5), (0,1,1,1,1,0), (0,2,0,3,0), (2,3,0,0,0,0,-1,-1,-1), (2,3,0,1,1,0,-1,-1,-1), (0,1,0,4,0),
        (2,2,0,1,1,0,-1,-1,-1), (0,1,0,1), (0,0,1,5), (2,1,1,0,0,0,2,-1,1), (0,2,1,3), (0,2,1,0,0), (0,2,0,1,0,1),
        (0,1,1,4), (0,2,0,2), (0,0,1,3), (0,2,0,0), (2,1,0,1,0,0,1,-1,0), (0,3,0,3,0,2), (0,2,1,1,1), (0,2,1,4,0),
        (0,3,0,0,0), (2,1,0,1,1,0,-1,-1,-1), (2,1,0,0,0,0,-1,-1,-1), (0,3,0,1,0), (0,3,1,3,1,2), (0,3,0,5,1),
        (0,2,1,2,2), (0,2,0,4), (0,3,1,5), (0,3,1,0,1,2), (0,3,0,2,0), (0,2,1,5), (0,3,1,1), (0,3,0,4), (0,3,1,4),
        (0,3,1,2),
    ),
    (
        (1,1,0,3,1), (2,1,3,1,0,1,-1,8,2), (2,1,1,0,0,1,-1,3,2), (1,1,0,0,1), (1,1,0,5,2), (1,1,0,1,1),
        (2,1,3,0,0,1,-1,7,2), (2,1,2,0,0,1,-1,5,2), (2,1,0,1,0,1,-1,2,2), (2,1,1,1,0,1,-1,3,1), (2,1,2,1,0,1,-1,2,0),
        (2,1,0,0,0,1,-1,1,2), (1,1,0,2,1), (1,1,0,4,1), (0,0,0,1,0,2), (2,0,1,1,0,0,0,-1,0), (2,1,2,1,1,1,2,6,2),
        (0,1,0,0,0), (2,0,3,1,0,0,1,0,2), (0,0,1,1,1,2), (2,2,1,0,0,0,-1,-1,-1), (0,0,0,4,0), (2,0,1,1,1,0,-1,-1,-1),
        (0,2,0,5,1,0), (0,0,0,2,2), (0,1,1,0), (2,2,1,1,0,0,3,-1,0), (0,0,0,5,2,0), (0,0,1,4), (0,2,0,0,0),
        (2,0,1,0,0,0,-1,-1,-1), (0,2,1,5), (0,2,0,3,1), (0,0,0,3,0), (2,2,1,1,1,0,-1,-1,-1), (0,1,0,4,1,0),
        (0,1,0,3,0), (0,0,1,5,1), (0,2,0,4), (0,0,1,0,0), (0,2,1,0,1), (0,2,0,2,0,1), (0,1,0,5,2,0), (0,0,1,3,2,1),
        (0,3,0,3,1), (0,0,1,2), (0,1,1,4,2), (0,2,1,3), (2,3,1,0,0,0,-1,-1,-1), (0,1,1,3,2), (0,3,0,0,1),
        (0,1,1,2,0), (0,0,0,0), (0,3,0,1,1,0), (0,1,1,1,0), (0,2,1,2,1,2), (2,3,1,1,1,0,-1,-1,-1), (0,1,1,5),
        (2,1,1,0,0,0,-1,-1,-1), (2,1,1,1,1,0,-1,-1,-1), (0,2,0,1), (0,1,0,2), (0,3,0,2,1,0), (0,3,1,1), (0,2,1,1,2),
        (0,2,1,4), (0,1,0,1,2), (0,3,1,3), (0,3,1,4,1,0), (0,3,1,2), (0,3,0,5), (0,3,1,5), (0,3,1,0), (0,3,0,4),
    ),
    (
        (0,1,0,0,1,0,2), (2,2,1,0,0,0,-1,10,1), (0,1,0,3,2), (2,2,2,1,0,0,-1,-1,0), (2,2,1,1,0,0,-1,11,1),
        (0,1,0,2,2), (2,2,3,0,0,0,-1,-1,1), (0,1,0,5,2,0), (2,2,3,1,0,0,-1,12,1), (0,1,0,1,0), (2,2,0,1,0,0,-1,8,0),
        (0,1,0,4,1,0), (2,2,0,0,0,0,-1,-1,2), (1,0,1,5,3), (0,1,1,0,2), (0,0,0,1), (2,0,3,0,0,0,0,-1,1), (1,0,1,0,3),
        (2,2,2,1,1,0,-1,-1,-1), (2,3,1,0,0,0,11,5,2), (1,0,1,1,3), (0,0,0,0,1,0), (2,3,0,1,0,0,10,4,2), (0,1,1,5),
        (0,0,0,4,0,1), (1,0,1,3,3), (2,3,2,0,0,0,-1,-1,-1), (0,1,1,1,2,1), (1,0,1,4,3), (2,3,0,0,0,0,9,-1,2),
        (2,2,0,1,1,0,8,-1,2), (0,0,0,3,0), (2,3,3,0,0,0,13,-1,1), (2,0,2,0,0,0,-1,-1,-1), (0,1,1,4), (1,0,1,2,3),
        (1,1,1,3,3), (2,3,1,1,1,0,12,14,1), (0,0,1,0), (0,2,0,0,0), (1,1,1,0,3), (2,1,1,0,0,0,3,2,2), (1,1,1,5,3),
        (0,0,1,4,1), (1,1,1,1,3), (2,3,2,1,1,0,-1,-1,-1), (0,2,0,1,2,0), (0,0,1,3), (2,0,2,1,1,0,-1,-1,-1),
        (2,3,3,1,1,0,14,-1,1), (2,1,3,0,0,1,6,-1,3), (0,2,1,0,1), (2,1,1,1,0,1,4,5,0), (2,1,2,0,0,0,-1,-1,-1),
        (0,2,0,4,0), (0,2,1,1), (0,0,1,2,0), (2,1,3,1,1,0,7,-1,1), (0,2,0,2), (2,1,1,1,1,1,5,4,3), (1,1,1,2,3),
        (2,1,0,1,0,0,2,1,2), (0,2,1,3,0), (0,2,1,4,2,1), (1,1,1,4,3), (2,1,0,0,0,0,1,-1,2), (0,3,0,0), (0,0,0,2),
        (0,0,1,1), (2,1,2,1,1,0,-1,-1,-1), (0,3,0,5,0,2), (0,2,0,3), (0,1,1,2,1), (0,0,0,5,0), (0,3,1,5,1,2),
        (0,2,0,5,0), (0,3,1,1,0), (0,0,1,5,1), (0,3,0,2,0), (0,3,0,3), (0,2,1,5,2), (0,3,0,4,2), (0,3,1,3),
        (0,3,0,1), (0,1,1,3), (0,2,1,2), (0,3,1,2), (0,3,1,4), (0,3,1,0),
    ),
    (
        (1,0,0,5,1), (1,0,0,0,1), (1,0,0,1,1), (2,3,1,0,0,1,-1,11,3), (1,0,0,3,1), (2,3,1,1,0,1,-1,13,0),
        (2,3,0,1,0,1,-1,10,3), (1,0,0,4,1), (2,3,2,0,0,1,-1,-1,3), (2,3,2,1,0,1,-1,15,0), (2,3,3,1,0,1,-1,16,0),
        (2,3,0,0,0,1,-1,9,3), (2,3,3,0,0,1,-1,13,3), (1,0,0,2,1), (0,1,0,0,2,0), (2,2,1,0,0,0,10,-1,2),
        (2,1,3,1,0,1,8,9,0), (2,3,1,1,1,1,13,12,3), (0,2,0,5,2,0), (2,1,1,0,0,1,3,3,3), (2,2,1,1,0,0,11,3,2),
        (2,3,2,1,1,1,15,-1,3), (0,2,0,0,2,1), (1,1,1,5,1), (2,3,3,1,1,1,16,14,3), (2,2,3,0,0,0,-1,-1,-1),
        (0,2,0,1,1), (2,1,3,0,0,1,7,6,1), (2,2,3,1,0,0,12,-1,0), (0,1,1,0), (0,2,0,3,2,0), (2,1,2,0,0,1,5,-1,3),
        (0,1,0,4,2), (2,1,3,1,1,1,9,7,3), (0,2,0,4,1,2), (2,1,0,1,0,1,2,2,3), (2,0,3,0,0,0,-1,-1,-1), (0,2,1,5),
        (0,2,0,2,2,1), (2,1,0,0,0,1,1,1,3), (0,0,0,0,0), (2,2,3,1,1,0,-1,-1,-1), (0,3,0,3,2,0), (0,0,0,1), (0,0,0,4),
        (0,2,1,3,1,2), (0,3,0,0,2,1,0), (2,1,2,1,1,1,6,-1,3), (0,1,1,1), (0,0,1,0), (0,3,0,5,1),
        (2,0,3,1,0,0,0,-1,0), (2,3,3,0,0,0,-1,-1,-1), (0,3,1,3), (0,3,0,1,2,0), (0,0,1,1), (2,3,1,1,1,0,14,-1,2),
        (0,3,1,0), (2,1,3,0,0,0,-1,-1,-1), (0,0,0,2,0), (0,0,1,4), (2,0,3,1,1,0,-1,-1,-1), (2,1,1,1,1,0,4,-1,2),
        (0,0,0,5,1), (2,3,3,1,1,0,-1,-1,-1), (0,3,1,1,1), (0,3,0,2,2,1,0), (0,2,1,0), (0,1,0,5,0), (0,0,1,2),
        (0,3,0,4,0,1), (0,0,1,3,0), (2,1,3,1,1,0,-1,-1,-1), (0,3,1,2), (0,1,1,4), (0,2,1,4,2), (0,1,1,5),
        (0,1,1,3,1,0), (0,3,1,4,2,1), (0,1,1,2,0), (0,2,1,2), (0,0,0,3), (0,3,1,5,2), (0,0,1,5), (0,1,0,3),
        (0,2,1,1), (0,1,0,2), (0,1,0,1),
    ),
)


def flipped(index, bits, devices):
    total, unit = index, 1
    while unit < devices:
        if bits & unit:
            total = total + unit * (1 - 2 * lax.rem(index // unit, 2))
        unit *= 2
    return total


class Place:
    def __init__(self):
        self.part, self.row = lax.axis_index("parts"), lax.axis_index("row")
        self.col, self.core = lax.axis_index("col"), lax.axis_index("rhs")
        self.half = self.row // 2
        self.low = lax.rem(self.row, 2)
        self.shard = self.row * 2 + self.col
        self.group = self.low * 4 + self.part * 2 + self.col
        self.foreign = lax.rem(self.half + self.part, 2)
        self.inner = lax.rem(self.half + self.low, 2)

    def link(self, way):
        if way == 0:
            return {"col": 1 - self.col}
        if way == 1:
            return {"parts": 1 - self.part}
        if way == 2:
            return {"row": self.half * 2 + 1 - self.low}
        return {"row": 3 - self.row}

    def tile_row(self, kind):
        return (3 * self.half, 1 + self.half, 2 - self.half, 3 - 3 * self.half)[kind]

    def solver(self, group):
        return {
            "row": 2 * self.part + group // 4,
            "parts": lax.rem(group // 2, 2),
            "col": lax.rem(group, 2),
        }

    def owner(self, shard):
        return {"row": shard // 2, "parts": self.half, "col": lax.rem(shard, 2)}


def greet_all(place, sibling):
    barrier = pltpu.get_barrier_semaphore()
    me = place.part * 8 + place.shard
    for offset in range(1, 16):
        other = lax.rem(me + offset, 16)
        peer = {"parts": other // 8, "row": lax.rem(other, 8) // 2, "col": lax.rem(other, 2)}
        pl.semaphore_signal(barrier, inc=1, device_id=peer, device_id_type=MESH)
    if sibling:
        pl.semaphore_signal(barrier, inc=1, device_id={"rhs": 1 - place.core}, device_id_type=MESH)
    pl.semaphore_wait(barrier, 15 + sibling)


def solve_kernel(
    stored, target, names, diag,
    first_home, second_home, scales, transit, hold,
    tiles, parcel, field, start, terms, image, first, away_out, away_in, hot, names_v, names_s, diag_v, scale, norm,
    piece_send, piece_recv, pass_recv, hold_recv, send, recv, own_sem, pair_sem, home_send, home_recv, home_own,
):
    place = Place()
    shard, core, foreign = place.shard, place.core, place.foreign
    half = tiles.shape[1]
    size = half // PIECES
    blocks, both, width = field.shape
    own = both // 2
    quarter = blocks // 8
    step_blocks = 16
    steps = blocks // step_blocks
    rows = hot.shape[1]
    fetch = pltpu.make_async_copy(target, first, own_sem.at[4])
    fetch.start()
    greet_all(place, 1)

    def part_of(k):
        return pl.ds(k * size, size)

    def mine(s):
        return field.at[pl.ds(s * quarter, quarter), pl.ds(0, own)]

    def piece_copy(source, target, way, send_sem, recv_sem):
        return pltpu.make_async_remote_copy(
            src_ref=source, dst_ref=target, send_sem=send_sem, recv_sem=recv_sem,
            device_id=place.link(way), device_id_type=MESH,
        )

    def source_shard(entry):
        solved = place.half if entry[5] == 0 else 1 - place.half
        row = (3 * solved, 3 - 3 * solved, 1 + solved, 2 - solved)[entry[1]]
        return row * 2 + (1 - place.col if entry[4] else place.col)

    def dest_group(entry):
        low = lax.rem(entry[2] // 2 + place.part, 2)
        part = 1 - place.part if entry[2] % 2 else place.part
        return low * 4 + part * 2 + (1 - place.col if entry[3] else place.col)

    def step(kind, entry, count):
        if entry[0] == 2:
            slot_in, slot_out, way = entry[6:]
            if entry[4] == 0 and slot_in < 0 and way >= 0:
                source = parcel.at[dest_group(entry)]
            elif way < 0:
                s = source_shard(entry)
                piece_copy(mine(s), mine(s), 0, piece_send.at[0], recv.at[2, s]).wait_recv()
                return count
            else:
                source = hold.at[slot_in]
                piece_copy(source, source, 0, piece_send.at[0], hold_recv.at[slot_in]).wait_recv()
            if slot_out < 0:
                s = source_shard(entry)
                target, sem = mine(s), recv.at[2, s]
            else:
                target, sem = hold.at[slot_out], hold_recv.at[slot_out]
            piece_copy(source, target, way, piece_send.at[count], sem).start()
            return count + 1
        k = entry[3]
        if entry[0] == 0:
            s = place.tile_row(entry[1]) * 2 + (1 - place.col if entry[2] else place.col)
            here = kind in (0, 2) and entry[1] == kind // 2 and entry[2] == 0
            source, sem = tiles.at[s, part_of(k)], piece_recv.at[s, k]
        else:
            s = place.tile_row(1 - entry[1]) * 2 + place.col
            here = entry[2] == 0
            source, sem = transit.at[entry[1], part_of(k)], pass_recv.at[entry[1], k]
        if here:
            source = stored.at[part_of(k), core]
        else:
            piece_copy(source, source, 0, piece_send.at[0], sem).wait_recv()
        for way in entry[4:]:
            if entry[0] == 0 or way == 3:
                target, sem = tiles.at[s, part_of(k)], piece_recv.at[s, k]
            else:
                target, sem = transit.at[entry[1], part_of(k)], pass_recv.at[entry[1], k]
            piece_copy(source, target, way, piece_send.at[count], sem).start()
            count += 1
        return count

    def sends(entry):
        return int(entry[8] >= 0) if entry[0] == 2 else len(entry) - 4

    def each_class(body):
        for kind in range(4):
            @pl.when((foreign == kind % 2) & (place.inner == kind // 2))
            def _(kind=kind):
                entries = ROUTES[kind]
                begin = [entry[0] for entry in entries].index(2)
                body(kind, entries, begin)

    def before_pack(kind, entries, begin):
        count = 0
        for entry in entries[:begin]:
            count = step(kind, entry, count)

    def sent(kind, entries, begin):
        count = 0
        for entry in entries:
            for _ in range(sends(entry)):
                block = parcel.at[0] if entry[0] == 2 else stored.at[part_of(0), core]
                piece_copy(block, block, 0, piece_send.at[count], piece_recv.at[shard, 0]).wait_send()
                count += 1

    each_class(before_pack)
    fetch.wait()

    def pack(n, carry):
        for u in range(4):
            b = n * 4 + u
            low = first[pl.ds(b * width, width)].astype(jnp.bfloat16).T
            parcel[:, b] = low.reshape(8, own, width)
        return carry

    lax.fori_loop(0, quarter // 4, pack, 0)
    side = quarter // 2

    def straight(n, bits, c=0):
        group = flipped(place.group, bits, 8)
        rows_of = pl.ds(c * side, side)
        return pltpu.make_async_remote_copy(
            src_ref=diag.at[rows_of] if n else names,
            dst_ref=diag_v.at[shard, rows_of] if n else names_v.at[shard],
            send_sem=send.at[n, bits],
            recv_sem=recv.at[n, shard],
            device_id=place.solver(group),
            device_id_type=MESH,
        )

    def arrival(n, bits, c=0):
        other = flipped(shard, bits, 8)
        landed = diag_v.at[other, pl.ds(c * side, side)] if n else names_v.at[other]
        return pltpu.make_async_remote_copy(
            src_ref=landed, dst_ref=landed, send_sem=send.at[n, 0],
            recv_sem=recv.at[n, other],
            device_id=place.link(0), device_id_type=MESH,
        )

    def each_core(body):
        for c in range(2):
            @pl.when(core == c)
            def _(c=c):
                body(c)

    def small_sends(first_bits, c):
        for bits in range(first_bits, 8):
            straight(0, bits).start()
            straight(1, bits, c).start()

    def small_arrivals(first_bits, c):
        for bits in range(first_bits, 8):
            for n in range(2):
                arrival(n, bits, c).wait_recv()
                straight(n, bits, c).wait_send()

    def local(n, c=0):
        rows_of = pl.ds(c * side, side)
        source, landed = (
            (names, names_v.at[shard]),
            (diag.at[rows_of], diag_v.at[shard, rows_of]),
            (parcel.at[place.group], mine(shard)),
            (stored.at[:, core], tiles.at[shard]),
        )[n]
        return pltpu.make_async_copy(source, landed, own_sem.at[n])

    @pl.when(foreign == 1)
    def _():
        each_core(lambda c: small_sends(0, c))

    @pl.when(foreign == 0)
    def _():
        each_core(lambda c: small_sends(1, c))
        each_core(lambda c: local(1, c).start())
        for n in (0, 2, 3):
            local(n).start()

    @pl.when(foreign == 1)
    def _():
        each_core(lambda c: small_arrivals(0, c))

    @pl.when(foreign == 0)
    def _():
        each_core(lambda c: small_arrivals(1, c))
        each_core(lambda c: local(1, c).wait())
        for n in (0, 2, 3):
            local(n).wait()

    read = pltpu.make_async_copy(names_v, names_s, own_sem.at[4])
    read.start()

    taken = 2 * half
    lane = lax.broadcasted_iota(jnp.int32, names_v.shape[1:], 1)
    at = lax.broadcasted_iota(jnp.int32, (blocks, LANES), 0)
    for q in range(rows // LANES):
        s, skip = q * LANES // taken, q * LANES % taken
        here = pltpu.roll(names_v[s], (LANES - skip) % LANES, 1)
        next = pltpu.roll(names_v[s + 1], taken - skip, 1)
        row = jnp.where(lane < taken - skip, here, next)[0:1]
        hot[:, q * LANES : (q + 1) * LANES] = jnp.where(at == row, 1.0, 0.0).astype(jnp.bfloat16)

    read.wait()
    def swap(n, source, landed):
        return pltpu.make_async_remote_copy(
            src_ref=source, dst_ref=landed, send_sem=pair_sem.at[n, 0], recv_sem=pair_sem.at[n, 1],
            device_id={"rhs": 1 - core}, device_id_type=MESH,
        )

    ours, theirs = field.at[:, pl.ds(0, own)], field.at[:, pl.ds(own, own)]
    pair = swap(0, ours, theirs)

    def diag_pair(c):
        rows_of = pl.ds(c * side, side)
        return swap(4, diag_v.at[:, rows_of], diag_v.at[:, rows_of])
    zero = jnp.zeros((own, width), jnp.float32)

    def chunk(ref, n):
        return ref[pl.ds(n * step_blocks, step_blocks)]

    def keep(n, total):
        low = field[pl.ds(n * step_blocks, step_blocks), 0:own]
        start[pl.ds(n * step_blocks, step_blocks)] = low
        value = low.astype(jnp.float32)
        return total + jnp.sum(value * value, axis=0)

    def keep_start():
        norm[...] = lax.fori_loop(0, steps, keep, zero)

    def product(s, k):
        results = []
        for u in range(size):
            slot = k * size + u
            i, j = names_s[s, 0, slot], names_s[s, 0, half + slot]
            block = tiles[s, slot]
            direct = lax.dot_general(
                field[j], block, (((1,), (1,)), ((), ())), preferred_element_type=jnp.float32
            )
            mirrored = lax.dot_general(
                field[i], block, (((1,), (0,)), ((), ())), preferred_element_type=jnp.float32
            )
            results.append((slot, slot < names_s[s, 1, 0], direct, mirrored))
        for slot, used, direct, mirrored in results:
            at = s * taken + slot
            terms[pl.ds(at, both, stride=rows)] = jnp.where(used, direct, 0.0)
            terms[pl.ds(at + half, both, stride=rows)] = jnp.where(used, mirrored, 0.0)

    def products(n, carry):
        product(n // PIECES, lax.rem(n, PIECES))
        return carry

    def product_pair(row, k):
        def one(col, carry):
            product(place.tile_row(row) * 2 + col, k)
            return carry

        lax.fori_loop(0, 2, one, 0)

    def diag_swapped(c):
        diag_pair(c).wait_send()
        diag_pair(1 - c).wait_recv()

    def after_pack(kind, entries, begin):
        count = sum(sends(entry) for entry in entries[:begin])
        ready = max(n for n, entry in enumerate(entries) if entry[0] == 2 and entry[8] < 0)
        landed, due = set(), []
        for n, entry in enumerate(entries):
            if n >= begin:
                count = step(kind, entry, count)
            if entry[0] == 0:
                landed.add(entry[1:4])
                if (entry[1], 1 - entry[2], entry[3]) in landed:
                    due.append((entry[1], entry[3]))
            if n == ready:
                pair.start()
                each_core(lambda c: diag_pair(c).start())
            if n == min(ready + 1, len(entries) - 1):
                keep_start()
            if n == min(ready + 2, len(entries) - 1):
                pair.wait()
                each_core(diag_swapped)
            if n >= ready + 2:
                for _ in range(-(-len(due) // (len(entries) - n))):
                    product_pair(*due.pop(0))
        for one in due:
            product_pair(*one)

    each_class(after_pack)
    each_class(sent)

    def gather_sums(n, carry):
        c = 2 * n
        pair = [terms[pl.ds((c + m) * rows, rows)].astype(jnp.bfloat16) for m in range(2)]
        total = jnp.dot(
            hot[...], jnp.concatenate(pair, axis=1), preferred_element_type=jnp.float32
        )
        for m in range(2):
            image[pl.ds(c + m, blocks, stride=both)] = total[:, m * width : (m + 1) * width]
        return carry

    def image_chunk(n):
        return image[pl.ds(n * step_blocks * both, step_blocks * both)].reshape(step_blocks, both, width)

    def first_chunk(n):
        return first[pl.ds(n * step_blocks * own, step_blocks * own)].reshape(step_blocks, own, width)

    def start_chunk(n):
        return chunk(start, n).astype(jnp.float32)

    def diag_chunk(n):
        per = quarter // step_blocks
        return diag_v[n // per, pl.ds(lax.rem(n, per) * step_blocks, step_blocks)][:, None, :]

    def operate(exchange, direction_chunk):
        lax.fori_loop(own // 2, own, gather_sums, 0)

        def away(n, carry):
            away_out[pl.ds(n * step_blocks, step_blocks)] = image_chunk(n)[:, own:].astype(jnp.bfloat16)
            return carry

        lax.fori_loop(0, steps, away, 0)
        over = swap(exchange, away_out, away_in)
        over.start()
        lax.fori_loop(0, own // 2, gather_sums, 0)
        over.wait()

        def join(n, total):
            direction = direction_chunk(n)
            value = image_chunk(n)[:, :own] + chunk(away_in, n).astype(jnp.float32)
            value = value + diag_chunk(n) * direction
            image[pl.ds(n * step_blocks * own, step_blocks * own)] = value.reshape(step_blocks * own, width)
            return total + jnp.sum(value * direction, axis=0)

        return jnp.sum(lax.fori_loop(0, steps, join, zero), axis=1, keepdims=True)

    def joined_chunk(n):
        return image[pl.ds(n * step_blocks * own, step_blocks * own)].reshape(step_blocks, own, width)

    home = ((scale, scales), (parcel, first_home), (away_out, second_home))

    def leaving(n, to):
        if n == 0:
            return scale
        return parcel.at[to] if n == 1 else away_out.at[pl.ds(to * quarter, quarter)]

    def home_copy(n, bits):
        to = flipped(shard, bits, 8)
        return pltpu.make_async_remote_copy(
            src_ref=leaving(n, to),
            dst_ref=home[n][1].at[place.group],
            send_sem=home_send.at[n, bits],
            recv_sem=home_recv.at[n, place.group],
            device_id=place.owner(to),
            device_id_type=MESH,
        )

    def home_arrival(n, bits):
        landed = home[n][1].at[flipped(place.group, bits, 8)]
        return pltpu.make_async_remote_copy(
            src_ref=landed, dst_ref=landed, send_sem=home_send.at[n, 0],
            recv_sem=home_recv.at[n, flipped(place.group, bits, 8)],
            device_id=place.link(0), device_id_type=MESH,
        )

    def home_local(n):
        return pltpu.make_async_copy(leaving(n, shard), home[n][1].at[place.group], home_own.at[n])

    def go_home(n):
        for bits in range(7, 0, -1):
            home_copy(n, bits).start()

        @pl.when(foreign == 1)
        def _():
            home_copy(n, 0).start()

        @pl.when(foreign == 0)
        def _():
            home_local(n).start()

    def arrive_home(n):
        for bits in range(1, 8):
            home_copy(n, bits).wait_send()
            home_arrival(n, bits).wait_recv()

        @pl.when(foreign == 1)
        def _():
            home_copy(n, 0).wait_send()
            home_arrival(n, 0).wait_recv()

        @pl.when(foreign == 0)
        def _():
            home_local(n).wait()

    per = quarter // step_blocks
    norm0 = jnp.sum(norm[...], axis=1, keepdims=True)
    alpha1 = norm0 / operate(1, start_chunk)

    def next_first(n, total):
        value = start_chunk(n) - alpha1[None] * joined_chunk(n)
        first[pl.ds(n * step_blocks * own, step_blocks * own)] = value.reshape(step_blocks * own, width)
        parcel[n // per, pl.ds(lax.rem(n, per) * step_blocks, step_blocks)] = value.astype(jnp.bfloat16)
        return total + jnp.sum(value * value, axis=0)

    norm1 = jnp.sum(lax.fori_loop(0, steps, next_first, zero), axis=1, keepdims=True)
    go_home(1)
    beta = norm1 / norm0

    def direction_chunk(n):
        return first_chunk(n) + beta[None] * start_chunk(n)

    def next_low(n, carry):
        field[pl.ds(n * step_blocks, step_blocks), 0:own] = direction_chunk(n).astype(jnp.bfloat16)
        return carry

    lax.fori_loop(0, steps, next_low, 0)
    pair = swap(2, ours, theirs)
    pair.start()
    pair.wait()
    lax.fori_loop(0, 8 * PIECES, products, 0)
    alpha2 = norm1 / operate(3, direction_chunk)

    def last(n, carry):
        value = first_chunk(n) - alpha2[None] * joined_chunk(n)
        away_out[pl.ds(n * step_blocks, step_blocks)] = value.astype(jnp.bfloat16)
        return carry

    lax.fori_loop(0, steps, last, 0)
    go_home(2)
    for n, value in enumerate((alpha1, alpha2, beta)):
        scale[n] = jnp.broadcast_to(value, (own, width))
    go_home(0)
    for n in (1, 2, 0):
        arrive_home(n)


def solve(stored, target, names, diag):
    half, cores, width, _ = stored.shape
    quarter, columns = target.shape[0] // width, target.shape[1]
    own = columns // 8
    parcel = (8, quarter, own, width)
    blocks, both, rows = 8 * quarter, 2 * own, 16 * half
    sends = max(
        sum(int(e[8] >= 0) if e[0] == 2 else len(e) - 4 for e in entries) for entries in ROUTES
    )
    dma = pltpu.SemaphoreType.DMA
    return pl.pallas_call(
        solve_kernel,
        out_shape=(
            jax.ShapeDtypeStruct(parcel, jnp.bfloat16),
            jax.ShapeDtypeStruct(parcel, jnp.bfloat16),
            jax.ShapeDtypeStruct((8, 3, own, width), jnp.float32),
            jax.ShapeDtypeStruct((2, half, width, width), stored.dtype),
            jax.ShapeDtypeStruct((HOLD,) + parcel[1:], jnp.bfloat16),
        ),
        in_specs=[ANY] * 4,
        out_specs=[ANY] * 5,
        scratch_shapes=[
            pltpu.VMEM((8, half, width, width), stored.dtype),
            pltpu.VMEM(parcel, jnp.bfloat16),
            pltpu.VMEM((blocks, both, width), jnp.bfloat16),
            pltpu.VMEM((blocks, own, width), jnp.bfloat16),
            pltpu.VMEM((both * rows + rows, width), jnp.float32),
            pltpu.VMEM((blocks * both, width), jnp.float32),
            pltpu.VMEM((blocks * own, width), jnp.float32),
            pltpu.VMEM((blocks, own, width), jnp.bfloat16),
            pltpu.VMEM((blocks, own, width), jnp.bfloat16),
            pltpu.VMEM((blocks, rows), jnp.bfloat16),
            pltpu.VMEM((8,) + names.shape, names.dtype),
            pltpu.SMEM((8,) + names.shape, names.dtype),
            pltpu.VMEM((8,) + diag.shape, diag.dtype),
            pltpu.VMEM((3, own, width), jnp.float32),
            pltpu.VMEM((own, width), jnp.float32),
            dma((sends,)),
            dma((8, PIECES)),
            dma((2, PIECES)),
            dma((HOLD,)),
            dma((2, 8)),
            dma((3, 8)),
            dma((5,)),
            dma((5, 2)),
            dma((3, 8)),
            dma((3, 8)),
            dma((3,)),
        ],
        compiler_params=pltpu.CompilerParams(
            collective_id=0, has_side_effects=True, vmem_limit_bytes=60 * 2**20
        ),
    )(stored, target, names, diag)[:3]


def finish_kernel(target_ref, diag_ref, first_ref, second_ref, scale_ref, answer_ref, residual_ref, scale_rows):
    blocks, width, columns = target_ref.shape

    @pl.when(pl.program_id(0) == 0)
    def _():
        for n in range(3):
            scale_rows[n] = scale_ref[:, n].reshape(columns, width).T[0:8]

    alpha1, alpha2, beta = scale_rows[0, 0:1], scale_rows[1, 0:1], scale_rows[2, 0:1]
    diags = diag_ref[...].T
    same = lax.broadcasted_iota(jnp.int32, (width, columns), 0) == lax.broadcasted_iota(
        jnp.int32, (width, columns), 1
    )
    unit = jnp.where(same, 1.0, 0.0).astype(jnp.bfloat16)

    def turned(value):
        return lax.dot_general(
            unit, value.reshape(columns, width), (((1,), (1,)), ((), ())), preferred_element_type=jnp.float32
        )

    for b in range(blocks):
        target = target_ref[b]
        diag = diags[:, b : b + 1]
        first, second = turned(first_ref[:, b]), turned(second_ref[:, b])
        lost = target - target.astype(jnp.bfloat16).astype(jnp.float32)
        lost1 = lost - alpha1 * diag * lost
        answer_ref[b] = alpha1 * target + alpha2 * (first + lost1 + beta * target)
        residual_ref[b] = second + lost1 - alpha2 * diag * (lost1 + beta * lost)


def finish(target, diag, first, second, scales):
    blocks, width, columns = target.shape
    devices, _, own, _ = second.shape
    step = 16
    whole = pl.BlockSpec((step, width, columns), lambda g: (g, 0, 0))
    part = pl.BlockSpec((devices, step, own, width), lambda g: (0, g, 0, 0))
    return pl.pallas_call(
        finish_kernel,
        out_shape=(jax.ShapeDtypeStruct(target.shape, jnp.float32),) * 2,
        grid=(blocks // step,),
        in_specs=[
            whole,
            pl.BlockSpec((step, width), lambda g: (g, 0)),
            part,
            part,
            pl.BlockSpec(scales.shape, lambda g: (0, 0, 0, 0)),
        ],
        out_specs=(whole, whole),
        scratch_shapes=[pltpu.VMEM((3, 8, columns), jnp.float32)],
        compiler_params=pltpu.CompilerParams(vmem_limit_bytes=40 * 2**20),
    )(target, diag, first, second, scales)


def by_columns(blocks, block_rows, block_cols, counts, diagonal, target):
    nrow, ncol = lax.axis_size("row"), lax.axis_size("col")
    devices = nrow * ncol
    stored = blocks[0, 0]
    slots, width, _ = stored.shape
    quarter = target.shape[0] // width
    row_blocks = ncol * quarter
    half = slots // 2
    row, col, core = lax.axis_index("row"), lax.axis_index("col"), lax.axis_index("rhs")

    irow = row * row_blocks + block_rows[0, 0]
    jcol = block_cols[0, 0]
    icol = (jcol // quarter * ncol + col) * quarter + jcol % quarter

    def every_other(index):
        return jnp.where(core == 0, index[0::2], index[1::2])

    used = (counts[0] - core + 1) // 2
    gap = jnp.zeros((LANES - 2 * half,), jnp.int32)
    slots = jnp.concatenate([every_other(irow), every_other(icol), gap])
    names = jnp.stack([slots, jnp.broadcast_to(used, (LANES,))])
    names = jnp.pad(names, ((0, 6), (0, 0)))
    diag_own = diagonal.reshape(quarter, width)
    target_blocks = target.reshape(quarter, width, target.shape[1])
    first_home, second_home, scales = solve(
        stored.reshape(half, 2, width, width), target, names, diag_own
    )
    answer, residual = finish(target_blocks, diag_own, first_home, second_home, scales)
    return (answer.reshape(target.shape), residual.reshape(target.shape))


def one_hot_slots(indices, valid, extent):
    return ((indices[None, :] == jnp.arange(extent)[:, None]) & valid[None, :]).astype(jnp.float32)


def picked(blocks, index):
    return lax.map(lambda i: lax.dynamic_index_in_dim(blocks, i, 0, keepdims=False), index)


def on_device(blocks, block_rows, block_cols, counts, diagonal, target):
    highest = lax.Precision.HIGHEST
    nrow = lax.axis_size("row")
    ncol = lax.axis_size("col")
    if (
        (lax.axis_size("parts"), nrow, ncol, lax.axis_size("rhs")) == (2, 4, 2, 2)
        and target.shape[1] == 128
        and blocks.shape[2] % (16 * PIECES) == 0
        and target.shape[0] // blocks.shape[3] % 64 == 0
    ):
        return by_columns(blocks, block_rows, block_cols, counts, diagonal, target)
    stored = blocks[0, 0]
    slots = stored.shape[0]
    width = stored.shape[1]
    local = target.shape[0]
    ncols = target.shape[1]
    quarter = local // width
    row_blocks = ncol * quarter
    col_blocks = nrow * quarter
    valid = jnp.arange(slots) < counts[0, 0]
    rows_hot = one_hot_slots(block_rows[0, 0], valid, row_blocks)
    cols_hot = one_hot_slots(block_cols[0, 0], valid, col_blocks)

    def squares(vector):
        return lax.psum(jnp.sum(vector * vector, axis=0), ("row", "col"))

    solution = jnp.zeros_like(target)
    residual = target
    direction = target
    norm_now = squares(residual)
    for step in range(ITERS):
        operate_field_low = direction.astype(jnp.bfloat16)
        direct_gathered = lax.all_gather(operate_field_low, "row", axis=0, tiled=True).reshape(
            col_blocks, width, ncols
        )
        prod = jnp.einsum(
            "kab,kbc->kac",
            stored,
            picked(direct_gathered, block_cols[0, 0]),
            preferred_element_type=jnp.float32,
        )
        direct_partial_value = jnp.einsum("ik,kac->iac", rows_hot, prod, precision=highest)
        direct = lax.psum_scatter(
            direct_partial_value.reshape(row_blocks * width, ncols).astype(jnp.bfloat16),
            "col",
            scatter_dimension=0,
            tiled=True,
        ).astype(jnp.float32)
        gathered = lax.all_gather(operate_field_low, "col", axis=0, tiled=True).reshape(
            row_blocks, width, ncols
        )
        tprod = jnp.einsum(
            "kba,kbc->kac",
            stored,
            picked(gathered, block_rows[0, 0]),
            preferred_element_type=jnp.float32,
        )
        partial_value = jnp.einsum("jk,kac->jac", cols_hot, tprod, precision=highest)
        parcel = partial_value.astype(jnp.bfloat16).reshape(nrow, local, ncols)
        mirrored = jnp.sum(
            lax.all_to_all(parcel, "row", split_axis=0, concat_axis=0, tiled=True).astype(
                jnp.float32
            ),
            axis=0,
        )
        image = diagonal[:, None] * direction + direct + mirrored
        curve = lax.psum(jnp.sum(direction * image, axis=0), ("row", "col"))
        alpha = norm_now / curve
        solution = solution + alpha * direction
        residual = residual - alpha * image
        if step + 1 < ITERS:
            norm_next = squares(residual)
            direction = residual + norm_next / norm_now * direction
            norm_now = norm_next
    return (solution, residual)


def solution(mesh):
    return jax.shard_map(
        on_device,
        mesh=mesh,
        in_specs=(
            P(("parts", "row"), "col", None, None, None),
            P(("parts", "row"), "col", None),
            P(("parts", "row"), "col", None),
            P(("parts", "row"), "col"),
            P(("parts", "row", "col")),
            P(("parts", "row", "col"), "rhs"),
        ),
        out_specs=(P(("parts", "row", "col"), "rhs"), P(("parts", "row", "col"), "rhs")),
        check_vma=False,
    )
```

```python
import functools
import jax
import jax.numpy as jnp
from jax import lax
from jax.experimental import pallas as pl
from jax.experimental.pallas import tpu as pltpu
from jax.sharding import PartitionSpec as P

ITERS = 2
LANES = 128
PIECES = 6
MESH = pl.DeviceIdType.MESH
ANY = pl.BlockSpec(memory_space=pl.ANY)


HOLD = 17
ROUTES = (
    (
        (0,0,0,1,1,2), (2,0,1,1,0,0,-1,0,1), (2,0,3,0,0,0,-1,0,2), (2,0,3,1,0,0,-1,1,1), (0,0,0,0,0,2),
        (0,0,0,4,2,1,0), (2,0,2,1,0,0,-1,0,0), (0,0,0,2,0,1), (0,0,0,5,1), (2,0,1,0,0,0,-1,-1,1),
        (2,0,0,1,0,0,-1,-1,0), (0,0,0,3,1,2), (2,0,2,0,0,0,-1,-1,2), (0,1,0,0), (1,1,1,3,2), (0,1,0,3,1,0),
        (1,1,1,0,2), (0,0,1,0,1), (1,1,1,1,2), (0,0,1,4), (0,1,0,2,0), (2,0,2,1,1,0,0,-1,2), (2,1,1,1,0,1,3,4,2),
        (0,1,0,5,1,0), (0,0,1,2,2,1), (1,1,1,2,2), (2,2,0,0,0,0,-1,-1,-1), (2,0,0,1,1,0,-1,-1,-1), (1,1,1,4,2),
        (0,1,1,0), (0,1,1,3), (2,3,1,0,0,0,5,-1,1), (0,0,1,1,2), (0,1,1,2,2,1), (2,3,0,1,0,0,4,-1,0), (0,2,0,5,2),
        (0,1,1,5), (0,1,1,1,1,0), (0,2,0,3,0), (2,3,0,0,0,0,-1,-1,-1), (2,3,0,1,1,0,-1,-1,-1), (0,1,0,4,0),
        (2,2,0,1,1,0,-1,-1,-1), (0,1,0,1), (0,0,1,5), (2,1,1,0,0,0,2,-1,1), (0,2,1,3), (0,2,1,0,0), (0,2,0,1,0,1),
        (0,1,1,4), (0,2,0,2), (0,0,1,3), (0,2,0,0), (2,1,0,1,0,0,1,-1,0), (0,3,0,3,0,2), (0,2,1,1,1), (0,2,1,4,0),
        (0,3,0,0,0), (2,1,0,1,1,0,-1,-1,-1), (2,1,0,0,0,0,-1,-1,-1), (0,3,0,1,0), (0,3,1,3,1,2), (0,3,0,5,1),
        (0,2,1,2,2), (0,2,0,4), (0,3,1,5), (0,3,1,0,1,2), (0,3,0,2,0), (0,2,1,5), (0,3,1,1), (0,3,0,4), (0,3,1,4),
        (0,3,1,2),
    ),
    (
        (1,1,0,3,1), (2,1,3,1,0,1,-1,8,2), (2,1,1,0,0,1,-1,3,2), (1,1,0,0,1), (1,1,0,5,2), (1,1,0,1,1),
        (2,1,3,0,0,1,-1,7,2), (2,1,2,0,0,1,-1,5,2), (2,1,0,1,0,1,-1,2,2), (2,1,1,1,0,1,-1,3,1), (2,1,2,1,0,1,-1,2,0),
        (2,1,0,0,0,1,-1,1,2), (1,1,0,2,1), (1,1,0,4,1), (0,0,0,1,0,2), (2,0,1,1,0,0,0,-1,0), (2,1,2,1,1,1,2,6,2),
        (0,1,0,0,0), (2,0,3,1,0,0,1,0,2), (0,0,1,1,1,2), (2,2,1,0,0,0,-1,-1,-1), (0,0,0,4,0), (2,0,1,1,1,0,-1,-1,-1),
        (0,2,0,5,1,0), (0,0,0,2,2), (0,1,1,0), (2,2,1,1,0,0,3,-1,0), (0,0,0,5,2,0), (0,0,1,4), (0,2,0,0,0),
        (2,0,1,0,0,0,-1,-1,-1), (0,2,1,5), (0,2,0,3,1), (0,0,0,3,0), (2,2,1,1,1,0,-1,-1,-1), (0,1,0,4,1,0),
        (0,1,0,3,0), (0,0,1,5,1), (0,2,0,4), (0,0,1,0,0), (0,2,1,0,1), (0,2,0,2,0,1), (0,1,0,5,2,0), (0,0,1,3,2,1),
        (0,3,0,3,1), (0,0,1,2), (0,1,1,4,2), (0,2,1,3), (2,3,1,0,0,0,-1,-1,-1), (0,1,1,3,2), (0,3,0,0,1),
        (0,1,1,2,0), (0,0,0,0), (0,3,0,1,1,0), (0,1,1,1,0), (0,2,1,2,1,2), (2,3,1,1,1,0,-1,-1,-1), (0,1,1,5),
        (2,1,1,0,0,0,-1,-1,-1), (2,1,1,1,1,0,-1,-1,-1), (0,2,0,1), (0,1,0,2), (0,3,0,2,1,0), (0,3,1,1), (0,2,1,1,2),
        (0,2,1,4), (0,1,0,1,2), (0,3,1,3), (0,3,1,4,1,0), (0,3,1,2), (0,3,0,5), (0,3,1,5), (0,3,1,0), (0,3,0,4),
    ),
    (
        (0,1,0,0,1,0,2), (2,2,1,0,0,0,-1,10,1), (0,1,0,3,2), (2,2,2,1,0,0,-1,-1,0), (2,2,1,1,0,0,-1,11,1),
        (0,1,0,2,2), (2,2,3,0,0,0,-1,-1,1), (0,1,0,5,2,0), (2,2,3,1,0,0,-1,12,1), (0,1,0,1,0), (2,2,0,1,0,0,-1,8,0),
        (0,1,0,4,1,0), (2,2,0,0,0,0,-1,-1,2), (1,0,1,5,3), (0,1,1,0,2), (0,0,0,1), (2,0,3,0,0,0,0,-1,1), (1,0,1,0,3),
        (2,2,2,1,1,0,-1,-1,-1), (2,3,1,0,0,0,11,5,2), (1,0,1,1,3), (0,0,0,0,1,0), (2,3,0,1,0,0,10,4,2), (0,1,1,5),
        (0,0,0,4,0,1), (1,0,1,3,3), (2,3,2,0,0,0,-1,-1,-1), (0,1,1,1,2,1), (1,0,1,4,3), (2,3,0,0,0,0,9,-1,2),
        (2,2,0,1,1,0,8,-1,2), (0,0,0,3,0), (2,3,3,0,0,0,13,-1,1), (2,0,2,0,0,0,-1,-1,-1), (0,1,1,4), (1,0,1,2,3),
        (1,1,1,3,3), (2,3,1,1,1,0,12,14,1), (0,0,1,0), (0,2,0,0,0), (1,1,1,0,3), (2,1,1,0,0,0,3,2,2), (1,1,1,5,3),
        (0,0,1,4,1), (1,1,1,1,3), (2,3,2,1,1,0,-1,-1,-1), (0,2,0,1,2,0), (0,0,1,3), (2,0,2,1,1,0,-1,-1,-1),
        (2,3,3,1,1,0,14,-1,1), (2,1,3,0,0,1,6,-1,3), (0,2,1,0,1), (2,1,1,1,0,1,4,5,0), (2,1,2,0,0,0,-1,-1,-1),
        (0,2,0,4,0), (0,2,1,1), (0,0,1,2,0), (2,1,3,1,1,0,7,-1,1), (0,2,0,2), (2,1,1,1,1,1,5,4,3), (1,1,1,2,3),
        (2,1,0,1,0,0,2,1,2), (0,2,1,3,0), (0,2,1,4,2,1), (1,1,1,4,3), (2,1,0,0,0,0,1,-1,2), (0,3,0,0), (0,0,0,2),
        (0,0,1,1), (2,1,2,1,1,0,-1,-1,-1), (0,3,0,5,0,2), (0,2,0,3), (0,1,1,2,1), (0,0,0,5,0), (0,3,1,5,1,2),
        (0,2,0,5,0), (0,3,1,1,0), (0,0,1,5,1), (0,3,0,2,0), (0,3,0,3), (0,2,1,5,2), (0,3,0,4,2), (0,3,1,3),
        (0,3,0,1), (0,1,1,3), (0,2,1,2), (0,3,1,2), (0,3,1,4), (0,3,1,0),
    ),
    (
        (1,0,0,5,1), (1,0,0,0,1), (1,0,0,1,1), (2,3,1,0,0,1,-1,11,3), (1,0,0,3,1), (2,3,1,1,0,1,-1,13,0),
        (2,3,0,1,0,1,-1,10,3), (1,0,0,4,1), (2,3,2,0,0,1,-1,-1,3), (2,3,2,1,0,1,-1,15,0), (2,3,3,1,0,1,-1,16,0),
        (2,3,0,0,0,1,-1,9,3), (2,3,3,0,0,1,-1,13,3), (1,0,0,2,1), (0,1,0,0,2,0), (2,2,1,0,0,0,10,-1,2),
        (2,1,3,1,0,1,8,9,0), (2,3,1,1,1,1,13,12,3), (0,2,0,5,2,0), (2,1,1,0,0,1,3,3,3), (2,2,1,1,0,0,11,3,2),
        (2,3,2,1,1,1,15,-1,3), (0,2,0,0,2,1), (1,1,1,5,1), (2,3,3,1,1,1,16,14,3), (2,2,3,0,0,0,-1,-1,-1),
        (0,2,0,1,1), (2,1,3,0,0,1,7,6,1), (2,2,3,1,0,0,12,-1,0), (0,1,1,0), (0,2,0,3,2,0), (2,1,2,0,0,1,5,-1,3),
        (0,1,0,4,2), (2,1,3,1,1,1,9,7,3), (0,2,0,4,1,2), (2,1,0,1,0,1,2,2,3), (2,0,3,0,0,0,-1,-1,-1), (0,2,1,5),
        (0,2,0,2,2,1), (2,1,0,0,0,1,1,1,3), (0,0,0,0,0), (2,2,3,1,1,0,-1,-1,-1), (0,3,0,3,2,0), (0,0,0,1), (0,0,0,4),
        (0,2,1,3,1,2), (0,3,0,0,2,1,0), (2,1,2,1,1,1,6,-1,3), (0,1,1,1), (0,0,1,0), (0,3,0,5,1),
        (2,0,3,1,0,0,0,-1,0), (2,3,3,0,0,0,-1,-1,-1), (0,3,1,3), (0,3,0,1,2,0), (0,0,1,1), (2,3,1,1,1,0,14,-1,2),
        (0,3,1,0), (2,1,3,0,0,0,-1,-1,-1), (0,0,0,2,0), (0,0,1,4), (2,0,3,1,1,0,-1,-1,-1), (2,1,1,1,1,0,4,-1,2),
        (0,0,0,5,1), (2,3,3,1,1,0,-1,-1,-1), (0,3,1,1,1), (0,3,0,2,2,1,0), (0,2,1,0), (0,1,0,5,0), (0,0,1,2),
        (0,3,0,4,0,1), (0,0,1,3,0), (2,1,3,1,1,0,-1,-1,-1), (0,3,1,2), (0,1,1,4), (0,2,1,4,2), (0,1,1,5),
        (0,1,1,3,1,0), (0,3,1,4,2,1), (0,1,1,2,0), (0,2,1,2), (0,0,0,3), (0,3,1,5,2), (0,0,1,5), (0,1,0,3),
        (0,2,1,1), (0,1,0,2), (0,1,0,1),
    ),
)


def flipped(index, bits, devices):
    total, unit = index, 1
    while unit < devices:
        if bits & unit:
            total = total + unit * (1 - 2 * lax.rem(index // unit, 2))
        unit *= 2
    return total


class Place:
    def __init__(self):
        self.part, self.row = lax.axis_index("parts"), lax.axis_index("row")
        self.col, self.core = lax.axis_index("col"), lax.axis_index("rhs")
        self.half = self.row // 2
        self.low = lax.rem(self.row, 2)
        self.shard = self.row * 2 + self.col
        self.group = self.low * 4 + self.part * 2 + self.col
        self.foreign = lax.rem(self.half + self.part, 2)
        self.inner = lax.rem(self.half + self.low, 2)

    def link(self, way):
        if way == 0:
            return {"col": 1 - self.col}
        if way == 1:
            return {"parts": 1 - self.part}
        if way == 2:
            return {"row": self.half * 2 + 1 - self.low}
        return {"row": 3 - self.row}

    def tile_row(self, kind):
        return (3 * self.half, 1 + self.half, 2 - self.half, 3 - 3 * self.half)[kind]

    def solver(self, group):
        return {
            "row": 2 * self.part + group // 4,
            "parts": lax.rem(group // 2, 2),
            "col": lax.rem(group, 2),
        }

    def owner(self, shard):
        return {"row": shard // 2, "parts": self.half, "col": lax.rem(shard, 2)}


def greet_all(place, sibling):
    barrier = pltpu.get_barrier_semaphore()
    me = place.part * 8 + place.shard
    for offset in range(1, 16):
        other = lax.rem(me + offset, 16)
        peer = {"parts": other // 8, "row": lax.rem(other, 8) // 2, "col": lax.rem(other, 2)}
        pl.semaphore_signal(barrier, inc=1, device_id=peer, device_id_type=MESH)
    if sibling:
        pl.semaphore_signal(barrier, inc=1, device_id={"rhs": 1 - place.core}, device_id_type=MESH)
    pl.semaphore_wait(barrier, 15 + sibling)


def solve_kernel(
    stored, target, names, diag,
    first_home, second_home, scales, transit, hold,
    tiles, parcel, field, start, terms, image, first, away_out, away_in, hot, names_v, names_s, diag_v, scale, norm,
    piece_send, piece_recv, pass_recv, hold_recv, send, recv, own_sem, pair_sem, home_send, home_recv, home_own,
):
    place = Place()
    shard, core, foreign = place.shard, place.core, place.foreign
    half = tiles.shape[1]
    size = half // PIECES
    blocks, both, width = field.shape
    own = both // 2
    quarter = blocks // 8
    step_blocks = 16
    steps = blocks // step_blocks
    rows = hot.shape[1]
    fetch = pltpu.make_async_copy(target, first, own_sem.at[4])
    fetch.start()
    greet_all(place, 1)

    def part_of(k):
        return pl.ds(k * size, size)

    def mine(s):
        return field.at[pl.ds(s * quarter, quarter), pl.ds(0, own)]

    def piece_copy(source, target, way, send_sem, recv_sem):
        return pltpu.make_async_remote_copy(
            src_ref=source, dst_ref=target, send_sem=send_sem, recv_sem=recv_sem,
            device_id=place.link(way), device_id_type=MESH,
        )

    def source_shard(entry):
        solved = place.half if entry[5] == 0 else 1 - place.half
        row = (3 * solved, 3 - 3 * solved, 1 + solved, 2 - solved)[entry[1]]
        return row * 2 + (1 - place.col if entry[4] else place.col)

    def dest_group(entry):
        low = lax.rem(entry[2] // 2 + place.part, 2)
        part = 1 - place.part if entry[2] % 2 else place.part
        return low * 4 + part * 2 + (1 - place.col if entry[3] else place.col)

    def step(kind, entry, count):
        if entry[0] == 2:
            slot_in, slot_out, way = entry[6:]
            if entry[4] == 0 and slot_in < 0 and way >= 0:
                source = parcel.at[dest_group(entry)]
            elif way < 0:
                s = source_shard(entry)
                piece_copy(mine(s), mine(s), 0, piece_send.at[0], recv.at[2, s]).wait_recv()
                return count
            else:
                source = hold.at[slot_in]
                piece_copy(source, source, 0, piece_send.at[0], hold_recv.at[slot_in]).wait_recv()
            if slot_out < 0:
                s = source_shard(entry)
                target, sem = mine(s), recv.at[2, s]
            else:
                target, sem = hold.at[slot_out], hold_recv.at[slot_out]
            piece_copy(source, target, way, piece_send.at[count], sem).start()
            return count + 1
        k = entry[3]
        if entry[0] == 0:
            s = place.tile_row(entry[1]) * 2 + (1 - place.col if entry[2] else place.col)
            here = kind in (0, 2) and entry[1] == kind // 2 and entry[2] == 0
            source, sem = tiles.at[s, part_of(k)], piece_recv.at[s, k]
        else:
            s = place.tile_row(1 - entry[1]) * 2 + place.col
            here = entry[2] == 0
            source, sem = transit.at[entry[1], part_of(k)], pass_recv.at[entry[1], k]
        if here:
            source = stored.at[part_of(k), core]
        else:
            piece_copy(source, source, 0, piece_send.at[0], sem).wait_recv()
        for way in entry[4:]:
            if entry[0] == 0 or way == 3:
                target, sem = tiles.at[s, part_of(k)], piece_recv.at[s, k]
            else:
                target, sem = transit.at[entry[1], part_of(k)], pass_recv.at[entry[1], k]
            piece_copy(source, target, way, piece_send.at[count], sem).start()
            count += 1
        return count

    def sends(entry):
        return int(entry[8] >= 0) if entry[0] == 2 else len(entry) - 4

    def each_class(body):
        for kind in range(4):
            @pl.when((foreign == kind % 2) & (place.inner == kind // 2))
            def _(kind=kind):
                entries = ROUTES[kind]
                begin = [entry[0] for entry in entries].index(2)
                body(kind, entries, begin)

    def before_pack(kind, entries, begin):
        count = 0
        for entry in entries[:begin]:
            count = step(kind, entry, count)

    def sent(kind, entries, begin):
        count = 0
        for entry in entries:
            for _ in range(sends(entry)):
                block = parcel.at[0] if entry[0] == 2 else stored.at[part_of(0), core]
                piece_copy(block, block, 0, piece_send.at[count], piece_recv.at[shard, 0]).wait_send()
                count += 1

    each_class(before_pack)
    fetch.wait()

    def pack(n, carry):
        for u in range(4):
            b = n * 4 + u
            low = first[pl.ds(b * width, width)].astype(jnp.bfloat16).T
            parcel[:, b] = low.reshape(8, own, width)
        return carry

    lax.fori_loop(0, quarter // 4, pack, 0)
    pairs = ((names, names_v), (diag, diag_v))

    def straight(n, bits):
        group = flipped(place.group, bits, 8)
        return pltpu.make_async_remote_copy(
            src_ref=pairs[n][0],
            dst_ref=pairs[n][1].at[shard],
            send_sem=send.at[n, bits],
            recv_sem=recv.at[n, shard],
            device_id=place.solver(group),
            device_id_type=MESH,
        )

    def arrival(n, bits):
        landed = pairs[n][1].at[flipped(shard, bits, 8)]
        return pltpu.make_async_remote_copy(
            src_ref=landed, dst_ref=landed, send_sem=send.at[n, 0],
            recv_sem=recv.at[n, flipped(shard, bits, 8)],
            device_id=place.link(0), device_id_type=MESH,
        )

    def local(n):
        source, landed = (
            (names, names_v.at[shard]),
            (diag, diag_v.at[shard]),
            (parcel.at[place.group], mine(shard)),
            (stored.at[:, core], tiles.at[shard]),
        )[n]
        return pltpu.make_async_copy(source, landed, own_sem.at[n])

    for n in range(2):
        for bits in range(1, 8):
            straight(n, bits).start()

    @pl.when(foreign == 1)
    def _():
        for n in range(2):
            straight(n, 0).start()

    @pl.when(foreign == 0)
    def _():
        for n in range(4):
            local(n).start()

    for n in range(2):
        for bits in range(1, 8):
            arrival(n, bits).wait_recv()
            straight(n, bits).wait_send()

    @pl.when(foreign == 1)
    def _():
        for n in range(2):
            arrival(n, 0).wait_recv()
            straight(n, 0).wait_send()

    @pl.when(foreign == 0)
    def _():
        for n in range(4):
            local(n).wait()

    read = pltpu.make_async_copy(names_v, names_s, own_sem.at[4])
    read.start()

    taken = 2 * half
    lane = lax.broadcasted_iota(jnp.int32, names_v.shape[1:], 1)
    at = lax.broadcasted_iota(jnp.int32, (blocks, LANES), 0)
    for q in range(rows // LANES):
        s, skip = q * LANES // taken, q * LANES % taken
        here = pltpu.roll(names_v[s], (LANES - skip) % LANES, 1)
        next = pltpu.roll(names_v[s + 1], taken - skip, 1)
        row = jnp.where(lane < taken - skip, here, next)[0:1]
        hot[:, q * LANES : (q + 1) * LANES] = jnp.where(at == row, 1.0, 0.0).astype(jnp.bfloat16)

    read.wait()
    def swap(n, source, landed):
        return pltpu.make_async_remote_copy(
            src_ref=source, dst_ref=landed, send_sem=pair_sem.at[n, 0], recv_sem=pair_sem.at[n, 1],
            device_id={"rhs": 1 - core}, device_id_type=MESH,
        )

    ours, theirs = field.at[:, pl.ds(0, own)], field.at[:, pl.ds(own, own)]
    pair = swap(0, ours, theirs)
    zero = jnp.zeros((own, width), jnp.float32)

    def chunk(ref, n):
        return ref[pl.ds(n * step_blocks, step_blocks)]

    def keep(n, total):
        low = field[pl.ds(n * step_blocks, step_blocks), 0:own]
        start[pl.ds(n * step_blocks, step_blocks)] = low
        value = low.astype(jnp.float32)
        return total + jnp.sum(value * value, axis=0)

    def keep_start():
        norm[...] = lax.fori_loop(0, steps, keep, zero)

    def product(s, k):
        results = []
        for u in range(size):
            slot = k * size + u
            i, j = names_s[s, 0, slot], names_s[s, 0, half + slot]
            block = tiles[s, slot]
            direct = lax.dot_general(
                field[j], block, (((1,), (1,)), ((), ())), preferred_element_type=jnp.float32
            )
            mirrored = lax.dot_general(
                field[i], block, (((1,), (0,)), ((), ())), preferred_element_type=jnp.float32
            )
            results.append((slot, slot < names_s[s, 1, 0], direct, mirrored))
        for slot, used, direct, mirrored in results:
            at = s * taken + slot
            terms[pl.ds(at, both, stride=rows)] = jnp.where(used, direct, 0.0)
            terms[pl.ds(at + half, both, stride=rows)] = jnp.where(used, mirrored, 0.0)

    def products(n, carry):
        product(n // PIECES, lax.rem(n, PIECES))
        return carry

    def product_pair(row, k):
        def one(col, carry):
            product(place.tile_row(row) * 2 + col, k)
            return carry

        lax.fori_loop(0, 2, one, 0)

    def after_pack(kind, entries, begin):
        count = sum(sends(entry) for entry in entries[:begin])
        ready = max(n for n, entry in enumerate(entries) if entry[0] == 2 and entry[8] < 0)
        landed, due = set(), []
        for n, entry in enumerate(entries):
            if n >= begin:
                count = step(kind, entry, count)
            if entry[0] == 0:
                landed.add(entry[1:4])
                if (entry[1], 1 - entry[2], entry[3]) in landed:
                    due.append((entry[1], entry[3]))
            if n == ready:
                pair.start()
            if n == min(ready + 1, len(entries) - 1):
                keep_start()
            if n == min(ready + 2, len(entries) - 1):
                pair.wait()
            if n >= ready + 2:
                for _ in range(-(-len(due) // (len(entries) - n))):
                    product_pair(*due.pop(0))
        for one in due:
            product_pair(*one)

    each_class(after_pack)
    each_class(sent)

    def gather_sums(n, carry):
        c = 2 * n
        pair = [terms[pl.ds((c + m) * rows, rows)].astype(jnp.bfloat16) for m in range(2)]
        total = jnp.dot(
            hot[...], jnp.concatenate(pair, axis=1), preferred_element_type=jnp.float32
        )
        for m in range(2):
            image[pl.ds(c + m, blocks, stride=both)] = total[:, m * width : (m + 1) * width]
        return carry

    def image_chunk(n):
        return image[pl.ds(n * step_blocks * both, step_blocks * both)].reshape(step_blocks, both, width)

    def first_chunk(n):
        return first[pl.ds(n * step_blocks * own, step_blocks * own)].reshape(step_blocks, own, width)

    def start_chunk(n):
        return chunk(start, n).astype(jnp.float32)

    def diag_chunk(n):
        per = quarter // step_blocks
        return diag_v[n // per, pl.ds(lax.rem(n, per) * step_blocks, step_blocks)][:, None, :]

    def operate(exchange, direction_chunk):
        lax.fori_loop(own // 2, own, gather_sums, 0)

        def away(n, carry):
            away_out[pl.ds(n * step_blocks, step_blocks)] = image_chunk(n)[:, own:].astype(jnp.bfloat16)
            return carry

        lax.fori_loop(0, steps, away, 0)
        over = swap(exchange, away_out, away_in)
        over.start()
        lax.fori_loop(0, own // 2, gather_sums, 0)
        over.wait()

        def join(n, total):
            direction = direction_chunk(n)
            value = image_chunk(n)[:, :own] + chunk(away_in, n).astype(jnp.float32)
            value = value + diag_chunk(n) * direction
            image[pl.ds(n * step_blocks * own, step_blocks * own)] = value.reshape(step_blocks * own, width)
            return total + jnp.sum(value * direction, axis=0)

        return jnp.sum(lax.fori_loop(0, steps, join, zero), axis=1, keepdims=True)

    def joined_chunk(n):
        return image[pl.ds(n * step_blocks * own, step_blocks * own)].reshape(step_blocks, own, width)

    home = ((scale, scales), (parcel, first_home), (away_out, second_home))

    def leaving(n, to):
        if n == 0:
            return scale
        return parcel.at[to] if n == 1 else away_out.at[pl.ds(to * quarter, quarter)]

    def home_copy(n, bits):
        to = flipped(shard, bits, 8)
        return pltpu.make_async_remote_copy(
            src_ref=leaving(n, to),
            dst_ref=home[n][1].at[place.group],
            send_sem=home_send.at[n, bits],
            recv_sem=home_recv.at[n, place.group],
            device_id=place.owner(to),
            device_id_type=MESH,
        )

    def home_arrival(n, bits):
        landed = home[n][1].at[flipped(place.group, bits, 8)]
        return pltpu.make_async_remote_copy(
            src_ref=landed, dst_ref=landed, send_sem=home_send.at[n, 0],
            recv_sem=home_recv.at[n, flipped(place.group, bits, 8)],
            device_id=place.link(0), device_id_type=MESH,
        )

    def home_local(n):
        return pltpu.make_async_copy(leaving(n, shard), home[n][1].at[place.group], home_own.at[n])

    def go_home(n):
        for bits in range(7, 0, -1):
            home_copy(n, bits).start()

        @pl.when(foreign == 1)
        def _():
            home_copy(n, 0).start()

        @pl.when(foreign == 0)
        def _():
            home_local(n).start()

    def arrive_home(n):
        for bits in range(1, 8):
            home_copy(n, bits).wait_send()
            home_arrival(n, bits).wait_recv()

        @pl.when(foreign == 1)
        def _():
            home_copy(n, 0).wait_send()
            home_arrival(n, 0).wait_recv()

        @pl.when(foreign == 0)
        def _():
            home_local(n).wait()

    per = quarter // step_blocks
    norm0 = jnp.sum(norm[...], axis=1, keepdims=True)
    alpha1 = norm0 / operate(1, start_chunk)

    def next_first(n, total):
        value = start_chunk(n) - alpha1[None] * joined_chunk(n)
        first[pl.ds(n * step_blocks * own, step_blocks * own)] = value.reshape(step_blocks * own, width)
        parcel[n // per, pl.ds(lax.rem(n, per) * step_blocks, step_blocks)] = value.astype(jnp.bfloat16)
        return total + jnp.sum(value * value, axis=0)

    norm1 = jnp.sum(lax.fori_loop(0, steps, next_first, zero), axis=1, keepdims=True)
    go_home(1)
    beta = norm1 / norm0

    def direction_chunk(n):
        return first_chunk(n) + beta[None] * start_chunk(n)

    def next_low(n, carry):
        field[pl.ds(n * step_blocks, step_blocks), 0:own] = direction_chunk(n).astype(jnp.bfloat16)
        return carry

    lax.fori_loop(0, steps, next_low, 0)
    pair = swap(2, ours, theirs)
    pair.start()
    pair.wait()
    lax.fori_loop(0, 8 * PIECES, products, 0)
    alpha2 = norm1 / operate(3, direction_chunk)

    def last(n, carry):
        value = first_chunk(n) - alpha2[None] * joined_chunk(n)
        away_out[pl.ds(n * step_blocks, step_blocks)] = value.astype(jnp.bfloat16)
        return carry

    lax.fori_loop(0, steps, last, 0)
    go_home(2)
    for n, value in enumerate((alpha1, alpha2, beta)):
        scale[n] = jnp.broadcast_to(value, (own, width))
    go_home(0)
    for n in (1, 2, 0):
        arrive_home(n)


def solve(stored, target, names, diag):
    half, cores, width, _ = stored.shape
    quarter, columns = target.shape[0] // width, target.shape[1]
    own = columns // 8
    parcel = (8, quarter, own, width)
    blocks, both, rows = 8 * quarter, 2 * own, 16 * half
    sends = max(
        sum(int(e[8] >= 0) if e[0] == 2 else len(e) - 4 for e in entries) for entries in ROUTES
    )
    dma = pltpu.SemaphoreType.DMA
    return pl.pallas_call(
        solve_kernel,
        out_shape=(
            jax.ShapeDtypeStruct(parcel, jnp.bfloat16),
            jax.ShapeDtypeStruct(parcel, jnp.bfloat16),
            jax.ShapeDtypeStruct((8, 3, own, width), jnp.float32),
            jax.ShapeDtypeStruct((2, half, width, width), stored.dtype),
            jax.ShapeDtypeStruct((HOLD,) + parcel[1:], jnp.bfloat16),
        ),
        in_specs=[ANY] * 4,
        out_specs=[ANY] * 5,
        scratch_shapes=[
            pltpu.VMEM((8, half, width, width), stored.dtype),
            pltpu.VMEM(parcel, jnp.bfloat16),
            pltpu.VMEM((blocks, both, width), jnp.bfloat16),
            pltpu.VMEM((blocks, own, width), jnp.bfloat16),
            pltpu.VMEM((both * rows + rows, width), jnp.float32),
            pltpu.VMEM((blocks * both, width), jnp.float32),
            pltpu.VMEM((blocks * own, width), jnp.float32),
            pltpu.VMEM((blocks, own, width), jnp.bfloat16),
            pltpu.VMEM((blocks, own, width), jnp.bfloat16),
            pltpu.VMEM((blocks, rows), jnp.bfloat16),
            pltpu.VMEM((8,) + names.shape, names.dtype),
            pltpu.SMEM((8,) + names.shape, names.dtype),
            pltpu.VMEM((8,) + diag.shape, diag.dtype),
            pltpu.VMEM((3, own, width), jnp.float32),
            pltpu.VMEM((own, width), jnp.float32),
            dma((sends,)),
            dma((8, PIECES)),
            dma((2, PIECES)),
            dma((HOLD,)),
            dma((2, 8)),
            dma((3, 8)),
            dma((5,)),
            dma((4, 2)),
            dma((3, 8)),
            dma((3, 8)),
            dma((3,)),
        ],
        compiler_params=pltpu.CompilerParams(
            collective_id=0, has_side_effects=True, vmem_limit_bytes=60 * 2**20
        ),
    )(stored, target, names, diag)[:3]


def finish_kernel(target_ref, diag_ref, first_ref, second_ref, scale_ref, answer_ref, residual_ref, scale_rows):
    blocks, width, columns = target_ref.shape

    @pl.when(pl.program_id(0) == 0)
    def _():
        for n in range(3):
            scale_rows[n] = scale_ref[:, n].reshape(columns, width).T[0:8]

    alpha1, alpha2, beta = scale_rows[0, 0:1], scale_rows[1, 0:1], scale_rows[2, 0:1]
    diags = diag_ref[...].T
    same = lax.broadcasted_iota(jnp.int32, (width, columns), 0) == lax.broadcasted_iota(
        jnp.int32, (width, columns), 1
    )
    unit = jnp.where(same, 1.0, 0.0).astype(jnp.bfloat16)

    def turned(value):
        return lax.dot_general(
            unit, value.reshape(columns, width), (((1,), (1,)), ((), ())), preferred_element_type=jnp.float32
        )

    for b in range(blocks):
        target = target_ref[b]
        diag = diags[:, b : b + 1]
        first, second = turned(first_ref[:, b]), turned(second_ref[:, b])
        lost = target - target.astype(jnp.bfloat16).astype(jnp.float32)
        lost1 = lost - alpha1 * diag * lost
        answer_ref[b] = alpha1 * target + alpha2 * (first + lost1 + beta * target)
        residual_ref[b] = second + lost1 - alpha2 * diag * (lost1 + beta * lost)


def finish(target, diag, first, second, scales):
    blocks, width, columns = target.shape
    devices, _, own, _ = second.shape
    step = 16
    whole = pl.BlockSpec((step, width, columns), lambda g: (g, 0, 0))
    part = pl.BlockSpec((devices, step, own, width), lambda g: (0, g, 0, 0))
    return pl.pallas_call(
        finish_kernel,
        out_shape=(jax.ShapeDtypeStruct(target.shape, jnp.float32),) * 2,
        grid=(blocks // step,),
        in_specs=[
            whole,
            pl.BlockSpec((step, width), lambda g: (g, 0)),
            part,
            part,
            pl.BlockSpec(scales.shape, lambda g: (0, 0, 0, 0)),
        ],
        out_specs=(whole, whole),
        scratch_shapes=[pltpu.VMEM((3, 8, columns), jnp.float32)],
        compiler_params=pltpu.CompilerParams(vmem_limit_bytes=40 * 2**20),
    )(target, diag, first, second, scales)


def by_columns(blocks, block_rows, block_cols, counts, diagonal, target):
    nrow, ncol = lax.axis_size("row"), lax.axis_size("col")
    devices = nrow * ncol
    stored = blocks[0, 0]
    slots, width, _ = stored.shape
    quarter = target.shape[0] // width
    row_blocks = ncol * quarter
    half = slots // 2
    row, col, core = lax.axis_index("row"), lax.axis_index("col"), lax.axis_index("rhs")

    irow = row * row_blocks + block_rows[0, 0]
    jcol = block_cols[0, 0]
    icol = (jcol // quarter * ncol + col) * quarter + jcol % quarter

    def every_other(index):
        return jnp.where(core == 0, index[0::2], index[1::2])

    used = (counts[0] - core + 1) // 2
    gap = jnp.zeros((LANES - 2 * half,), jnp.int32)
    slots = jnp.concatenate([every_other(irow), every_other(icol), gap])
    names = jnp.stack([slots, jnp.broadcast_to(used, (LANES,))])
    names = jnp.pad(names, ((0, 6), (0, 0)))
    diag_own = diagonal.reshape(quarter, width)
    target_blocks = target.reshape(quarter, width, target.shape[1])
    first_home, second_home, scales = solve(
        stored.reshape(half, 2, width, width), target, names, diag_own
    )
    answer, residual = finish(target_blocks, diag_own, first_home, second_home, scales)
    return (answer.reshape(target.shape), residual.reshape(target.shape))


def one_hot_slots(indices, valid, extent):
    return ((indices[None, :] == jnp.arange(extent)[:, None]) & valid[None, :]).astype(jnp.float32)


def picked(blocks, index):
    return lax.map(lambda i: lax.dynamic_index_in_dim(blocks, i, 0, keepdims=False), index)


def on_device(blocks, block_rows, block_cols, counts, diagonal, target):
    highest = lax.Precision.HIGHEST
    nrow = lax.axis_size("row")
    ncol = lax.axis_size("col")
    if (
        (lax.axis_size("parts"), nrow, ncol, lax.axis_size("rhs")) == (2, 4, 2, 2)
        and target.shape[1] == 128
        and blocks.shape[2] % (16 * PIECES) == 0
        and target.shape[0] // blocks.shape[3] % 64 == 0
    ):
        return by_columns(blocks, block_rows, block_cols, counts, diagonal, target)
    stored = blocks[0, 0]
    slots = stored.shape[0]
    width = stored.shape[1]
    local = target.shape[0]
    ncols = target.shape[1]
    quarter = local // width
    row_blocks = ncol * quarter
    col_blocks = nrow * quarter
    valid = jnp.arange(slots) < counts[0, 0]
    rows_hot = one_hot_slots(block_rows[0, 0], valid, row_blocks)
    cols_hot = one_hot_slots(block_cols[0, 0], valid, col_blocks)

    def squares(vector):
        return lax.psum(jnp.sum(vector * vector, axis=0), ("row", "col"))

    solution = jnp.zeros_like(target)
    residual = target
    direction = target
    norm_now = squares(residual)
    for step in range(ITERS):
        operate_field_low = direction.astype(jnp.bfloat16)
        direct_gathered = lax.all_gather(operate_field_low, "row", axis=0, tiled=True).reshape(
            col_blocks, width, ncols
        )
        prod = jnp.einsum(
            "kab,kbc->kac",
            stored,
            picked(direct_gathered, block_cols[0, 0]),
            preferred_element_type=jnp.float32,
        )
        direct_partial_value = jnp.einsum("ik,kac->iac", rows_hot, prod, precision=highest)
        direct = lax.psum_scatter(
            direct_partial_value.reshape(row_blocks * width, ncols).astype(jnp.bfloat16),
            "col",
            scatter_dimension=0,
            tiled=True,
        ).astype(jnp.float32)
        gathered = lax.all_gather(operate_field_low, "col", axis=0, tiled=True).reshape(
            row_blocks, width, ncols
        )
        tprod = jnp.einsum(
            "kba,kbc->kac",
            stored,
            picked(gathered, block_rows[0, 0]),
            preferred_element_type=jnp.float32,
        )
        partial_value = jnp.einsum("jk,kac->jac", cols_hot, tprod, precision=highest)
        parcel = partial_value.astype(jnp.bfloat16).reshape(nrow, local, ncols)
        mirrored = jnp.sum(
            lax.all_to_all(parcel, "row", split_axis=0, concat_axis=0, tiled=True).astype(
                jnp.float32
            ),
            axis=0,
        )
        image = diagonal[:, None] * direction + direct + mirrored
        curve = lax.psum(jnp.sum(direction * image, axis=0), ("row", "col"))
        alpha = norm_now / curve
        solution = solution + alpha * direction
        residual = residual - alpha * image
        if step + 1 < ITERS:
            norm_next = squares(residual)
            direction = residual + norm_next / norm_now * direction
            norm_now = norm_next
    return (solution, residual)


def solution(mesh):
    return jax.shard_map(
        on_device,
        mesh=mesh,
        in_specs=(
            P(("parts", "row"), "col", None, None, None),
            P(("parts", "row"), "col", None),
            P(("parts", "row"), "col", None),
            P(("parts", "row"), "col"),
            P(("parts", "row", "col")),
            P(("parts", "row", "col"), "rhs"),
        ),
        out_specs=(P(("parts", "row", "col"), "rhs"), P(("parts", "row", "col"), "rhs")),
        check_vma=False,
    )
```
